32 devices in a mesh: fsdp: 32 (over z, y, x, core).
Axes of the slice: x: 2, y: 2, z: 4, core: 2. Of those that a mesh axis runs over, the one named last changes fastest.
Arguments:
- block_input: bfloat16 [32, 784, 768], P('fsdp'), may hold values from -6 to 6
- seg_ids: int32 [32, 784], P('fsdp'), may hold values from 0 to 3, as said below
- gain_attn: bfloat16 [768], P('fsdp'), may hold values from 0.099609375 to 1.8984375
- w_query: bfloat16 [768, 768], P('fsdp'), may hold values from -0.21875 to 0.21875
- w_key: bfloat16 [768, 768], P('fsdp'), may hold values from -0.21875 to 0.21875
- w_value: bfloat16 [768, 768], P('fsdp'), may hold values from -0.21875 to 0.21875
- w_out: bfloat16 [768, 768], P('fsdp'), may hold values from -0.875 to 0.875
- gain_ffn: bfloat16 [768], P('fsdp'), may hold values from 0.099609375 to 1.8984375
- w_gate: bfloat16 [768, 2048], P('fsdp'), may hold values from -0.21875 to 0.21875
- w_up: bfloat16 [768, 2048], P('fsdp'), may hold values from -0.21875 to 0.21875
- w_down: bfloat16 [2048, 768], P('fsdp'), may hold values from -0.125 to 0.125
- cotangent: bfloat16 [32, 784, 768], P('fsdp'), may hold values from -6 to 6
Outputs:
- block_output: bfloat16 [32, 784, 768], P('fsdp')
- input_grad: bfloat16 [32, 784, 768], P('fsdp')
- gain_attn_grad: float32 [768], P('fsdp')
- w_query_grad: float32 [768, 768], P('fsdp')
- w_key_grad: float32 [768, 768], P('fsdp')
- w_value_grad: float32 [768, 768], P('fsdp')
- w_out_grad: float32 [768, 768], P('fsdp')
- gain_ffn_grad: float32 [768], P('fsdp')
- w_gate_grad: float32 [768, 2048], P('fsdp')
- w_up_grad: float32 [768, 2048], P('fsdp')
- w_down_grad: float32 [2048, 768], P('fsdp')
The draws below stay inside these ranges and needn't reach their ends.
Inputs may be any that keep to these rules, and one draw needn't show every extreme that they name: `seg_ids`: each row holds, from slot 0 on, either one image of 577 tokens (segment 0) or two or three images of 257 tokens (segments 0, 1, 2 in order), and padding with segment number 3 in all remaining slots, at least one of them.
All inputs are finite; a program needn't handle non-finite values.
Results may differ from the reference program's by a relative error of at most 0.015.
Values may be sent and summed in bfloat16 or wider, within the bound.
A program may use at most 128 MiB of HBM per device.

```python
import jax
import jax.numpy as jnp
from jax import lax

D = 768
FF = 2048
HEADS = 12
HEAD = 64
ROW = 784
LONG = 577
SHORT = 257
ROWS = 32
TOKENS = 25088


def draw_seg_ids(key, part):
    layouts = jax.random.randint(key, (ROWS,), 0, 3)
    places = jnp.arange(ROW, dtype=jnp.int32)
    one_long = jnp.where(places < LONG, 0, 3)
    shorts = layouts[:, None] + 1
    several = jnp.where(places[None, :] < shorts * SHORT, places[None, :] // SHORT, 3)
    return jnp.where(layouts[:, None] == 0, one_long[None, :], several).astype(jnp.int32)


def strengthened(drawn, stream_key, source, target, parts, factor):
    def block_of(dim):
        return (jnp.arange(drawn.shape[dim]) // (drawn.shape[dim] // parts)).reshape((-1,) + (1,) * (drawn.ndim - 1 - dim))

    one_side = jax.random.permutation(stream_key, parts)[block_of(target)]
    second = (block_of(target) + parts // 2) % parts
    return jnp.where((block_of(source) == one_side) | (block_of(source) == second), factor * drawn, drawn)


def block_scale(stream_key, dims, cuts, smallest, largest):
    level, own = 1.0, jax.random.fold_in(stream_key, 6)
    for dim, parts in cuts:
        steps = jnp.exp(jax.random.uniform(jax.random.fold_in(own, dim), (parts,), jnp.float32, smallest / len(cuts), largest / len(cuts)))
        level = level * jnp.repeat(steps, dims[dim] // parts).reshape([-1 if axis == dim else 1 for axis in range(len(dims))])
    return level


def bell_draw(own_key, shape, width, most, shards=(), kind=jnp.bfloat16):
    entries = jax.random.normal(own_key, shape, jnp.float32) * width
    if len(shards) > 0:
        entries = block_scale(own_key, shape, shards, -0.22, 0.18) * entries
    return jnp.clip(entries, min=-most, max=most).astype(kind)


def noise_with(rng, dims, scale, most, shards, heavy, kind=jnp.bfloat16):
    values = scale * jax.random.normal(rng, dims, jnp.float32)
    if shards:
        values = values * block_scale(rng, dims, shards, -0.22, 0.18)
    return jnp.clip(strengthened(values, jax.random.fold_in(rng, 3), *heavy), -most, most).astype(kind)


def setup_inputs(seed: int = 0) -> dict:
    arg_keys = jax.random.split(jax.random.key(seed), 13)
    block_input = noise_with(arg_keys[0], (ROWS, ROW, D), 1.0, 6.0, ((0, 32),), (0, 2, 32, 2.75))
    seg_ids = draw_seg_ids(jax.random.fold_in(arg_keys[12], 71), 0)
    gain_attn = jnp.clip(1.0 + 0.18 * jax.random.normal(arg_keys[2], (D,), jnp.float32), 0.099609375, 1.8984375).astype(jnp.bfloat16)
    w_query = bell_draw(arg_keys[3], (D, D), D ** -0.5, 0.21875, ((0, 32),))
    w_key = bell_draw(arg_keys[4], (D, D), D ** -0.5, 0.21875, ((0, 32),))
    w_value = bell_draw(arg_keys[5], (D, D), D ** -0.5, 0.21875, ((0, 32),))
    w_out = bell_draw(arg_keys[6], (D, D), (D // 16) ** -0.5, 0.875, ((0, 32),))
    gain_ffn = jnp.clip(1.0 + 0.18 * jax.random.normal(arg_keys[7], (D,), jnp.float32), 0.099609375, 1.8984375).astype(jnp.bfloat16)
    w_gate = bell_draw(arg_keys[8], (D, FF), D ** -0.5, 0.21875, ((0, 32),))
    w_up = bell_draw(arg_keys[9], (D, FF), D ** -0.5, 0.21875, ((0, 32),))
    w_down = bell_draw(arg_keys[10], (FF, D), FF ** -0.5, 0.125, ((0, 32),))
    cotangent = noise_with(arg_keys[11], (ROWS, ROW, D), 1.0, 6.0, ((0, 32),), (0, 2, 32, 2.75))
    return dict(block_input=block_input, seg_ids=seg_ids, gain_attn=gain_attn, w_query=w_query, w_key=w_key, w_value=w_value, w_out=w_out, gain_ffn=gain_ffn, w_gate=w_gate, w_up=w_up, w_down=w_down, cotangent=cotangent)


@jax.custom_vjp
def low(v):
    return lax.optimization_barrier(v.astype(jnp.bfloat16)).astype(jnp.float32)

@jax.custom_vjp
def low_back(v):
    return v

def low_keep(v):
    return (low(v), None)

def low_pass(kept, grad):
    return (grad,)

def back_keep(v):
    return (v, None)

def back_low(kept, grad):
    return (low(grad),)
low.defvjp(low_keep, low_pass)
low_back.defvjp(back_keep, back_low)
EPSILON = 1e-05

def product(left, right):
    return jnp.dot(left, right, precision=lax.Precision.HIGHEST, preferred_element_type=jnp.float32)

def rms_scaled(values, gain):
    inverse = lax.rsqrt(lax.optimization_barrier(jnp.mean(values * values, axis=-1, keepdims=True)) + EPSILON)
    return values * inverse * gain

def rope_tables(segment_row):
    places = jnp.arange(ROW, dtype=jnp.int32)
    labels = jnp.arange(4, dtype=jnp.int32)
    counts = lax.optimization_barrier(jnp.sum((segment_row[:, None] == labels[None, :]).astype(jnp.int32), axis=0))
    before = (labels[None, :] < segment_row[:, None]).astype(jnp.int32)
    starts = lax.optimization_barrier(jnp.sum(before * counts[None, :], axis=1))
    offsets = (places - starts).astype(jnp.float32)
    frequency = 10000.0 ** (-(jnp.arange(HEAD // 2, dtype=jnp.float32) * 2.0) / HEAD)
    angles = offsets[:, None] * frequency[None, :]
    return (jnp.cos(angles), jnp.sin(angles))

def rotate(values, cosine, sine_table):
    half_size = values.shape[-1] // 2
    lower_half = values[..., :half_size]
    upper_half = values[..., half_size:]
    cosine = cosine[:, None, :]
    sine_table = sine_table[:, None, :]
    return jnp.concatenate([lower_half * cosine - upper_half * sine_table, upper_half * cosine + lower_half * sine_table], axis=-1)

def attend(operands):
    queries, key_vectors, value_vectors, segment_row = operands
    cosine, sine_table = rope_tables(segment_row)
    query_rot = low(rotate(queries, cosine, sine_table))
    key_rot = low(rotate(key_vectors, cosine, sine_table))
    raw_scores = jnp.einsum('lhe,mhe->hlm', query_rot, key_rot, precision=lax.Precision.HIGHEST)
    scores = low_back(raw_scores * HEAD ** (-0.5))
    places = jnp.arange(ROW, dtype=jnp.int32)
    allowed = (segment_row[:, None] == segment_row[None, :]) & (places[None, :] <= places[:, None])
    masked = jnp.where(allowed[None], scores, -1e+30)
    highest = lax.optimization_barrier(jnp.max(masked, axis=-1, keepdims=True))
    exponent = jnp.exp(masked - highest)
    probabilities = low(exponent / lax.optimization_barrier(jnp.sum(exponent, axis=-1, keepdims=True)))
    mixture = jnp.einsum('hlm,mhe->lhe', probabilities, value_vectors, precision=lax.Precision.HIGHEST)
    return low(low_back(mixture))

def forward(block_input, seg_ids, gain_attn, w_query, w_key, w_value, w_out, gain_ffn, w_gate, w_up, w_down):
    inputs = block_input.reshape(TOKENS, D)
    normed_one = low(rms_scaled(inputs, gain_attn))
    queries = low_back(product(normed_one, w_query)).reshape(ROWS, ROW, HEADS, HEAD)
    key_vectors = low_back(product(normed_one, w_key)).reshape(ROWS, ROW, HEADS, HEAD)
    value_vectors = low(low_back(product(normed_one, w_value))).reshape(ROWS, ROW, HEADS, HEAD)
    mixture = lax.map(jax.checkpoint(attend), (queries, key_vectors, value_vectors, seg_ids))
    mixture = mixture.reshape(TOKENS, D)
    middle = inputs + low_back(product(mixture, w_out))
    normed_two = low(rms_scaled(middle, gain_ffn))
    gate_proj = low_back(product(normed_two, w_gate))
    up_proj = low_back(product(normed_two, w_up))
    hidden = low(gate_proj / (1.0 + jnp.exp(-gate_proj)) * up_proj)
    result = middle + low_back(product(hidden, w_down))
    return result.reshape(ROWS, ROW, D)

def reference(block_input, seg_ids, gain_attn, w_query, w_key, w_value, w_out, gain_ffn, w_gate, w_up, w_down, cotangent):
    floats = [array.astype(jnp.float32) for array in (block_input, gain_attn, w_query, w_key, w_value, w_out, gain_ffn, w_gate, w_up, w_down)]

    def closed(inputs, gain_one, query_w, key_w, value_w, out_w, gain_two, gate_w, up_w, down_w):
        return forward(inputs, seg_ids, gain_one, query_w, key_w, value_w, out_w, gain_two, gate_w, up_w, down_w)
    output, pullback = jax.vjp(closed, *floats)
    grads = pullback(cotangent.astype(jnp.float32))
    return (output.astype(jnp.bfloat16), grads[0].astype(jnp.bfloat16), grads[1], grads[2], grads[3], grads[4], grads[5], grads[6], grads[7], grads[8], grads[9])
```

```python
from functools import partial

import jax
import jax.numpy as jnp
from jax import lax
from jax.experimental import pallas as pl
from jax.experimental.pallas import tpu as pltpu
from jax.sharding import PartitionSpec as P

HEAD = 64
EPSILON = 1e-05
CELLS = 32
MESH = pl.DeviceIdType.MESH
F32 = jnp.float32
BF16 = jnp.bfloat16


def place(fold):
    me = lax.axis_index("fsdp")
    cell = me // fold
    k = cell % 2
    x = (cell // 2) % 2
    y = (cell // 4) % 2
    z = cell // 8
    ids = {
        "core": me + (1 - 2 * k) * fold,
        "x": me + (1 - 2 * x) * (2 * fold),
        "y": me + (1 - 2 * y) * (4 * fold),
    }
    for r in (1, 2, 3):
        ids[r] = me + ((z + r) % 4 - z) * (8 * fold)
    return z, y, x, k, ids


def greet(ids):
    barrier = pltpu.get_barrier_semaphore()
    for peer in ids.values():
        pl.semaphore_signal(barrier, inc=1, device_id=(peer,), device_id_type=MESH)
    pl.semaphore_wait(barrier, len(ids))


class Gather:
    def __init__(self, where, own, full, send, recv, local):
        self.where, self.own, self.full = where, own, full
        self.send, self.recv, self.local = send, recv, local
        self.half = full.shape[-1] // 2
        self.copies = {}

    def push(self, slot, src, dst, peer):
        copy = pltpu.make_async_remote_copy(
            src_ref=src,
            dst_ref=dst,
            send_sem=self.send.at[slot],
            recv_sem=self.recv.at[slot],
            device_id=(peer,),
            device_id_type=MESH,
        )
        copy.start()
        self.copies[slot] = copy

    def arrive(self, *slots):
        for slot in slots:
            self.copies[slot].wait_recv()

    def step0(self):
        z, y, x, k, ids = self.where
        self.keep = pltpu.make_async_copy(self.own, self.full.at[z, y, x, k], self.local)
        self.keep.start()
        for r in (2, 1, 3):
            self.push(r - 1, self.own, self.full.at[z, y, x, k], ids[r])

    def step1(self):
        z, y, x, k, ids = self.where
        h, n = self.half, self.full.shape[-1]
        self.keep.wait()
        self.arrive(0, 1, 2)
        a = self.full.at[:, y, x, k, :, pl.ds(0, h)]
        b = self.full.at[:, y, x, k, :, pl.ds(h, n - h)]
        self.push(3, a, a, ids["y"])
        self.push(4, b, b, ids["x"])

    def step2(self):
        z, y, x, k, ids = self.where
        h, n = self.half, self.full.shape[-1]
        self.arrive(3, 4)
        a = self.full.at[:, :, x, k, :, pl.ds(0, h)]
        b = self.full.at[:, y, :, k, :, pl.ds(h, n - h)]
        self.push(5, a, a, ids["x"])
        self.push(6, b, b, ids["y"])

    def step3(self):
        z, y, x, k, ids = self.where
        self.arrive(5, 6)
        part = self.full.at[:, :, :, k]
        self.push(7, part, part, ids["core"])

    def step4(self):
        self.arrive(7)

    def settle(self):
        for copy in self.copies.values():
            copy.wait_send()


class Scatter:
    def __init__(self, where, full, bufs, send, recv):
        self.where, self.full = where, full
        self.r0, self.r1, self.r2, self.r3 = bufs
        self.send, self.recv = send, recv
        self.half = full.shape[-1] // 2
        self.copies = {}

    push = Gather.push
    arrive = Gather.arrive
    settle = Gather.settle

    def step0(self):
        z, y, x, k, ids = self.where
        self.push(0, self.full.at[:, :, :, 1 - k], self.r0, ids["core"])

    def step1(self):
        z, y, x, k, ids = self.where
        h, n = self.half, self.full.shape[-1]
        self.arrive(0)

        def add(i, _):
            a, b, c = i // 4, (i // 2) % 2, i % 2
            self.r0[a, b, c] = (
                self.r0[a, b, c].astype(F32) + self.full[a, b, c, k].astype(F32)
            ).astype(BF16)
            return 0

        lax.fori_loop(0, 16, add, 0)
        self.push(
            1, self.r0.at[:, :, 1 - x, :, pl.ds(0, h)], self.r1.at[:, :, :, pl.ds(0, h)], ids["x"]
        )
        self.push(
            2,
            self.r0.at[:, 1 - y, :, :, pl.ds(h, n - h)],
            self.r1.at[:, :, :, pl.ds(h, n - h)],
            ids["y"],
        )

    def step2(self):
        z, y, x, k, ids = self.where
        h, n = self.half, self.full.shape[-1]
        self.arrive(1, 2)

        def add(i, _):
            a, b = i // 2, i % 2
            self.r1[a, b, :, :h] = (
                self.r1[a, b, :, :h].astype(F32) + self.r0[a, b, x, :, :h].astype(F32)
            ).astype(BF16)
            self.r1[a, b, :, h:] = (
                self.r1[a, b, :, h:].astype(F32) + self.r0[a, y, b, :, h:].astype(F32)
            ).astype(BF16)
            return 0

        lax.fori_loop(0, 8, add, 0)
        self.push(
            3, self.r1.at[:, 1 - y, :, pl.ds(0, h)], self.r2.at[:, :, pl.ds(0, h)], ids["y"]
        )
        self.push(
            4,
            self.r1.at[:, 1 - x, :, pl.ds(h, n - h)],
            self.r2.at[:, :, pl.ds(h, n - h)],
            ids["x"],
        )

    def step3(self):
        z, y, x, k, ids = self.where
        h = self.half
        self.arrive(3, 4)

        def add(a, _):
            self.r2[a, :, :h] = (
                self.r2[a, :, :h].astype(F32) + self.r1[a, y, :, :h].astype(F32)
            ).astype(BF16)
            self.r2[a, :, h:] = (
                self.r2[a, :, h:].astype(F32) + self.r1[a, x, :, h:].astype(F32)
            ).astype(BF16)
            return 0

        lax.fori_loop(0, 4, add, 0)
        for r in (2, 1, 3):
            self.push(4 + r, self.r2.at[(z + r) % 4], self.r3.at[r - 1], ids[r])

    def step4(self):
        z = self.where[0]
        self.arrive(5, 6, 7)
        return (
            self.r2[z].astype(F32)
            + self.r3[0].astype(F32)
            + self.r3[1].astype(F32)
            + self.r3[2].astype(F32)
        )


def gather_kernel(fold, count, *refs):
    owns, fulls = refs[:count], refs[count : 2 * count]
    send, recv, local = refs[2 * count :]
    where = place(fold)
    greet(where[4])
    groups = [
        Gather(where, owns[i], fulls[i], send.at[i], recv.at[i], local.at[i]) for i in range(count)
    ]
    for t in range(count + 4):
        for i in range(count):
            if 0 <= t - i <= 4:
                getattr(groups[i], "step%d" % (t - i))()
    for group in groups:
        group.settle()


def scatter_kernel(fold, count, *refs):
    fulls_hbm, outs = refs[:count], refs[count : 2 * count]
    bufs = refs[2 * count : 7 * count]
    send, recv, local = refs[7 * count :]
    where = place(fold)
    greet(where[4])
    groups, loads = [], []
    for i in range(count):
        full, *rest = bufs[5 * i : 5 * i + 5]
        loads.append(pltpu.make_async_copy(fulls_hbm[i], full, local.at[i]))
        loads[-1].start()
        groups.append(Scatter(where, full, rest, send.at[i], recv.at[i]))
    for t in range(count + 4):
        for i in range(count):
            s = t - i
            if s == 0:
                loads[i].wait()
            if 0 <= s < 4:
                getattr(groups[i], "step%d" % s)()
            if s == 4:
                outs[i][...] = groups[i].step4()
    for group in groups:
        group.settle()


def gather_all(fold, blocks):
    count = len(blocks)
    shapes = [(4, 2, 2, 2) + b.shape for b in blocks]
    fulls = pl.pallas_call(
        partial(gather_kernel, fold, count),
        out_shape=[jax.ShapeDtypeStruct(s, BF16) for s in shapes],
        in_specs=[pl.BlockSpec(memory_space=pl.ANY)] * count,
        out_specs=[pl.BlockSpec(memory_space=pl.ANY)] * count,
        scratch_shapes=[
            pltpu.SemaphoreType.DMA((count, 8)),
            pltpu.SemaphoreType.DMA((count, 8)),
            pltpu.SemaphoreType.DMA((count,)),
        ],
        compiler_params=pltpu.CompilerParams(
            collective_id=0, has_side_effects=True, vmem_limit_bytes=8 * 2**20
        ),
    )(*blocks)
    return [f.reshape(-1, f.shape[-1]) for f in fulls]


def scatter_all(fold, parts):
    count = len(parts)
    fulls = [p.reshape(4, 2, 2, 2, p.shape[0] // CELLS, p.shape[1]) for p in parts]
    scratch = []
    for f in fulls:
        r, c = f.shape[-2:]
        for lead in ((4, 2, 2, 2), (4, 2, 2), (4, 2), (4,), (3,)):
            scratch.append(pltpu.VMEM(lead + (r, c), BF16))
    return pl.pallas_call(
        partial(scatter_kernel, fold, count),
        out_shape=[jax.ShapeDtypeStruct(f.shape[-2:], F32) for f in fulls],
        in_specs=[pl.BlockSpec(memory_space=pl.ANY)] * count,
        out_specs=[pl.BlockSpec(memory_space=pltpu.VMEM)] * count,
        scratch_shapes=scratch
        + [
            pltpu.SemaphoreType.DMA((count, 8)),
            pltpu.SemaphoreType.DMA((count, 8)),
            pltpu.SemaphoreType.DMA((count,)),
        ],
        compiler_params=pltpu.CompilerParams(
            collective_id=1, has_side_effects=True, vmem_limit_bytes=58 * 2**20
        ),
    )(*fulls)


def rope_tables(segment_row, head_size):
    length = segment_row.shape[0]
    places = jnp.arange(length, dtype=jnp.int32)
    labels = jnp.arange(4, dtype=jnp.int32)
    counts = jnp.sum((segment_row[:, None] == labels[None, :]).astype(jnp.int32), axis=0)
    before = (labels[None, :] < segment_row[:, None]).astype(jnp.int32)
    starts = jnp.sum(before * counts[None, :], axis=1)
    offsets = (places - starts).astype(F32)
    frequency = 10000.0 ** (-(jnp.arange(head_size // 2, dtype=F32) * 2.0) / head_size)
    angles = offsets[:, None] * frequency[None, :]
    return (jnp.cos(angles), jnp.sin(angles))


def rotate(values, cosine, sine_table):
    half_size = values.shape[-1] // 2
    lower_half = values[..., :half_size]
    upper_half = values[..., half_size:]
    cosine = cosine[..., None, :]
    sine_table = sine_table[..., None, :]
    return jnp.concatenate(
        [
            lower_half * cosine - upper_half * sine_table,
            upper_half * cosine + lower_half * sine_table,
        ],
        axis=-1,
    )


def unrotate(gradient, cosine, sine_table):
    half_size = gradient.shape[-1] // 2
    lower_half = gradient[..., :half_size]
    upper_half = gradient[..., half_size:]
    cosine = cosine[..., None, :]
    sine_table = sine_table[..., None, :]
    return jnp.concatenate(
        [
            lower_half * cosine + upper_half * sine_table,
            upper_half * cosine - lower_half * sine_table,
        ],
        axis=-1,
    )


def head_forward(query_head, key_head, value_head, allowed, score_scale):
    raw_scores = jnp.einsum("le,me->lm", query_head, key_head, preferred_element_type=F32)
    masked = jnp.where(allowed, raw_scores * score_scale, -1e30)
    highest = jnp.max(masked, axis=-1, keepdims=True)
    exponent = jnp.exp(masked - highest)
    denominator = jnp.sum(exponent, axis=-1, keepdims=True)
    weights = (exponent / denominator).astype(BF16)
    mixture = jnp.dot(weights, value_head, preferred_element_type=F32)
    return (mixture, (highest + jnp.log(denominator))[:, 0])


def head_backward(query_head, key_head, value_head, grad_head, logsum, allowed, score_scale):
    raw_scores = jnp.einsum("le,me->lm", query_head, key_head, preferred_element_type=F32)
    masked = jnp.where(allowed, raw_scores * score_scale, -1e30)
    probabilities = jnp.exp(masked - logsum[:, None])
    weights = probabilities.astype(BF16)
    grad_value = jnp.einsum("lm,le->me", weights, grad_head, preferred_element_type=F32)
    grad_probs = jnp.einsum("le,me->lm", grad_head, value_head, preferred_element_type=F32)
    grad_scores = probabilities * (
        grad_probs - jnp.sum(grad_probs * probabilities, axis=-1, keepdims=True)
    )
    grad_scores = grad_scores.astype(BF16)
    grad_query = jnp.dot(grad_scores, key_head, preferred_element_type=F32) * score_scale
    grad_key = (
        jnp.einsum("lm,le->me", grad_scores, query_head, preferred_element_type=F32)
        * score_scale
    )
    return (grad_query, grad_key, grad_value)


def fold_groups(fold):
    return [[c * fold + j for j in range(fold)] for c in range(CELLS)]


def norm_backward(scaled, normed, inverse):
    return inverse * (scaled - normed * jnp.mean(scaled * normed, axis=-1, keepdims=True))


def per_device(
    fold,
    block_input,
    seg_ids,
    gain_attn,
    w_query,
    w_key,
    w_value,
    w_out,
    gain_ffn,
    w_gate,
    w_up,
    w_down,
    cotangent,
):
    row_count, length, width = block_input.shape
    head_count = width // HEAD
    tokens = row_count * length
    score_scale = HEAD ** (-0.5)
    groups = fold_groups(fold)
    gain_one = gain_attn.astype(F32)[:, None]
    gain_two = gain_ffn.astype(F32)[:, None]
    blocks = [
        (w.astype(F32) * gain_one).astype(BF16) for w in (w_query, w_key, w_value)
    ] + [w_out, w_down] + [(w.astype(F32) * gain_two).astype(BF16) for w in (w_gate, w_up)]
    if fold > 1:
        blocks = [
            lax.all_gather(w, "fsdp", axis=0, tiled=True, axis_index_groups=groups) for w in blocks
        ]
    wq, wk, wv, wo, wd, wg, wu = gather_all(fold, blocks)
    cosine, sine_table = jax.vmap(partial(rope_tables, head_size=HEAD))(seg_ids)
    places = jnp.arange(length, dtype=jnp.int32)
    allowed = (seg_ids[:, :, None] == seg_ids[:, None, :]) & (
        places[None, None, :] <= places[None, :, None]
    )
    inputs = block_input.reshape(tokens, width).astype(F32)
    scale_one = lax.rsqrt(jnp.mean(inputs * inputs, axis=-1, keepdims=True) + EPSILON)
    normed_one = inputs * scale_one
    normed_low = normed_one.astype(BF16)
    queries = jnp.dot(normed_low, wq, preferred_element_type=F32).reshape(
        row_count, length, head_count, HEAD
    )
    key_vectors = jnp.dot(normed_low, wk, preferred_element_type=F32).reshape(
        row_count, length, head_count, HEAD
    )
    value_vectors = jnp.dot(normed_low, wv, preferred_element_type=F32).astype(
        BF16
    )
    value_vectors = value_vectors.reshape(row_count, length, head_count, HEAD)
    query_rot = rotate(queries, cosine, sine_table).astype(BF16)
    key_rot = rotate(key_vectors, cosine, sine_table).astype(BF16)
    query_heads = jnp.moveaxis(query_rot, 2, 1)
    key_heads = jnp.moveaxis(key_rot, 2, 1)
    value_heads = jnp.moveaxis(value_vectors, 2, 1)

    def row_forward(operands):
        query_row, key_row, value_row, allowed_row = operands

        def one_head(head_parts):
            return head_forward(
                head_parts[0], head_parts[1], head_parts[2], allowed_row, score_scale
            )

        return lax.map(one_head, (query_row, key_row, value_row))

    mixture, logsum = lax.map(row_forward, (query_heads, key_heads, value_heads, allowed))
    attn_low = jnp.moveaxis(mixture, 1, 2).reshape(tokens, width).astype(BF16)
    middle = inputs + jnp.dot(attn_low, wo, preferred_element_type=F32)
    scale_two = lax.rsqrt(jnp.mean(middle * middle, axis=-1, keepdims=True) + EPSILON)
    normed_two = middle * scale_two
    ffn_low = normed_two.astype(BF16)
    gate_proj = jnp.dot(ffn_low, wg, preferred_element_type=F32)
    up_proj = jnp.dot(ffn_low, wu, preferred_element_type=F32)
    gate_sigm = jax.nn.sigmoid(gate_proj)
    activated = gate_proj * gate_sigm
    hidden = (activated * up_proj).astype(BF16)
    output_full = middle + jnp.dot(hidden, wd, preferred_element_type=F32)
    output = output_full.astype(BF16).reshape(row_count, length, width)
    grad_out = cotangent.reshape(tokens, width).astype(F32)
    grad_low = grad_out.astype(BF16)
    down_grad = jnp.einsum("tf,td->fd", hidden, grad_low, preferred_element_type=F32)
    grad_hidden = jnp.einsum("td,fd->tf", grad_low, wd, preferred_element_type=F32)
    gate_grad_low = (
        grad_hidden * up_proj * gate_sigm * (1.0 + gate_proj * (1.0 - gate_sigm))
    ).astype(BF16)
    up_grad_low = (grad_hidden * activated).astype(BF16)
    gate_grad = jnp.einsum("td,tf->df", ffn_low, gate_grad_low, preferred_element_type=F32)
    up_grad = jnp.einsum("td,tf->df", ffn_low, up_grad_low, preferred_element_type=F32)
    grad_normed_two = jnp.einsum(
        "tf,df->td", gate_grad_low, wg, preferred_element_type=F32
    )
    grad_normed_two = grad_normed_two + jnp.einsum(
        "tf,df->td", up_grad_low, wu, preferred_element_type=F32
    )
    grad_middle = grad_out + norm_backward(
        grad_normed_two, normed_two, scale_two
    )
    branch_low = grad_middle.astype(BF16)
    out_grad = jnp.einsum("te,td->ed", attn_low, branch_low, preferred_element_type=F32)
    grad_attn = jnp.einsum(
        "td,ed->te", branch_low, wo, preferred_element_type=F32
    ).astype(BF16)
    grad_heads = jnp.moveaxis(grad_attn.reshape(row_count, length, head_count, HEAD), 2, 1)

    def row_backward(operands):
        query_row, key_row, value_row, grad_row, logsum_row, allowed_row = operands

        def one_head(head_parts):
            return head_backward(
                head_parts[0],
                head_parts[1],
                head_parts[2],
                head_parts[3],
                head_parts[4],
                allowed_row,
                score_scale,
            )

        return lax.map(one_head, (query_row, key_row, value_row, grad_row, logsum_row))

    grad_query_heads, grad_key_heads, grad_value_heads = lax.map(
        row_backward, (query_heads, key_heads, value_heads, grad_heads, logsum, allowed)
    )
    query_grad_low = (
        unrotate(jnp.moveaxis(grad_query_heads, 1, 2), cosine, sine_table)
        .reshape(tokens, width)
        .astype(BF16)
    )
    key_grad_low = (
        unrotate(jnp.moveaxis(grad_key_heads, 1, 2), cosine, sine_table)
        .reshape(tokens, width)
        .astype(BF16)
    )
    value_grad_low = (
        jnp.moveaxis(grad_value_heads, 1, 2).reshape(tokens, width).astype(BF16)
    )
    query_grad = jnp.einsum(
        "td,te->de", normed_low, query_grad_low, preferred_element_type=F32
    )
    key_grad = jnp.einsum("td,te->de", normed_low, key_grad_low, preferred_element_type=F32)
    value_grad = jnp.einsum(
        "td,te->de", normed_low, value_grad_low, preferred_element_type=F32
    )
    grad_normed_one = jnp.einsum(
        "te,de->td", query_grad_low, wq, preferred_element_type=F32
    )
    grad_normed_one = grad_normed_one + jnp.einsum(
        "te,de->td", key_grad_low, wk, preferred_element_type=F32
    )
    grad_normed_one = grad_normed_one + jnp.einsum(
        "te,de->td", value_grad_low, wv, preferred_element_type=F32
    )
    input_full = grad_middle + norm_backward(
        grad_normed_one, normed_one, scale_one
    )
    input_grad = input_full.astype(BF16).reshape(row_count, length, width)
    parts = scatter_all(
        fold,
        [
            g.astype(BF16)
            for g in (query_grad, key_grad, value_grad, out_grad, down_grad, gate_grad, up_grad)
        ],
    )
    if fold > 1:
        parts = [
            lax.psum_scatter(
                g, "fsdp", scatter_dimension=0, tiled=True, axis_index_groups=groups
            )
            for g in parts
        ]
    dq, dk, dv, do, dd, dg, du = parts
    gain_one_grad = sum(
        jnp.sum(w.astype(F32) * g, axis=1)
        for w, g in ((w_query, dq), (w_key, dk), (w_value, dv))
    )
    gain_two_grad = sum(
        jnp.sum(w.astype(F32) * g, axis=1) for w, g in ((w_gate, dg), (w_up, du))
    )
    return (
        output,
        input_grad,
        gain_one_grad,
        dq * gain_one,
        dk * gain_one,
        dv * gain_one,
        do,
        gain_two_grad,
        dg * gain_two,
        du * gain_two,
        dd,
    )


def solution(mesh):
    fold = mesh.shape["fsdp"] // CELLS
    placed = (
        P("fsdp", None, None),
        P("fsdp", None),
        P("fsdp"),
        P("fsdp", None),
        P("fsdp", None),
        P("fsdp", None),
        P("fsdp", None),
        P("fsdp"),
        P("fsdp", None),
        P("fsdp", None),
        P("fsdp", None),
        P("fsdp", None, None),
    )
    return jax.shard_map(
        partial(per_device, fold),
        mesh=mesh,
        in_specs=placed,
        out_specs=(
            P("fsdp", None, None),
            P("fsdp", None, None),
            P("fsdp"),
            P("fsdp", None),
            P("fsdp", None),
            P("fsdp", None),
            P("fsdp", None),
            P("fsdp"),
            P("fsdp", None),
            P("fsdp", None),
            P("fsdp", None),
        ),
        check_vma=False,
    )
```

```python
from types import SimpleNamespace

import jax
import jax.numpy as jnp
import numpy as np
from jax import lax
from jax.experimental import pallas as pl
from jax.experimental.pallas import tpu as pltpu
from jax.sharding import PartitionSpec as P

AXIS = "fsdp"
HEAD = 64
EPSILON = 1e-05
CELLS = 32
MESH = pl.DeviceIdType.MESH
F32 = jnp.float32
BF16 = jnp.bfloat16
NN = (((1,), (0,)), ((), ()))
NT = (((1,), (1,)), ((), ()))
TN = (((0,), (0,)), ((), ()))
TILE = 112
GAINS, ATT, OUT, DOWN, FFN = 0, (1, 2, 3), 4, 5, (6, 7, 8, 9)
X, Y, CORE = 4, 5, 6


def dot(a, b, dims=NN):
    return lax.dot_general(a, b, dims, preferred_element_type=F32)


def tiles(length, body):
    def step(i, carry):
        body(pl.ds(pl.multiple_of(i * TILE, TILE), TILE))
        return carry

    lax.fori_loop(0, length // TILE, step, 0)


def place(fold):
    me = lax.axis_index(AXIS)
    cell = me // fold
    k = cell % 2
    x = (cell // 2) % 2
    y = (cell // 4) % 2
    z = cell // 8
    ids = {
        CORE: me + (1 - 2 * k) * fold,
        X: me + (1 - 2 * x) * (2 * fold),
        Y: me + (1 - 2 * y) * (4 * fold),
    }
    for r in (1, 2, 3):
        ids[r] = me + ((z + r) % 4 - z) * (8 * fold)
    return z, y, x, k, ids


def greet(ids):
    barrier = pltpu.get_barrier_semaphore()
    for peer in ids.values():
        pl.semaphore_signal(barrier, inc=1, device_id=(peer,), device_id_type=MESH)
    pl.semaphore_wait(barrier, len(ids))


def remote(src, dst, send, recv, peer):
    return pltpu.make_async_remote_copy(
        src_ref=src,
        dst_ref=dst,
        send_sem=send,
        recv_sem=recv,
        device_id=(peer,),
        device_id_type=MESH,
    )


class Exchange:
    def copy(self, slot):
        src, dst, peer = self.route(slot)
        return remote(src, dst, self.send.at[slot], self.recv.at[slot], self.where[4][peer])

    def start(self, *slots):
        for slot in slots:
            self.copy(slot).start()

    def arrive(self, *slots):
        for slot in slots:
            self.copy(slot).wait_recv()

    def settle(self, *slots):
        for slot in slots:
            self.copy(slot).wait_send()


class Gather(Exchange):
    def __init__(self, where, full, send, recv):
        self.where, self.full, self.send, self.recv = where, full, send, recv

    def route(self, slot):
        z, y, x, k, ids = self.where
        half = self.full.shape[-1] // 2
        mine = pl.ds(pl.multiple_of(k * half, 128), half)
        low, high = pl.ds(0, 2), pl.ds(2, 2)
        index, peer = (
            ((z, y, x), 1),
            ((z, y, x), 2),
            ((z, y, x), 3),
            ((low, y, x), Y),
            ((high, y, x), X),
            ((low, slice(None), x), X),
            ((high, y), Y),
            ((), CORE),
        )[slot]
        index = index + (slice(None),) * (4 - len(index)) + (mine,)
        part = self.full.at[index]
        return part, part, peer

    def step(self, n):
        if n == 0:
            self.start(1, 0, 2)
        elif n == 1:
            self.arrive(0, 1, 2)
            self.start(3, 4)
        elif n == 2:
            self.arrive(3, 4)
            self.start(5, 6)
        elif n == 3:
            self.arrive(5, 6)
            self.start(7)
        elif n == 4:
            self.arrive(7)
            self.settle(*range(8))


class Scatter(Exchange):
    def __init__(self, where, full, bufs, send, recv, finish):
        self.where, self.full, self.send, self.recv = where, full, send, recv
        self.r0, self.r1, self.r2, self.r3, self.give, self.r4 = bufs
        self.finish = finish

    def columns(self, k):
        half = self.r0.shape[-1]
        return pl.ds(pl.multiple_of(k * half, 128), half)

    def route(self, slot):
        z, y, x, k, ids = self.where
        low, high = pl.ds(0, 2), pl.ds(2, 2)
        if slot == 0:
            return self.full.at[:, :, :, :, self.columns(1 - k)], self.r0, CORE
        if slot == 1:
            return self.r0.at[low, :, 1 - x], self.r1.at[low], X
        if slot == 2:
            return self.r0.at[high, 1 - y], self.r1.at[high], Y
        if slot == 3:
            return self.r1.at[low, 1 - y], self.r2.at[low], Y
        if slot == 4:
            return self.r1.at[high, 1 - x], self.r2.at[high], X
        if slot == 8:
            return self.give, self.r4, CORE
        r = slot - 4
        return self.r2.at[(z + r) % 4], self.r3.at[r - 1], r

    def total(self):
        total = self.r2[self.where[0]].astype(F32)
        for r in range(3):
            total = total + self.r3[r].astype(F32)
        n = total.shape[0] // 2
        return total[:n], total[n:]

    def step(self, n):
        z, y, x, k, ids = self.where
        r0, r1, r2, full = self.r0, self.r1, self.r2, self.full
        if n == 0:
            self.start(0)
        elif n == 1:
            self.arrive(0)
            mine = self.columns(k)

            def add(i, carry):
                p, q, r = i // 4, (i // 2) % 2, i % 2
                total = r0[p, q, r].astype(F32) + full[p, q, r, :, mine].astype(F32)
                r0[p, q, r] = total.astype(BF16)
                return carry

            lax.fori_loop(0, 16, add, 0)
            self.start(1, 2)
            self.settle(0)
        elif n == 2:
            self.arrive(1, 2)

            def add(i, carry):
                p, q = i // 2, i % 2
                total = r1[p, q].astype(F32) + r0[p, q, x].astype(F32)
                r1[p, q] = total.astype(BF16)
                total = r1[p + 2, q].astype(F32) + r0[p + 2, y, q].astype(F32)
                r1[p + 2, q] = total.astype(BF16)
                return carry

            lax.fori_loop(0, 4, add, 0)
            self.start(3, 4)
        elif n == 3:
            self.arrive(3, 4)
            for p in range(2):
                r2[p] = (r2[p].astype(F32) + r1[p, y].astype(F32)).astype(BF16)
                r2[p + 2] = (r2[p + 2].astype(F32) + r1[p + 2, x].astype(F32)).astype(BF16)
            self.start(6, 5, 7)
        elif n == 4:
            self.arrive(5, 6, 7)
            first, second = self.total()
            self.give[...] = jnp.where(k == 0, second, first)
            self.start(8)
        elif n == 5:
            self.arrive(8)
            first, second = self.total()
            own, other = jnp.where(k == 0, first, second), self.r4[...]
            self.finish(
                jnp.concatenate(
                    [jnp.where(k == 0, own, other), jnp.where(k == 0, other, own)], axis=1
                )
            )
            self.settle(*range(1, 9))


def swap_halves(v):
    lane = lax.broadcasted_iota(jnp.int32, (1, 128), 1)
    return jnp.where(lane % HEAD < HEAD // 2, pltpu.roll(v, 96, 1), pltpu.roll(v, 32, 1))


def attend_forward(p, blocks, r):
    q, k, v, bias, lse = r.q, r.k, r.v, r.bias, r.lse
    cols = pl.ds(pl.multiple_of(p * 128, 128), 128)
    lane = lax.broadcasted_iota(jnp.int32, (1, 128), 1)
    first = lane < HEAD
    for r0, r1, c0, c1 in blocks:
        rows, keys = pl.ds(r0, r1 - r0), pl.ds(c0, c1 - c0)
        q2, k2, v2 = q[rows, cols], k[keys, cols], v[keys, cols]
        mask = bias[rows, pl.ds(0, c1 - c0)].astype(F32)
        mix, logs = [], []
        for mine in (first, ~first):
            s = dot(jnp.where(mine, q2, jnp.zeros_like(q2)), k2, NT) + mask
            top = jnp.max(s, axis=1, keepdims=True)
            e = jnp.exp(s - top)
            total = jnp.sum(e, axis=1, keepdims=True)
            mix.append(dot(e.astype(BF16), v2) * (1.0 / total))
            logs.append(top + jnp.log(total))
        r.attn[rows, cols] = jnp.where(first, mix[0], mix[1]).astype(BF16)
        kept = jnp.where(lane == 2 * p, logs[0], lse[rows, :])
        lse[rows, :] = jnp.where(lane == 2 * p + 1, logs[1], kept)


def attend_backward(p, i, blocks, length, r):
    q, k, v, bias, cos, sin, sums, out = r.q, r.k, r.v, r.bias, r.cos, r.sin, r.gu, r.t2
    cols = pl.ds(pl.multiple_of(p * 128, 128), 128)
    lane = lax.broadcasted_iota(jnp.int32, (1, 128), 1)
    first = lane < HEAD

    def place_of(which):
        return pl.ds(pl.multiple_of(which * 256 + i * 128, 128), 128)

    def clear(rows):
        sums[rows, pl.ds(0, 256)] = jnp.zeros((TILE, 256), F32)

    tiles(length, clear)
    for r0, r1, c0, c1 in blocks:
        rows, keys = pl.ds(r0, r1 - r0), pl.ds(c0, c1 - c0)
        q2, k2, v2, d2 = q[rows, cols], k[keys, cols], v[keys, cols], r.t1[rows, cols]
        both = r.attn[rows, cols].astype(F32) * d2.astype(F32)
        stat = r.lse[rows, :]
        mask = bias[rows, pl.ds(0, c1 - c0)].astype(F32)
        dqs, dks, dvs = [], [], []
        for h, mine in enumerate((first, ~first)):
            delta = jnp.sum(jnp.where(mine, both, 0.0), axis=1, keepdims=True)
            log = jnp.sum(jnp.where(lane == 2 * p + h, stat, 0.0), axis=1, keepdims=True)
            s = dot(jnp.where(mine, q2, jnp.zeros_like(q2)), k2, NT) + mask
            prob = jnp.exp(s - log)
            dp = dot(jnp.where(mine, d2, jnp.zeros_like(d2)), v2, NT)
            ds = (prob * (dp - delta)).astype(BF16)
            dvs.append(dot(prob.astype(BF16), d2, TN))
            dqs.append(dot(ds, k2))
            dks.append(dot(ds, q2, TN))
        dq = jnp.where(first, dqs[0], dqs[1]) * (HEAD**-0.5)
        dq = dq * cos[rows, :] - swap_halves(dq) * sin[rows, :]
        out[rows, place_of(0)] = dq.astype(BF16)
        n = min(c1, length) - c0
        sums[pl.ds(c0, n), pl.ds(0, 128)] += jnp.where(first, dks[0], dks[1])[:n]
        sums[pl.ds(c0, n), pl.ds(128, 128)] += jnp.where(first, dvs[0], dvs[1])[:n]

    def store(rows):
        dk = sums[rows, pl.ds(0, 128)]
        dk = dk * cos[rows, :] - swap_halves(dk) * sin[rows, :]
        out[rows, place_of(1)] = dk.astype(BF16)
        out[rows, place_of(2)] = sums[rows, pl.ds(128, 128)].astype(BF16)

    tiles(length, store)


def layer_kernel(fold, blocks, r):
    x, gy, gain, norms = r.x, r.gy, r.gain, r.norms
    xn, hn, q, kk, v, bias, lse = r.xn, r.hn, r.q, r.k, r.v, r.bias, r.lse
    h1, acc1, acc2, gu, dh, t1, t2 = r.h1, r.acc1, r.acc2, r.gu, r.dh, r.t1, r.t2
    length, width = x.shape
    where = place(fold)
    z, y, xx, k, ids = where
    full = r.full
    flat = [f.reshape(-1, f.shape[-1]) for f in full]
    gather = [Gather(where, f, r.sems[0].at[i], r.sems[1].at[i]) for i, f in enumerate(full)]

    def finish(i):
        def put(total):
            if i in ATT:
                cols = pl.ds(256 * (i - ATT[0]), 256)
                for which, out in enumerate((r.g_q, r.g_k, r.g_v)):
                    out[:, cols] = total[:, 256 * which : 256 * which + 256]
            elif i in FFN:
                n = total.shape[1] // 2
                cols = pl.ds(n * (i - FFN[0]), n)
                r.g_g[:, cols] = total[:, :n]
                r.g_u[:, cols] = total[:, n:]
            else:
                (r.g_o if i == OUT else r.g_d)[...] = total

        return put

    holder = {i: FFN[i - ATT[0]] if i in ATT else i for i in range(1, len(full))}
    scatter = {
        i: Scatter(
            where, full[h], r.bufs[i - 1], r.sems[2].at[i], r.sems[3].at[i], finish(i)
        )
        for i, h in holder.items()
    }

    inputs = (r.gains, r.wq, r.wk, r.wv, r.wo, r.wg, r.wu, r.wd)
    swapped = [
        remote(w, o, r.swap[0].at[i], r.swap[1].at[i], ids[CORE])
        for i, (w, o) in enumerate(zip(inputs, r.other))
    ]

    def own(g):
        n = full[g].shape[-1] // 2
        if g in ATT:
            c = pl.ds(256 * (g - ATT[0]), 256)
            parts = [(1, c), (2, c), (3, c)]
        elif g in FFN:
            c = pl.ds(n * (g - FFN[0]), n)
            parts = [(5, c), (6, c)]
        else:
            parts = [({GAINS: 0, OUT: 4, DOWN: 7}[g], slice(None))]
        a, b = (
            jnp.concatenate([refs[w][:, c].astype(F32) for w, c in parts], axis=1)
            for refs in (inputs, r.other)
        )
        a, b = (jnp.where(k == 0, t[:, :n], t[:, n:]) for t in (a, b))
        both = jnp.concatenate([jnp.where(k == 0, a, b), jnp.where(k == 0, b, a)], axis=0)
        cols = pl.ds(pl.multiple_of(k * n, 128), n)
        full[g][z, y, xx, :, cols] = both.astype(BF16)

    state = {}
    points = iter(SCHEDULE)

    def run(event):
        kind, g, step = event // 100, event // 10 % 10, event % 10
        while state.get((kind, g), 0) <= step:
            n = state.get((kind, g), 0)
            if kind == 0 and n == 0:
                own(g)
            (scatter if kind else gather)[g].step(n)
            state[kind, g] = n + 1

    def point():
        for event in next(points):
            run(event)

    def pairs(body):
        point()

        def step(i, carry):
            @pl.when(i == 1)
            def _():
                point()

            body(i)
            return carry

        lax.fori_loop(0, 2, step, 0)

    point()
    greet(ids)
    for copy in swapped:
        copy.start()

    def norm_one(rows):
        xf = x[rows, :].astype(F32)
        norms[rows, 0:1] = lax.rsqrt(jnp.mean(xf * xf, axis=1, keepdims=True) + EPSILON)
        lse[rows, :] = jnp.zeros((TILE, 128), F32)

    for copy in swapped:
        copy.wait_recv()
    point()
    tiles(length, norm_one)

    point()
    ends, count = [], jnp.zeros((1, 1), F32)
    for label in range(3):
        count = count + jnp.sum((r.seg[...] == label).astype(F32), axis=1, keepdims=True)
        ends.append(count)

    def tables(rows):
        i = lax.broadcasted_iota(jnp.int32, (TILE, 1), 0).astype(F32) + rows.start.astype(F32)
        first = jnp.zeros_like(i)
        for end in ends:
            first = jnp.where(i >= end, end, first)
        angle = (i - first) * r.freq[...]
        lane = lax.broadcasted_iota(jnp.int32, (1, 128), 1)
        r.cos[rows, :] = jnp.cos(angle)
        r.sin[rows, :] = jnp.where(lane % HEAD < HEAD // 2, -1.0, 1.0) * jnp.sin(angle)

    tiles(length, tables)

    def label_of(i):
        return sum((i >= end).astype(F32) for end in ends)

    point()
    for r0, r1, c0, c1 in blocks:
        i = (lax.broadcasted_iota(jnp.int32, (r1 - r0, 1), 0) + r0).astype(F32)
        j = (lax.broadcasted_iota(jnp.int32, (1, c1 - c0), 1) + c0).astype(F32)
        allowed = (label_of(i) == label_of(j)) & (j <= i)
        bias[pl.ds(r0, r1 - r0), pl.ds(0, c1 - c0)] = jnp.where(allowed, 0.0, -1e30).astype(BF16)
    extra = kk.shape[0] - length
    kk[pl.ds(length, extra), :] = jnp.zeros((extra, width), BF16)
    v[pl.ds(length, extra), :] = jnp.zeros((extra, width), BF16)

    point()
    run(10 * GAINS + 4)
    for i in range(2):
        turned = jnp.transpose(flat[GAINS][:, pl.ds(128 * i, 128)].astype(F32))
        gain[i : i + 1, :] = turned[0:1, :]

    def scale_one(rows):
        xn[rows, :] = (x[rows, :].astype(F32) * norms[rows, 0:1] * gain[0:1, :]).astype(BF16)

    tiles(length, scale_one)

    for i, g in enumerate(ATT):
        point()
        run(10 * g + 4)
        gu[:, pl.ds(0, width)] = dot(xn[...], flat[g][...])

        def turn(rows):
            c, s = r.cos[rows, :], r.sin[rows, :]
            for j in range(2):
                cols = pl.ds(256 * i + 128 * j, 128)
                part = gu[rows, pl.ds(128 * j, 128)]
                part = part * c + swap_halves(part) * s
                q[rows, cols] = (part.astype(BF16).astype(F32) * HEAD**-0.5).astype(BF16)
                part = gu[rows, pl.ds(256 + 128 * j, 128)]
                kk[rows, cols] = (part * c + swap_halves(part) * s).astype(BF16)
                v[rows, cols] = gu[rows, pl.ds(512 + 128 * j, 128)].astype(BF16)

        tiles(length, turn)
        pairs(lambda j: attend_forward(2 * i + j, blocks, r))

    point()
    run(10 * OUT + 4)
    h1[...] = dot(r.attn[...], flat[OUT][...])

    def norm_two(rows):
        h = h1[rows, :] + x[rows, :].astype(F32)
        h1[rows, :] = h
        s = lax.rsqrt(jnp.mean(h * h, axis=1, keepdims=True) + EPSILON)
        norms[rows, 1:2] = s
        hn[rows, :] = (h * s * gain[1:2, :]).astype(BF16)

    tiles(length, norm_two)

    chunk = full[FFN[0]].shape[-1] // 2
    for j, g in enumerate(FFN):
        point()
        run(10 * DOWN + 4)
        run(10 * g + 4)
        down = flat[DOWN].at[pl.ds(chunk * j, chunk)]
        gu[...] = dot(hn[...], flat[g][...])
        dh[...] = dot(gy[...], down[...], NT)

        def gated(rows):
            gate, up, d = gu[rows, pl.ds(0, chunk)], gu[rows, pl.ds(chunk, chunk)], dh[rows, :]
            sig = 1.0 / (1.0 + jnp.exp(-gate))
            act = gate * sig
            t1[rows, pl.ds(0, chunk)] = (act * up).astype(BF16)
            t2[rows, pl.ds(0, chunk)] = (d * up * (sig * (1.0 + gate * (1.0 - sig)))).astype(BF16)
            t2[rows, pl.ds(chunk, chunk)] = (d * act).astype(BF16)

        point()
        tiles(length, gated)
        point()
        if j == 0:
            acc1[...] = dot(t1[:, pl.ds(0, chunk)], down[...])
            acc2[...] = dot(t2[...], flat[g][...], NT)
        else:
            acc1[...] += dot(t1[:, pl.ds(0, chunk)], down[...])
            acc2[...] += dot(t2[...], flat[g][...], NT)
        point()
        flat[g][...] = dot(hn[...], t2[...], TN).astype(BF16)
        run(100 + 10 * g)
        point()
        down[...] = dot(t1[:, pl.ds(0, chunk)], gy[...], TN).astype(BF16)
    run(100 + 10 * DOWN)

    def between(rows):
        h, s = h1[rows, :], norms[rows, 1:2]
        t1[rows, :] = (h + acc1[rows, :]).astype(BF16)
        n = h * s
        scaled = acc2[rows, :] * gain[1:2, :]
        d = gy[rows, :].astype(F32) + s * (scaled - n * jnp.mean(scaled * n, axis=1, keepdims=True))
        acc1[rows, :] = d
        hn[rows, :] = d.astype(BF16)

    point()
    tiles(length, between)
    out_copy = pltpu.make_async_copy(t1, r.out, r.local.at[0])
    out_copy.start()
    point()
    out_copy.wait()
    t1[...] = dot(hn[...], flat[OUT][...], NT).astype(BF16)
    point()
    flat[OUT][...] = dot(r.attn[...], hn[...], TN).astype(BF16)
    run(100 + 10 * OUT)

    for i, g in enumerate(ATT):
        pairs(lambda j: attend_backward(2 * i + j, j, blocks, length, r))
        point()
        run(100 + 10 * holder[g] + 1)
        flat[holder[g]][:, pl.ds(0, width)] = dot(xn[...], t2[:, pl.ds(0, width)], TN).astype(BF16)
        run(100 + 10 * g)
        point()
        step = dot(t2[:, pl.ds(0, width)], flat[g][...], NT)
        if i == 0:
            acc2[...] = step
        else:
            acc2[...] += step

    def last(rows):
        s = norms[rows, 0:1]
        n = x[rows, :].astype(F32) * s
        scaled = acc2[rows, :] * gain[0:1, :]
        d = acc1[rows, :] + s * (scaled - n * jnp.mean(scaled * n, axis=1, keepdims=True))
        t1[rows, :] = d.astype(BF16)

    point()
    tiles(length, last)
    in_copy = pltpu.make_async_copy(t1, r.in_grad, r.local.at[0])
    in_copy.start()
    point()
    for step in range(6):
        for g in FFN + (DOWN, OUT) + ATT:
            run(100 + 10 * g + step)
    for copy in swapped:
        copy.wait_send()
    in_copy.wait()


SCHEDULE = (
    (),
    (0, 10, 20,),
    (),
    (1,),
    (11, 2, 30, 21, 12, 40, 3, 22, 50, 4, 31,),
    (13, 41, 23, 14,),
    (32, 42, 24, 60, 70,),
    (51,),
    (33,),
    (43, 61, 34,),
    (71,),
    (44, 52, 80, 62, 90,),
    (72,),
    (),
    (81,),
    (53, 91, 63, 54, 64,),
    (73, 82,),
    (),
    (74, 92,),
    (160, 83,),
    (),
    (93, 161, 84,),
    (),
    (94,),
    (170, 162,),
    (),
    (171, 163,),
    (),
    (),
    (180, 164, 172,),
    (),
    (165, 181, 173,),
    (),
    (),
    (190, 174, 182,),
    (150,),
    (175, 191, 183,),
    (151,),
    (140, 192, 184,),
    (185, 141,),
    (),
    (110, 152, 193,),
    (111, 142,),
    (153, 194,),
    (195, 143, 112,),
    (120,),
    (),
    (154, 113, 121,),
    (155, 144,),
    (130, 114, 145, 122,),
    (),
    (131, 115, 123, 132, 124, 125, 133, 134, 135,),
)


def layer(fold, ins):
    length, width = ins["x"].shape
    hidden = ins["wg"].shape[1]
    rows, drows = ins["wq"].shape[0], ins["wd"].shape[0]
    padded = (length + 127) // 128 * 128
    blocks = ((0, 256, 0, 256), (256, 592, 0, 640), (592, length, 512, padded))
    wide = hidden // 4 * 2
    names = dict(g_q="wq", g_k="wk", g_v="wv", g_o="wo", g_g="wg", g_u="wu", g_d="wd")
    big = jax.ShapeDtypeStruct((length, width), BF16)
    outs = dict(out=big, in_grad=big)
    outs.update({n: jax.ShapeDtypeStruct(ins[w].shape, F32) for n, w in names.items()})
    sizes = [(rows, 256)] + 3 * [(rows, width)] + [(rows, width), (drows, width)] + 4 * [(rows, wide)]
    vmem = pltpu.VMEM
    lead = ((4, 2, 2), (4, 2), (4,), (3,))
    low, wider = vmem((length, width), BF16), vmem((padded, width), BF16)
    lane, high = vmem((length, 128), F32), vmem((length, width), F32)
    sems = pltpu.SemaphoreType.DMA((len(sizes), 9))
    weights = ("gains", "wq", "wk", "wv", "wo", "wg", "wu", "wd")
    scratch = dict(
        full=[vmem((4, 2, 2, 2 * m, c), BF16) for m, c in sizes],
        bufs=[
            [vmem(d + (2 * m, c // 2), BF16) for d in lead] + 2 * [vmem((m, c // 2), F32)]
            for m, c in sizes[1:]
        ],
        other=[vmem(ins[n].shape, BF16) for n in weights],
        sems=4 * [sems],
        swap=2 * [pltpu.SemaphoreType.DMA((8,))],
        local=pltpu.SemaphoreType.DMA((1,)),
        xn=low,
        q=low,
        attn=low,
        hn=low,
        t1=low,
        k=wider,
        v=wider,
        t2=vmem((length, wide), BF16),
        h1=high,
        acc1=high,
        acc2=high,
        gu=vmem((length, wide), F32),
        dh=vmem((length, wide // 2), F32),
        bias=vmem((length, 640), BF16),
        cos=lane,
        sin=lane,
        lse=lane,
        norms=vmem((length, 2), F32),
        gain=vmem((8, width), F32),
    )
    leaves, tree = jax.tree.flatten(scratch)
    given = list(ins) + list(outs)

    def body(*refs):
        named = dict(zip(given, refs), **jax.tree.unflatten(tree, refs[len(given) :]))
        layer_kernel(fold, blocks, SimpleNamespace(**named))

    near, anywhere = pl.BlockSpec(memory_space=vmem), pl.BlockSpec(memory_space=pl.ANY)
    return pl.pallas_call(
        body,
        out_shape=list(outs.values()),
        in_specs=[near] * len(ins),
        out_specs=[anywhere] * 2 + [near] * (len(outs) - 2),
        scratch_shapes=leaves,
        compiler_params=pltpu.CompilerParams(
            collective_id=0, has_side_effects=True, vmem_limit_bytes=62 * 2**20
        ),
    )(*ins.values())


def per_device(
    fold,
    block_input,
    seg_ids,
    gain_attn,
    w_query,
    w_key,
    w_value,
    w_out,
    gain_ffn,
    w_gate,
    w_up,
    w_down,
    cotangent,
):
    row_count, length, width = block_input.shape
    groups = [[c * fold + j for j in range(fold)] for c in range(CELLS)]
    gains = jnp.concatenate(
        [jnp.broadcast_to(g[:, None], (g.shape[0], 128)) for g in (gain_attn, gain_ffn)], axis=1
    )
    blocks = [gains, w_query, w_key, w_value, w_out, w_gate, w_up, w_down]
    if fold > 1:
        blocks = [
            lax.all_gather(w, AXIS, axis=0, tiled=True, axis_index_groups=groups) for w in blocks
        ]
    exponent = (np.arange(HEAD // 2, dtype=np.float32) * np.float32(2.0)) / np.float32(HEAD)
    freq = jnp.asarray(np.tile(np.float32(10000.0) ** -exponent, 4)[None].astype(np.float32))
    gains, wq, wk, wv, wo, wg, wu, wd = blocks
    output, input_grad, *parts = layer(
        fold,
        dict(
            x=block_input.reshape(row_count * length, width),
            seg=seg_ids,
            gains=gains,
            freq=freq,
            wq=wq,
            wk=wk,
            wv=wv,
            wo=wo,
            wg=wg,
            wu=wu,
            wd=wd,
            gy=cotangent.reshape(row_count * length, width),
        ),
    )
    if fold > 1:
        parts = [
            lax.psum_scatter(g, AXIS, scatter_dimension=0, tiled=True, axis_index_groups=groups)
            for g in parts
        ]
    dq, dk, dv, do, dg, du, dd = parts

    def gain_grad(gain, *pairs):
        return sum(jnp.sum(w.astype(F32) * g, axis=1) for w, g in pairs) / gain.astype(F32)

    gain_one_grad = gain_grad(gain_attn, (w_query, dq), (w_key, dk), (w_value, dv))
    gain_two_grad = gain_grad(gain_ffn, (w_gate, dg), (w_up, du))
    output, input_grad = (a.reshape(block_input.shape) for a in (output, input_grad))
    return (output, input_grad, gain_one_grad, dq, dk, dv, do, gain_two_grad, dg, du, dd)


def solution(mesh):
    fold = mesh.shape[AXIS] // CELLS
    rows, flat = P(AXIS, None), P(AXIS)
    cube = P(AXIS, None, None)

    def run(*args):
        return per_device(fold, *args)

    return jax.shard_map(
        run,
        mesh=mesh,
        in_specs=(cube, rows, flat, rows, rows, rows, rows, flat, rows, rows, rows, cube),
        out_specs=(cube, cube, flat, rows, rows, rows, rows, flat, rows, rows, rows),
        check_vma=False,
    )
```

```python
from types import SimpleNamespace

import jax
import jax.numpy as jnp
import numpy as np
from jax import lax
from jax.experimental import pallas as pl
from jax.experimental.pallas import tpu as pltpu
from jax.sharding import PartitionSpec as P

AXIS = "fsdp"
HEAD = 64
EPSILON = 1e-05
CELLS = 32
MESH = pl.DeviceIdType.MESH
F32 = jnp.float32
BF16 = jnp.bfloat16
NN = (((1,), (0,)), ((), ()))
NT = (((1,), (1,)), ((), ()))
TN = (((0,), (0,)), ((), ()))
TILE = 112
GAINS, ATT, OUT, FFN, DOWN = 0, (1, 2, 3), 4, (5, 6, 7, 8), 9
X, Y, CORE = 4, 5, 6


def dot(a, b, dims=NN):
    return lax.dot_general(a, b, dims, preferred_element_type=F32)


def tiles(length, body):
    def step(i, carry):
        body(pl.ds(pl.multiple_of(i * TILE, TILE), TILE))
        return carry

    lax.fori_loop(0, length // TILE, step, 0)


def place(fold):
    me = lax.axis_index(AXIS)
    cell = me // fold
    k = cell % 2
    x = (cell // 2) % 2
    y = (cell // 4) % 2
    z = cell // 8
    ids = {
        CORE: me + (1 - 2 * k) * fold,
        X: me + (1 - 2 * x) * (2 * fold),
        Y: me + (1 - 2 * y) * (4 * fold),
    }
    for r in (1, 2, 3):
        ids[r] = me + ((z + r) % 4 - z) * (8 * fold)
    return z, y, x, k, ids


def greet(ids):
    barrier = pltpu.get_barrier_semaphore()
    for peer in ids.values():
        pl.semaphore_signal(barrier, inc=1, device_id=(peer,), device_id_type=MESH)
    pl.semaphore_wait(barrier, len(ids))


def remote(src, dst, send, recv, peer):
    return pltpu.make_async_remote_copy(
        src_ref=src,
        dst_ref=dst,
        send_sem=send,
        recv_sem=recv,
        device_id=(peer,),
        device_id_type=MESH,
    )


class Exchange:
    def copy(self, slot):
        src, dst, peer = self.route(slot)
        return remote(src, dst, self.send.at[slot], self.recv.at[slot], self.where[4][peer])

    def start(self, *slots):
        for slot in slots:
            self.copy(slot).start()

    def arrive(self, *slots):
        for slot in slots:
            self.copy(slot).wait_recv()

    def settle(self, *slots):
        for slot in slots:
            self.copy(slot).wait_send()


class Gather(Exchange):
    def __init__(self, where, full, send, recv, own):
        self.where, self.full, self.send, self.recv, self.own = where, full, send, recv, own

    def route(self, slot):
        z, y, x, k, ids = self.where
        half = self.full.shape[-1] // 2
        mine = pl.ds(pl.multiple_of(k * half, 128), half)
        low, high = pl.ds(0, 2), pl.ds(2, 2)
        index, peer = (
            ((z, y, x), 1),
            ((z, y, x), 2),
            ((z, y, x), 3),
            ((low, y, x), Y),
            ((high, y, x), X),
            ((low, slice(None), x), X),
            ((high, y), Y),
            ((), CORE),
        )[slot]
        index = index + (slice(None),) * (4 - len(index)) + (mine,)
        part = self.full.at[index]
        return part, part, peer

    def step(self, n):
        if n == 0:
            self.own()
            self.start(1, 0, 2)
        elif n == 1:
            self.arrive(0, 1, 2)
            self.start(3, 4)
        elif n == 2:
            self.arrive(3, 4)
            self.start(5, 6)
        elif n == 3:
            self.arrive(5, 6)
            self.start(7)
        elif n == 4:
            self.arrive(7)
            self.settle(*range(8))


class PlaneGather(Exchange):
    def __init__(self, where, j, full, send, recv, own):
        self.where, self.j, self.full, self.send, self.recv = where, j, full, send, recv
        self.own = own

    def route(self, slot):
        z, y, x, k, ids = self.where
        half, rows = self.full.shape[-1] // 2, self.full.shape[-2]
        mine = pl.ds(pl.multiple_of(k * half, 128), half)
        low, high, every = pl.ds(0, rows // 2), pl.ds(rows // 2, rows // 2), slice(None)
        index, peer = (
            ((y, x, every), 1),
            ((y, x, every), 2),
            ((y, x, every), 3),
            ((y, x, low), Y),
            ((y, x, high), X),
            ((every, x, low), X),
            ((y, every, high), Y),
            ((every, every, every), CORE),
        )[slot]
        part = self.full.at[(self.j,) + index + (mine,)]
        return part, part, peer

    def copy(self, slot):
        src, dst, peer = self.route(slot)
        recv = self.recv.at[max(slot, 2)]
        return remote(src, dst, self.send.at[slot], recv, self.where[4][peer])

    def step(self, n):
        here = self.where[0] == self.j
        if n == 0:

            @pl.when(here)
            def _():
                self.own()
                self.start(1, 0, 2)

        elif n == 1:

            @pl.when(jnp.logical_not(here))
            def _():
                self.arrive(2)

            self.start(3, 4)
        elif n == 2:
            self.arrive(3, 4)
            self.start(5, 6)
        elif n == 3:
            self.arrive(5, 6)
            self.start(7)
        elif n == 4:
            self.arrive(7)
            self.settle(*range(3, 8))

            @pl.when(here)
            def _():
                self.settle(0, 1, 2)


class Scatter(Exchange):
    def __init__(self, where, full, bufs, send, recv, finish):
        self.where, self.full, self.send, self.recv = where, full, send, recv
        self.r0, self.r1, self.r2, self.r3, self.give, self.r4 = bufs
        self.finish = finish

    def columns(self, k):
        half = self.r0.shape[-1]
        return pl.ds(pl.multiple_of(k * half, 128), half)

    def route(self, slot):
        z, y, x, k, ids = self.where
        low, high = pl.ds(0, 2), pl.ds(2, 2)
        if slot == 0:
            return self.full.at[:, :, :, :, self.columns(1 - k)], self.r0, CORE
        if slot == 1:
            return self.r0.at[low, :, 1 - x], self.r1.at[low], X
        if slot == 2:
            return self.r0.at[high, 1 - y], self.r1.at[high], Y
        if slot == 3:
            return self.r1.at[low, 1 - y], self.r2.at[low], Y
        if slot == 4:
            return self.r1.at[high, 1 - x], self.r2.at[high], X
        if slot == 8:
            return self.give, self.r4, CORE
        r = slot - 4
        return self.r2.at[(z + r) % 4], self.r3.at[r - 1], r

    def total(self):
        total = self.r2[self.where[0]].astype(F32)
        for r in range(3):
            total = total + self.r3[r].astype(F32)
        n = total.shape[0] // 2
        return total[:n], total[n:]

    def step(self, n):
        z, y, x, k, ids = self.where
        r0, r1, r2, full = self.r0, self.r1, self.r2, self.full
        if n == 0:
            self.start(0)
        elif n == 1:
            self.arrive(0)
            mine = self.columns(k)

            def add(i, carry):
                p, q, r = i // 4, (i // 2) % 2, i % 2
                total = r0[p, q, r].astype(F32) + full[p, q, r, :, mine].astype(F32)
                r0[p, q, r] = total.astype(BF16)
                return carry

            lax.fori_loop(0, 16, add, 0)
            self.start(1, 2)
            self.settle(0)
        elif n == 2:
            self.arrive(1, 2)

            def add(i, carry):
                p, q = i // 2, i % 2
                total = r1[p, q].astype(F32) + r0[p, q, x].astype(F32)
                r1[p, q] = total.astype(BF16)
                total = r1[p + 2, q].astype(F32) + r0[p + 2, y, q].astype(F32)
                r1[p + 2, q] = total.astype(BF16)
                return carry

            lax.fori_loop(0, 4, add, 0)
            self.start(3, 4)
        elif n == 3:
            self.arrive(3, 4)
            for p in range(2):
                r2[p] = (r2[p].astype(F32) + r1[p, y].astype(F32)).astype(BF16)
                r2[p + 2] = (r2[p + 2].astype(F32) + r1[p + 2, x].astype(F32)).astype(BF16)
            self.start(6, 5, 7)
        elif n == 4:
            self.arrive(5, 6, 7)
            first, second = self.total()
            self.give[...] = jnp.where(k == 0, second, first)
            self.start(8)
        elif n == 5:
            self.arrive(8)
            first, second = self.total()
            own, other = jnp.where(k == 0, first, second), self.r4[...]
            self.finish(
                jnp.concatenate(
                    [jnp.where(k == 0, own, other), jnp.where(k == 0, other, own)], axis=1
                )
            )
            self.settle(*range(1, 9))


def swap_halves(v):
    lane = lax.broadcasted_iota(jnp.int32, (1, 128), 1)
    return jnp.where(lane % HEAD < HEAD // 2, pltpu.roll(v, 96, 1), pltpu.roll(v, 32, 1))


def attend_forward(p, blocks, r):
    q, k, v, bias, lse = r.q, r.k, r.v, r.bias, r.lse
    cols = pl.ds(pl.multiple_of(p * 128, 128), 128)
    lane = lax.broadcasted_iota(jnp.int32, (1, 128), 1)
    first = lane < HEAD
    for r0, r1, c0, c1 in blocks:
        rows, keys = pl.ds(r0, r1 - r0), pl.ds(c0, c1 - c0)
        q2, k2, v2 = q[rows, cols], k[keys, cols], v[keys, cols]
        mask = bias[rows, pl.ds(0, c1 - c0)].astype(F32)
        mix, logs = [], []
        for mine in (first, ~first):
            s = dot(jnp.where(mine, q2, jnp.zeros_like(q2)), k2, NT) + mask
            top = jnp.max(s, axis=1, keepdims=True)
            e = jnp.exp(s - top)
            total = jnp.sum(e, axis=1, keepdims=True)
            mix.append(dot(e.astype(BF16), v2) * (1.0 / total))
            logs.append(top + jnp.log(total))
        r.attn[rows, cols] = jnp.where(first, mix[0], mix[1]).astype(BF16)
        kept = jnp.where(lane == 2 * p, logs[0], lse[rows, :])
        lse[rows, :] = jnp.where(lane == 2 * p + 1, logs[1], kept)


def attend_backward(p, blocks, length, r):
    q, k, v, bias, cos, sin, sums = r.q, r.k, r.v, r.bias, r.cos, r.sin, r.gu
    cols = pl.ds(pl.multiple_of(p * 128, 128), 128)
    lane = lax.broadcasted_iota(jnp.int32, (1, 128), 1)
    first = lane < HEAD

    def clear(rows):
        sums[rows, pl.ds(0, 256)] = jnp.zeros((TILE, 256), F32)

    tiles(length, clear)
    for r0, r1, c0, c1 in blocks:
        rows, keys = pl.ds(r0, r1 - r0), pl.ds(c0, c1 - c0)
        q2, k2, v2, d2 = q[rows, cols], k[keys, cols], v[keys, cols], r.t1[rows, cols]
        both = r.attn[rows, cols].astype(F32) * d2.astype(F32)
        stat = r.lse[rows, :]
        mask = bias[rows, pl.ds(0, c1 - c0)].astype(F32)
        dqs, dks, dvs = [], [], []
        for h, mine in enumerate((first, ~first)):
            delta = jnp.sum(jnp.where(mine, both, 0.0), axis=1, keepdims=True)
            log = jnp.sum(jnp.where(lane == 2 * p + h, stat, 0.0), axis=1, keepdims=True)
            s = dot(jnp.where(mine, q2, jnp.zeros_like(q2)), k2, NT) + mask
            prob = jnp.exp(s - log)
            dp = dot(jnp.where(mine, d2, jnp.zeros_like(d2)), v2, NT)
            ds = (prob * (dp - delta)).astype(BF16)
            dvs.append(dot(prob.astype(BF16), d2, TN))
            dqs.append(dot(ds, k2))
            dks.append(dot(ds, q2, TN))
        dq = jnp.where(first, dqs[0], dqs[1]) * (HEAD**-0.5)
        dq = dq * cos[rows, :] - swap_halves(dq) * sin[rows, :]
        q[rows, cols] = dq.astype(BF16)
        n = min(c1, length) - c0
        sums[pl.ds(c0, n), pl.ds(0, 128)] += jnp.where(first, dks[0], dks[1])[:n]
        sums[pl.ds(c0, n), pl.ds(128, 128)] += jnp.where(first, dvs[0], dvs[1])[:n]

    def store(rows):
        dk = sums[rows, pl.ds(0, 128)]
        dk = dk * cos[rows, :] - swap_halves(dk) * sin[rows, :]
        k[rows, cols] = dk.astype(BF16)
        v[rows, cols] = sums[rows, pl.ds(128, 128)].astype(BF16)

    tiles(length, store)


def layer_kernel(fold, blocks, r):
    x, gy, gain, norms = r.x, r.gy, r.gain, r.norms
    xn, hn, q, kk, v, bias, lse = r.xn, r.hn, r.q, r.k, r.v, r.bias, r.lse
    h1, acc1, acc2, gu, dh, t1, t2 = r.h1, r.acc1, r.acc2, r.gu, r.dh, r.t1, r.t2
    length, width = x.shape
    where = place(fold)
    z, y, xx, k, ids = where
    full = r.full
    flat = [f.reshape(-1, f.shape[-1]) for f in full]

    def finish(i):
        def put(total):
            if i in ATT:
                cols = pl.ds(256 * (i - ATT[0]), 256)
                for which, out in enumerate((r.g_q, r.g_k, r.g_v)):
                    out[:, cols] = total[:, 256 * which : 256 * which + 256]
            elif i in FFN:
                n = total.shape[1] // 2
                cols = pl.ds(n * (i - FFN[0]), n)
                r.g_g[:, cols] = total[:, :n]
                r.g_u[:, cols] = total[:, n:]
            else:
                (r.g_o if i == OUT else r.g_d)[...] = total

        return put

    holder = {i: FFN[i - ATT[0]] if i in ATT else i for i in range(1, len(full))}
    scatter = {
        i: Scatter(
            where, full[h], r.bufs[i - 1], r.sems[2].at[i], r.sems[3].at[i], finish(i)
        )
        for i, h in holder.items()
    }

    for i, g in enumerate((r.ga, r.gf)):
        n = g.shape[1]
        same = lax.broadcasted_iota(jnp.int32, (n, n), 0) == lax.broadcasted_iota(jnp.int32, (n, n), 1)
        column = jnp.sum(jnp.where(same, g[...].astype(F32), 0.0), axis=1, keepdims=True)
        r.gains[:, pl.ds(128 * i, 128)] = jnp.broadcast_to(column, (n, 128)).astype(BF16)
    inputs = (r.gains, r.wq, r.wk, r.wv, r.wo, r.wg, r.wu, r.wd)
    swapped = [
        remote(w, o, r.swap[0].at[i], r.swap[1].at[i], ids[CORE])
        for i, (w, o) in enumerate(zip(inputs, r.other))
    ]

    def own(g):
        n = full[g].shape[-1] // 2
        if g in ATT:
            c = pl.ds(256 * (g - ATT[0]), 256)
            parts = [(1, c), (2, c), (3, c)]
        elif g in FFN:
            c = pl.ds(n * (g - FFN[0]), n)
            parts = [(5, c), (6, c)]
        else:
            parts = [({GAINS: 0, OUT: 4, DOWN: 7}[g], slice(None))]
        a, b = (
            jnp.concatenate([refs[w][:, c].astype(F32) for w, c in parts], axis=1)
            for refs in (inputs, r.other)
        )
        a, b = (jnp.where(k == 0, t[:, :n], t[:, n:]) for t in (a, b))
        both = jnp.concatenate([jnp.where(k == 0, a, b), jnp.where(k == 0, b, a)], axis=0)
        cols = pl.ds(pl.multiple_of(k * n, 128), n)
        full[g][z, y, xx, :, cols] = both.astype(BF16)

    gather = [
        Gather(where, full[i], r.sems[0].at[i], r.sems[1].at[i], lambda i=i: own(i))
        for i in range(DOWN)
    ] + [
        PlaneGather(
            where, j, full[DOWN], r.sems[0].at[DOWN + j], r.sems[1].at[DOWN + j], lambda: own(DOWN)
        )
        for j in range(4)
    ]
    state = {}
    points = iter(SCHEDULE)

    def run(event):
        kind, g, step = event // 1000, event // 10 % 100, event % 10
        while state.get((kind, g), 0) <= step:
            n = state.get((kind, g), 0)
            (scatter if kind else gather)[g].step(n)
            state[kind, g] = n + 1

    def point():
        for event in next(points):
            run(event)

    def pairs(body):
        point()

        def step(i, carry):
            @pl.when(i == 1)
            def _():
                point()

            body(i)
            return carry

        lax.fori_loop(0, 2, step, 0)

    point()
    greet(ids)
    for copy in swapped:
        copy.start()

    def norm_one(rows):
        xf = x[rows, :].astype(F32)
        norms[rows, 0:1] = lax.rsqrt(jnp.mean(xf * xf, axis=1, keepdims=True) + EPSILON)
        lse[rows, :] = jnp.zeros((TILE, 128), F32)

    for copy in swapped[:4]:
        copy.wait_recv()
    point()
    for copy in swapped[4:]:
        copy.wait_recv()
    tiles(length, norm_one)

    point()
    ends, count = [], jnp.zeros((1, 1), F32)
    for label in range(3):
        count = count + jnp.sum((r.seg[...] == label).astype(F32), axis=1, keepdims=True)
        ends.append(count)

    def tables(rows):
        i = lax.broadcasted_iota(jnp.int32, (TILE, 1), 0).astype(F32) + rows.start.astype(F32)
        first = jnp.zeros_like(i)
        for end in ends:
            first = jnp.where(i >= end, end, first)
        angle = (i - first) * r.freq[...]
        lane = lax.broadcasted_iota(jnp.int32, (1, 128), 1)
        r.cos[rows, :] = jnp.cos(angle)
        r.sin[rows, :] = jnp.where(lane % HEAD < HEAD // 2, -1.0, 1.0) * jnp.sin(angle)

    tiles(length, tables)

    def label_of(i):
        return sum((i >= end).astype(F32) for end in ends)

    point()
    for r0, r1, c0, c1 in blocks:
        i = (lax.broadcasted_iota(jnp.int32, (r1 - r0, 1), 0) + r0).astype(F32)
        j = (lax.broadcasted_iota(jnp.int32, (1, c1 - c0), 1) + c0).astype(F32)
        allowed = (label_of(i) == label_of(j)) & (j <= i)
        bias[pl.ds(r0, r1 - r0), pl.ds(0, c1 - c0)] = jnp.where(allowed, 0.0, -1e30).astype(BF16)
    extra = kk.shape[0] - length
    kk[pl.ds(length, extra), :] = jnp.zeros((extra, width), BF16)
    v[pl.ds(length, extra), :] = jnp.zeros((extra, width), BF16)

    point()
    run(10 * GAINS + 4)
    for i in range(2):
        turned = jnp.transpose(flat[GAINS][:, pl.ds(128 * i, 128)].astype(F32))
        gain[i : i + 1, :] = turned[0:1, :]

    def scale_one(rows):
        xn[rows, :] = (x[rows, :].astype(F32) * norms[rows, 0:1] * gain[0:1, :]).astype(BF16)

    tiles(length, scale_one)

    for i, g in enumerate(ATT):
        point()
        run(10 * g + 4)
        gu[:, pl.ds(0, width)] = dot(xn[...], flat[g][...])

        def turn(rows):
            c, s = r.cos[rows, :], r.sin[rows, :]
            for j in range(2):
                cols = pl.ds(256 * i + 128 * j, 128)
                part = gu[rows, pl.ds(128 * j, 128)]
                part = part * c + swap_halves(part) * s
                q[rows, cols] = (part.astype(BF16).astype(F32) * HEAD**-0.5).astype(BF16)
                part = gu[rows, pl.ds(256 + 128 * j, 128)]
                kk[rows, cols] = (part * c + swap_halves(part) * s).astype(BF16)
                v[rows, cols] = gu[rows, pl.ds(512 + 128 * j, 128)].astype(BF16)

        tiles(length, turn)
        pairs(lambda j: attend_forward(2 * i + j, blocks, r))

    point()
    run(10 * OUT + 4)
    h1[...] = dot(r.attn[...], flat[OUT][...])

    def norm_two(rows):
        h = h1[rows, :] + x[rows, :].astype(F32)
        h1[rows, :] = h
        s = lax.rsqrt(jnp.mean(h * h, axis=1, keepdims=True) + EPSILON)
        norms[rows, 1:2] = s
        hn[rows, :] = (h * s * gain[1:2, :]).astype(BF16)

    tiles(length, norm_two)

    chunk = full[FFN[0]].shape[-1] // 2
    for j, g in enumerate(FFN):
        point()
        run(10 * g + 4)
        run(10 * (DOWN + j) + 4)
        down = flat[DOWN].at[pl.ds(chunk * j, chunk)]
        gu[...] = dot(hn[...], flat[g][...])
        dh[...] = dot(gy[...], down[...], NT)

        def gated(rows):
            gate, up, d = gu[rows, pl.ds(0, chunk)], gu[rows, pl.ds(chunk, chunk)], dh[rows, :]
            sig = 1.0 / (1.0 + jnp.exp(-gate))
            act = gate * sig
            t1[rows, pl.ds(0, chunk)] = (act * up).astype(BF16)
            t2[rows, pl.ds(0, chunk)] = (d * up * (sig * (1.0 + gate * (1.0 - sig)))).astype(BF16)
            t2[rows, pl.ds(chunk, chunk)] = (d * act).astype(BF16)

        point()
        tiles(length, gated)
        point()
        if j == 0:
            acc1[...] = dot(t1[:, pl.ds(0, chunk)], down[...])
            acc2[...] = dot(t2[...], flat[g][...], NT)
        else:
            acc1[...] += dot(t1[:, pl.ds(0, chunk)], down[...])
            acc2[...] += dot(t2[...], flat[g][...], NT)
        point()
        flat[g][...] = dot(hn[...], t2[...], TN).astype(BF16)
        run(1000 + 10 * g)
        point()
        down[...] = dot(t1[:, pl.ds(0, chunk)], gy[...], TN).astype(BF16)
    run(1000 + 10 * DOWN)

    def between(rows):
        h, s = h1[rows, :], norms[rows, 1:2]
        t1[rows, :] = (h + acc1[rows, :]).astype(BF16)
        n = h * s
        scaled = acc2[rows, :] * gain[1:2, :]
        d = gy[rows, :].astype(F32) + s * (scaled - n * jnp.mean(scaled * n, axis=1, keepdims=True))
        acc1[rows, :] = d
        hn[rows, :] = d.astype(BF16)

    point()
    tiles(length, between)
    out_copy = pltpu.make_async_copy(t1, r.out, r.local.at[0])
    out_copy.start()
    point()
    out_copy.wait()
    t1[...] = dot(hn[...], flat[OUT][...], NT).astype(BF16)
    point()
    flat[OUT][...] = dot(r.attn[...], hn[...], TN).astype(BF16)
    run(1000 + 10 * OUT)

    def joined(i):
        cols = pl.ds(256 * i, 256)
        return jnp.concatenate([a[pl.ds(0, length), cols] for a in (q, kk, v)], axis=1)

    for i, g in enumerate(ATT):
        pairs(lambda j: attend_backward(2 * i + j, blocks, length, r))
        point()
        run(1000 + 10 * holder[g] + 1)
        flat[holder[g]][:, pl.ds(0, width)] = dot(xn[...], joined(i), TN).astype(BF16)
        run(1000 + 10 * g)
    for i, g in enumerate(ATT):
        point()
        if i == 0:
            acc2[...] = dot(joined(i), flat[g][...], NT)
        else:
            acc2[...] += dot(joined(i), flat[g][...], NT)

    def last(rows):
        s = norms[rows, 0:1]
        n = x[rows, :].astype(F32) * s
        scaled = acc2[rows, :] * gain[0:1, :]
        d = acc1[rows, :] + s * (scaled - n * jnp.mean(scaled * n, axis=1, keepdims=True))
        t1[rows, :] = d.astype(BF16)

    point()
    tiles(length, last)
    in_copy = pltpu.make_async_copy(t1, r.in_grad, r.local.at[0])
    in_copy.start()
    point()
    for step in range(6):
        for g in FFN + (DOWN, OUT) + ATT:
            run(1000 + 10 * g + step)
    for copy in swapped:
        copy.wait_send()
    in_copy.wait()


SCHEDULE = (
    (),
    (0, 10, 20,),
    (30,),
    (1, 11, 90, 50, 40, 2, 21, 12, 60, 110, 31, 22, 3, 4, 13,),
    (100, 32, 91, 70,),
    (80, 14,),
    (51, 23,),
    (41,),
    (33, 24, 92, 52,),
    (34,),
    (42, 93,),
    (61,),
    (),
    (43, 101, 53, 111,),
    (62, 94, 71, 120, 44,),
    (54,),
    (102,),
    (63, 112,),
    (121, 72, 103,),
    (64,),
    (122, 113, 104,),
    (1050, 81,),
    (73,),
    (),
    (114, 74, 123, 1060, 82, 1051,),
    (),
    (124,),
    (),
    (83,),
    (1061, 1070,),
    (84,),
    (1071,),
    (),
    (),
    (1052,),
    (1090, 1080, 1062, 1072,),
    (),
    (),
    (1091,),
    (1063, 1053, 1081,),
    (),
    (1010, 1040, 1073, 1092,),
    (1011, 1041, 1082,),
    (1093,),
    (1020,),
    (1021, 1012,),
    (1083,),
    (1030, 1022, 1042, 1064, 1013,),
    (1031, 1023, 1054,),
    (1084, 1043, 1094, 1032, 1014, 1074, 1033, 1015, 1095,),
    (1055, 1044, 1085, 1045, 1024, 1034, 1075, 1065,),
    (1025, 1035,),
)


def layer(fold, ins):
    length, width = ins["x"].shape
    hidden = ins["wg"].shape[1]
    rows, drows = ins["wq"].shape[0], ins["wd"].shape[0]
    padded = (length + 127) // 128 * 128
    blocks = ((0, 256, 0, 256), (256, 592, 0, 640), (592, length, 512, padded))
    wide = hidden // 4 * 2
    names = dict(g_q="wq", g_k="wk", g_v="wv", g_o="wo", g_g="wg", g_u="wu", g_d="wd")
    big = jax.ShapeDtypeStruct((length, width), BF16)
    outs = dict(out=big, in_grad=big)
    outs.update({n: jax.ShapeDtypeStruct(ins[w].shape, F32) for n, w in names.items()})
    sizes = [(rows, 256)] + 4 * [(rows, width)] + 4 * [(rows, wide)] + [(drows, width)]
    vmem = pltpu.VMEM
    lead = ((4, 2, 2), (4, 2), (4,), (3,))
    low, wider = vmem((length, width), BF16), vmem((padded, width), BF16)
    lane, high = vmem((length, 128), F32), vmem((length, width), F32)
    sems = pltpu.SemaphoreType.DMA((len(sizes) + 3, 9))
    weights = ("wq", "wk", "wv", "wo", "wg", "wu", "wd")
    scratch = dict(
        full=[vmem((4, 2, 2, 2 * m, c), BF16) for m, c in sizes],
        bufs=[
            [vmem(d + (2 * m, c // 2), BF16) for d in lead] + 2 * [vmem((m, c // 2), F32)]
            for m, c in sizes[1:]
        ],
        gains=vmem((rows, 256), BF16),
        other=[vmem((rows, 256), BF16)] + [vmem(ins[n].shape, BF16) for n in weights],
        sems=4 * [sems],
        swap=2 * [pltpu.SemaphoreType.DMA((8,))],
        local=pltpu.SemaphoreType.DMA((1,)),
        xn=low,
        q=low,
        attn=low,
        hn=low,
        t1=low,
        k=wider,
        v=wider,
        t2=vmem((length, wide), BF16),
        h1=high,
        acc1=high,
        acc2=high,
        gu=vmem((length, wide), F32),
        dh=vmem((length, wide // 2), F32),
        bias=vmem((length, 640), BF16),
        cos=lane,
        sin=lane,
        lse=lane,
        norms=vmem((length, 2), F32),
        gain=vmem((8, width), F32),
    )
    leaves, tree = jax.tree.flatten(scratch)
    given = list(ins) + list(outs)

    def body(*refs):
        named = dict(zip(given, refs), **jax.tree.unflatten(tree, refs[len(given) :]))
        layer_kernel(fold, blocks, SimpleNamespace(**named))

    near, anywhere = pl.BlockSpec(memory_space=vmem), pl.BlockSpec(memory_space=pl.ANY)
    return pl.pallas_call(
        body,
        out_shape=list(outs.values()),
        in_specs=[near] * len(ins),
        out_specs=[anywhere] * 2 + [near] * (len(outs) - 2),
        scratch_shapes=leaves,
        compiler_params=pltpu.CompilerParams(
            collective_id=0, has_side_effects=True, vmem_limit_bytes=62 * 2**20
        ),
    )(*ins.values())


def finish_kernel(count, *refs):
    raw, weights, gains = refs[:count], refs[count : count + 5], refs[count + 5 : count + 7]
    outs, sums, sems = refs[count + 7 : 2 * count + 7], refs[2 * count + 7 : -1], refs[-1]
    copies = [pltpu.make_async_copy(a, b, sems.at[i]) for i, (a, b) in enumerate(zip(raw[:2], outs))]
    for copy in copies:
        copy.start()
    for a, b in zip(raw[2:], outs[2:]):
        b[...] = a[...]
    for gain, out, which in zip(gains, sums, ((0, 1, 2), (3, 4))):
        n = gain.shape[1]
        at = (2, 3, 4, 6, 7)
        column = sum(
            jnp.sum(weights[i][...].astype(F32) * raw[at[i]][...], axis=1, keepdims=True)
            for i in which
        )
        same = lax.broadcasted_iota(jnp.int32, (n, n), 0) == lax.broadcasted_iota(jnp.int32, (n, n), 1)
        row = jnp.sum(jnp.where(same, column, 0.0), axis=0, keepdims=True)
        out[...] = row / gain[...].astype(F32)
    for copy in copies:
        copy.wait()


def finish_all(raw, weights, gains):
    near, anywhere = pl.BlockSpec(memory_space=pltpu.VMEM), pl.BlockSpec(memory_space=pl.ANY)
    specs = [anywhere] * 2 + [near] * (len(raw) - 2)
    return pl.pallas_call(
        lambda *refs: finish_kernel(len(raw), *refs),
        out_shape=[jax.ShapeDtypeStruct(a.shape, a.dtype) for a in raw]
        + [jax.ShapeDtypeStruct(g.shape, F32) for g in gains],
        in_specs=specs + [near] * 7,
        out_specs=specs + [near] * 2,
        scratch_shapes=[pltpu.SemaphoreType.DMA((2,))],
        compiler_params=pltpu.CompilerParams(vmem_limit_bytes=16 * 2**20),
    )(*raw, *weights, *gains)


def per_device(
    fold,
    block_input,
    seg_ids,
    gain_attn,
    w_query,
    w_key,
    w_value,
    w_out,
    gain_ffn,
    w_gate,
    w_up,
    w_down,
    cotangent,
):
    row_count, length, width = block_input.shape
    groups = [[c * fold + j for j in range(fold)] for c in range(CELLS)]
    gains = (gain_attn[None], gain_ffn[None])
    blocks = [w_query, w_key, w_value, w_out, w_gate, w_up, w_down]
    if fold > 1:
        blocks = [
            lax.all_gather(w, AXIS, axis=0, tiled=True, axis_index_groups=groups) for w in blocks
        ]
        gains = tuple(
            lax.all_gather(g, AXIS, axis=1, tiled=True, axis_index_groups=groups) for g in gains
        )
    exponent = (np.arange(HEAD // 2, dtype=np.float32) * np.float32(2.0)) / np.float32(HEAD)
    freq = jnp.asarray(np.tile(np.float32(10000.0) ** -exponent, 4)[None].astype(np.float32))
    wq, wk, wv, wo, wg, wu, wd = blocks
    output, input_grad, *parts = layer(
        fold,
        dict(
            x=block_input.reshape(row_count * length, width),
            seg=seg_ids,
            ga=gains[0],
            gf=gains[1],
            freq=freq,
            wq=wq,
            wk=wk,
            wv=wv,
            wo=wo,
            wg=wg,
            wu=wu,
            wd=wd,
            gy=cotangent.reshape(row_count * length, width),
        ),
    )
    if fold > 1:
        parts = [
            lax.psum_scatter(g, AXIS, scatter_dimension=0, tiled=True, axis_index_groups=groups)
            for g in parts
        ]
    output, input_grad, dq, dk, dv, do, dg, du, dd, gain_one, gain_two = finish_all(
        [output, input_grad] + parts,
        (w_query, w_key, w_value, w_gate, w_up),
        (gain_attn[None], gain_ffn[None]),
    )
    output, input_grad = (a.reshape(block_input.shape) for a in (output, input_grad))
    return (output, input_grad, gain_one[0], dq, dk, dv, do, gain_two[0], dg, du, dd)


def solution(mesh):
    fold = mesh.shape[AXIS] // CELLS
    rows, flat = P(AXIS, None), P(AXIS)
    cube = P(AXIS, None, None)

    def run(*args):
        return per_device(fold, *args)

    return jax.shard_map(
        run,
        mesh=mesh,
        in_specs=(cube, rows, flat, rows, rows, rows, rows, flat, rows, rows, rows, cube),
        out_specs=(cube, cube, flat, rows, rows, rows, rows, flat, rows, rows, rows),
        check_vma=False,
    )
```

```python
from types import SimpleNamespace

import jax
import jax.numpy as jnp
import numpy as np
from jax import lax
from jax.experimental import pallas as pl
from jax.experimental.pallas import tpu as pltpu
from jax.sharding import PartitionSpec as P

AXIS = "fsdp"
HEAD = 64
EPSILON = 1e-05
CELLS = 32
MESH = pl.DeviceIdType.MESH
F32 = jnp.float32
BF16 = jnp.bfloat16
NN = (((1,), (0,)), ((), ()))
NT = (((1,), (1,)), ((), ()))
TN = (((0,), (0,)), ((), ()))
TILE = 112
GAINS, ATT, OUT, FFN, DOWN = 0, (1, 2, 3), 4, (5, 6, 7, 8), 9
LAST = (10, 11, 12)
SUMMED = (1, 2, 4, 5, 6, 7, 8, 9) + LAST
X, Y, CORE = 4, 5, 6


def dot(a, b, dims=NN):
    return lax.dot_general(a, b, dims, preferred_element_type=F32)


def tiles(length, body):
    def step(i, carry):
        body(pl.ds(pl.multiple_of(i * TILE, TILE), TILE))
        return carry

    lax.fori_loop(0, length // TILE, step, 0)


def place(fold):
    me = lax.axis_index(AXIS)
    cell = me // fold
    k = cell % 2
    x = (cell // 2) % 2
    y = (cell // 4) % 2
    z = cell // 8
    ids = {
        CORE: me + (1 - 2 * k) * fold,
        X: me + (1 - 2 * x) * (2 * fold),
        Y: me + (1 - 2 * y) * (4 * fold),
    }
    for r in (1, 2, 3):
        ids[r] = me + ((z + r) % 4 - z) * (8 * fold)
    return z, y, x, k, ids


def greet(ids):
    barrier = pltpu.get_barrier_semaphore()
    for peer in ids.values():
        pl.semaphore_signal(barrier, inc=1, device_id=(peer,), device_id_type=MESH)
    pl.semaphore_wait(barrier, len(ids))


def remote(src, dst, send, recv, peer):
    return pltpu.make_async_remote_copy(
        src_ref=src,
        dst_ref=dst,
        send_sem=send,
        recv_sem=recv,
        device_id=(peer,),
        device_id_type=MESH,
    )


class Exchange:
    def copy(self, slot):
        src, dst, peer = self.route(slot)
        return remote(src, dst, self.send.at[slot], self.recv.at[slot], self.where[4][peer])

    def start(self, *slots):
        for slot in slots:
            self.copy(slot).start()

    def arrive(self, *slots):
        for slot in slots:
            self.copy(slot).wait_recv()

    def settle(self, *slots):
        for slot in slots:
            self.copy(slot).wait_send()


class Gather(Exchange):
    def __init__(self, where, full, send, recv, own):
        self.where, self.full, self.send, self.recv, self.own = where, full, send, recv, own

    def route(self, slot):
        z, y, x, k, ids = self.where
        half = self.full.shape[-1] // 2
        mine = pl.ds(pl.multiple_of(k * half, 128), half)
        low, high = pl.ds(0, 2), pl.ds(2, 2)
        index, peer = (
            ((z, y, x), 1),
            ((z, y, x), 2),
            ((z, y, x), 3),
            ((low, y, x), Y),
            ((high, y, x), X),
            ((low, slice(None), x), X),
            ((high, y), Y),
            ((), CORE),
        )[slot]
        index = index + (slice(None),) * (4 - len(index)) + (mine,)
        part = self.full.at[index]
        return part, part, peer

    def step(self, n):
        if n == 0:
            self.own()
            self.start(1, 0, 2)
        elif n == 1:
            self.arrive(0, 1, 2)
            self.start(3, 4)
        elif n == 2:
            self.arrive(3, 4)
            self.start(5, 6)
        elif n == 3:
            self.arrive(5, 6)
            self.start(7)
        elif n == 4:
            self.arrive(7)
            self.settle(*range(8))


class PlaneGather(Exchange):
    def __init__(self, where, j, full, send, recv, own):
        self.where, self.j, self.full, self.send, self.recv = where, j, full, send, recv
        self.own = own

    def route(self, slot):
        z, y, x, k, ids = self.where
        half, rows = self.full.shape[-1] // 2, self.full.shape[-2]
        mine = pl.ds(pl.multiple_of(k * half, 128), half)
        low, high, every = pl.ds(0, rows // 2), pl.ds(rows // 2, rows // 2), slice(None)
        index, peer = (
            ((y, x, every), 1),
            ((y, x, every), 2),
            ((y, x, every), 3),
            ((y, x, low), Y),
            ((y, x, high), X),
            ((every, x, low), X),
            ((y, every, high), Y),
            ((every, every, every), CORE),
        )[slot]
        part = self.full.at[(self.j,) + index + (mine,)]
        return part, part, peer

    def copy(self, slot):
        src, dst, peer = self.route(slot)
        recv = self.recv.at[max(slot, 2)]
        return remote(src, dst, self.send.at[slot], recv, self.where[4][peer])

    def step(self, n):
        here = self.where[0] == self.j
        if n == 0:

            @pl.when(here)
            def _():
                self.own()
                self.start(1, 0, 2)

        elif n == 1:

            @pl.when(jnp.logical_not(here))
            def _():
                self.arrive(2)

            self.start(3, 4)
        elif n == 2:
            self.arrive(3, 4)
            self.start(5, 6)
        elif n == 3:
            self.arrive(5, 6)
            self.start(7)
        elif n == 4:
            self.arrive(7)
            self.settle(*range(3, 8))

            @pl.when(here)
            def _():
                self.settle(0, 1, 2)


class Scatter(Exchange):
    def __init__(self, where, full, base, bufs, send, recv, finish):
        self.where, self.full, self.base = where, full, base
        self.send, self.recv = send, recv
        self.r0, self.r1, self.r2, self.r3, self.give, self.r4 = bufs
        self.finish = finish

    def columns(self, k):
        half = self.r0.shape[-1]
        return pl.ds(pl.multiple_of(self.base + k * half, 128), half)

    def route(self, slot):
        z, y, x, k, ids = self.where
        low, high = pl.ds(0, 2), pl.ds(2, 2)
        if slot == 0:
            return self.full.at[:, :, :, :, self.columns(1 - k)], self.r0, CORE
        if slot == 1:
            return self.r0.at[low, :, 1 - x], self.r1.at[low], X
        if slot == 2:
            return self.r0.at[high, 1 - y], self.r1.at[high], Y
        if slot == 3:
            return self.r1.at[low, 1 - y], self.r2.at[low], Y
        if slot == 4:
            return self.r1.at[high, 1 - x], self.r2.at[high], X
        if slot == 8:
            return self.give, self.r4, CORE
        r = slot - 4
        return self.r2.at[(z + r) % 4], self.r3.at[r - 1], r

    def total(self):
        total = self.r2[self.where[0]].astype(F32)
        for r in range(3):
            total = total + self.r3[r].astype(F32)
        n = total.shape[0] // 2
        return total[:n], total[n:]

    def step(self, n):
        z, y, x, k, ids = self.where
        r0, r1, r2, full = self.r0, self.r1, self.r2, self.full
        if n == 0:
            self.start(0)
        elif n == 1:
            self.arrive(0)
            mine = self.columns(k)

            def add(i, carry):
                p, q, r = i // 4, (i // 2) % 2, i % 2
                total = r0[p, q, r].astype(F32) + full[p, q, r, :, mine].astype(F32)
                r0[p, q, r] = total.astype(BF16)
                return carry

            lax.fori_loop(0, 16, add, 0)
            self.start(1, 2)
            self.settle(0)
        elif n == 2:
            self.arrive(1, 2)

            def add(i, carry):
                p, q = i // 2, i % 2
                total = r1[p, q].astype(F32) + r0[p, q, x].astype(F32)
                r1[p, q] = total.astype(BF16)
                total = r1[p + 2, q].astype(F32) + r0[p + 2, y, q].astype(F32)
                r1[p + 2, q] = total.astype(BF16)
                return carry

            lax.fori_loop(0, 4, add, 0)
            self.start(3, 4)
        elif n == 3:
            self.arrive(3, 4)
            for p in range(2):
                r2[p] = (r2[p].astype(F32) + r1[p, y].astype(F32)).astype(BF16)
                r2[p + 2] = (r2[p + 2].astype(F32) + r1[p + 2, x].astype(F32)).astype(BF16)
            self.start(6, 5, 7)
        elif n == 4:
            self.arrive(5, 6, 7)
            first, second = self.total()
            self.give[...] = jnp.where(k == 0, second, first)
            self.start(8)
        elif n == 5:
            self.arrive(8)
            first, second = self.total()
            own, other = jnp.where(k == 0, first, second), self.r4[...]
            self.finish(
                jnp.concatenate(
                    [jnp.where(k == 0, own, other), jnp.where(k == 0, other, own)], axis=1
                )
            )
            self.settle(*range(1, 9))


def swap_halves(v):
    lane = lax.broadcasted_iota(jnp.int32, (1, 128), 1)
    return jnp.where(lane % HEAD < HEAD // 2, pltpu.roll(v, 96, 1), pltpu.roll(v, 32, 1))


def both_heads(a):
    first = lax.broadcasted_iota(jnp.int32, (1, 128), 1) < HEAD
    zero = jnp.zeros_like(a)
    return jnp.concatenate([jnp.where(first, a, zero), jnp.where(first, zero, a)], axis=0)


def attend_forward(p, blocks, r):
    q, k, v, bias, lse = r.q, r.k, r.v, r.bias, r.lse
    cols = pl.ds(pl.multiple_of(p * 128, 128), 128)
    lane = lax.broadcasted_iota(jnp.int32, (1, 128), 1)
    first = lane < HEAD
    for r0, r1, c0, c1 in blocks:
        rows, keys = pl.ds(r0, r1 - r0), pl.ds(c0, c1 - c0)
        q2, k2, v2 = q[rows, cols], k[keys, cols], v[keys, cols]
        mask = bias[rows, pl.ds(0, c1 - c0)].astype(F32)
        weights, logs, scale = [], [], []
        for mine in (first, ~first):
            s = dot(jnp.where(mine, q2, jnp.zeros_like(q2)), k2, NT) + mask
            top = jnp.max(s, axis=1, keepdims=True)
            e = jnp.exp(s - top)
            total = jnp.sum(e, axis=1, keepdims=True)
            weights.append(e.astype(BF16))
            scale.append(1.0 / total)
            logs.append(top + jnp.log(total))
        mix = dot(jnp.concatenate(weights, axis=1), both_heads(v2))
        r.attn[rows, cols] = (mix * jnp.where(first, scale[0], scale[1])).astype(BF16)
        kept = jnp.where(lane == 2 * p, logs[0], lse[rows, :])
        lse[rows, :] = jnp.where(lane == 2 * p + 1, logs[1], kept)


def attend_backward(p, blocks, length, r):
    q, k, v, bias, cos, sin, sums = r.q, r.k, r.v, r.bias, r.cos, r.sin, r.gu
    cols = pl.ds(pl.multiple_of(p * 128, 128), 128)
    lane = lax.broadcasted_iota(jnp.int32, (1, 128), 1)
    first = lane < HEAD

    def clear(rows):
        sums[rows, pl.ds(0, 256)] = jnp.zeros((TILE, 256), F32)

    tiles(length, clear)
    for r0, r1, c0, c1 in blocks:
        rows, keys = pl.ds(r0, r1 - r0), pl.ds(c0, c1 - c0)
        q2, k2, v2, d2 = q[rows, cols], k[keys, cols], v[keys, cols], r.t1[rows, cols]
        both = r.attn[rows, cols].astype(F32) * d2.astype(F32)
        stat = r.lse[rows, :]
        mask = bias[rows, pl.ds(0, c1 - c0)].astype(F32)
        probs, grads = [], []
        for h, mine in enumerate((first, ~first)):
            delta = jnp.sum(jnp.where(mine, both, 0.0), axis=1, keepdims=True)
            log = jnp.sum(jnp.where(lane == 2 * p + h, stat, 0.0), axis=1, keepdims=True)
            s = dot(jnp.where(mine, q2, jnp.zeros_like(q2)), k2, NT) + mask
            prob = jnp.exp(s - log)
            dp = dot(jnp.where(mine, d2, jnp.zeros_like(d2)), v2, NT)
            grads.append((prob * (dp - delta)).astype(BF16))
            probs.append(prob.astype(BF16))
        dv = dot(jnp.concatenate(probs, axis=0), both_heads(d2), TN)
        dk = dot(jnp.concatenate(grads, axis=0), both_heads(q2), TN)
        dq = dot(jnp.concatenate(grads, axis=1), both_heads(k2)) * (HEAD**-0.5)
        dq = dq * cos[rows, :] - swap_halves(dq) * sin[rows, :]
        q[rows, cols] = dq.astype(BF16)
        n = min(c1, length) - c0
        sums[pl.ds(c0, n), pl.ds(0, 128)] += dk[:n]
        sums[pl.ds(c0, n), pl.ds(128, 128)] += dv[:n]

    def store(rows):
        dk = sums[rows, pl.ds(0, 128)]
        dk = dk * cos[rows, :] - swap_halves(dk) * sin[rows, :]
        k[rows, cols] = dk.astype(BF16)
        v[rows, cols] = sums[rows, pl.ds(128, 128)].astype(BF16)

    tiles(length, store)


def layer_kernel(fold, blocks, r):
    x, gy, gain, norms = r.x, r.gy, r.gain, r.norms
    xn, hn, q, kk, v, bias, lse = r.xn, r.hn, r.q, r.k, r.v, r.bias, r.lse
    h1, acc1, acc2, gu, dh, t1, t2 = r.h1, r.acc1, r.acc2, r.gu, r.dh, r.t1, r.t2
    length, width = x.shape
    where = place(fold)
    z, y, xx, k, ids = where
    full = r.full
    flat = [f.reshape(-1, f.shape[-1]) for f in full]

    def finish(i):
        def put(total):
            if i in ATT:
                cols = pl.ds(256 * (i - ATT[0]), 256)
                for which, out in enumerate((r.g_q, r.g_k, r.g_v)):
                    out[:, cols] = total[:, 256 * which : 256 * which + 256]
            elif i in FFN:
                n = total.shape[1] // 2
                cols = pl.ds(n * (i - FFN[0]), n)
                r.g_g[:, cols] = total[:, :n]
                r.g_u[:, cols] = total[:, n:]
            else:
                (r.g_o if i == OUT else r.g_d)[...] = total

        return put

    def rest(n):
        def put(total):
            (r.g_q, r.g_k, r.g_v)[n][:, pl.ds(256 * (len(ATT) - 1), 256)] = total

        return put

    spots = {i: (full[FFN[i - ATT[0]] if i in ATT else i], 0, finish(i)) for i in SUMMED[:-3]}
    spots.update({LAST[n]: (full[FFN[len(ATT) - 1]], 256 * n, rest(n)) for n in range(3)})
    scatter = {
        i: Scatter(where, f, base, b, r.sems[2].at[i], r.sems[3].at[i], put)
        for (i, (f, base, put)), b in zip(spots.items(), r.bufs)
    }

    for i, g in enumerate((r.ga, r.gf)):
        n = g.shape[1]
        same = lax.broadcasted_iota(jnp.int32, (n, n), 0) == lax.broadcasted_iota(jnp.int32, (n, n), 1)
        column = jnp.sum(jnp.where(same, g[...].astype(F32), 0.0), axis=1, keepdims=True)
        r.gains[:, pl.ds(128 * i, 128)] = jnp.broadcast_to(column, (n, 128)).astype(BF16)
    inputs = (r.gains, r.wq, r.wk, r.wv, r.wo, r.wg, r.wu, r.wd)
    swapped = [
        remote(w, o, r.swap[0].at[i], r.swap[1].at[i], ids[CORE])
        for i, (w, o) in enumerate(zip(inputs, r.other))
    ]

    def own(g):
        n = full[g].shape[-1] // 2
        if g in ATT:
            c = pl.ds(256 * (g - ATT[0]), 256)
            parts = [(1, c), (2, c), (3, c)]
        elif g in FFN:
            c = pl.ds(n * (g - FFN[0]), n)
            parts = [(5, c), (6, c)]
        else:
            parts = [({GAINS: 0, OUT: 4, DOWN: 7}[g], slice(None))]
        a, b = (
            jnp.concatenate([refs[w][:, c].astype(F32) for w, c in parts], axis=1)
            for refs in (inputs, r.other)
        )
        a, b = (jnp.where(k == 0, t[:, :n], t[:, n:]) for t in (a, b))
        both = jnp.concatenate([jnp.where(k == 0, a, b), jnp.where(k == 0, b, a)], axis=0)
        cols = pl.ds(pl.multiple_of(k * n, 128), n)
        full[g][z, y, xx, :, cols] = both.astype(BF16)

    gather = [
        Gather(where, full[i], r.sems[0].at[i], r.sems[1].at[i], lambda i=i: own(i))
        for i in range(DOWN)
    ] + [
        PlaneGather(
            where, j, full[DOWN], r.sems[0].at[DOWN + j], r.sems[1].at[DOWN + j], lambda: own(DOWN)
        )
        for j in range(4)
    ]
    state = {}
    points = iter(SCHEDULE)

    def run(event):
        kind, g, step = event // 1000, event // 10 % 100, event % 10
        while state.get((kind, g), 0) <= step:
            n = state.get((kind, g), 0)
            (scatter if kind else gather)[g].step(n)
            state[kind, g] = n + 1

    def point():
        for event in next(points):
            run(event)

    def pairs(body):
        point()

        def step(i, carry):
            @pl.when(i == 1)
            def _():
                point()

            body(i)
            return carry

        lax.fori_loop(0, 2, step, 0)

    point()
    greet(ids)
    for copy in swapped:
        copy.start()

    def norm_one(rows):
        xf = x[rows, :].astype(F32)
        norms[rows, 0:1] = lax.rsqrt(jnp.mean(xf * xf, axis=1, keepdims=True) + EPSILON)
        lse[rows, :] = jnp.zeros((TILE, 128), F32)

    for copy in swapped[:4]:
        copy.wait_recv()
    point()
    for copy in swapped[4:]:
        copy.wait_recv()
    tiles(length, norm_one)

    point()
    ends, count = [], jnp.zeros((1, 1), F32)
    for label in range(3):
        count = count + jnp.sum((r.seg[...] == label).astype(F32), axis=1, keepdims=True)
        ends.append(count)

    def tables(rows):
        i = lax.broadcasted_iota(jnp.int32, (TILE, 1), 0).astype(F32) + rows.start.astype(F32)
        first = jnp.zeros_like(i)
        for end in ends:
            first = jnp.where(i >= end, end, first)
        angle = (i - first) * r.freq[...]
        lane = lax.broadcasted_iota(jnp.int32, (1, 128), 1)
        r.cos[rows, :] = jnp.cos(angle)
        r.sin[rows, :] = jnp.where(lane % HEAD < HEAD // 2, -1.0, 1.0) * jnp.sin(angle)

    tiles(length, tables)

    def label_of(i):
        return sum((i >= end).astype(F32) for end in ends)

    point()
    for r0, r1, c0, c1 in blocks:
        i = (lax.broadcasted_iota(jnp.int32, (r1 - r0, 1), 0) + r0).astype(F32)
        j = (lax.broadcasted_iota(jnp.int32, (1, c1 - c0), 1) + c0).astype(F32)
        allowed = (label_of(i) == label_of(j)) & (j <= i)
        bias[pl.ds(r0, r1 - r0), pl.ds(0, c1 - c0)] = jnp.where(allowed, 0.0, -1e30).astype(BF16)
    extra = kk.shape[0] - length
    kk[pl.ds(length, extra), :] = jnp.zeros((extra, width), BF16)
    v[pl.ds(length, extra), :] = jnp.zeros((extra, width), BF16)

    point()
    run(10 * GAINS + 4)
    for i in range(2):
        turned = jnp.transpose(flat[GAINS][:, pl.ds(128 * i, 128)].astype(F32))
        gain[i : i + 1, :] = turned[0:1, :]

    def scale_one(rows):
        xn[rows, :] = (x[rows, :].astype(F32) * norms[rows, 0:1] * gain[0:1, :]).astype(BF16)

    tiles(length, scale_one)

    for i, g in enumerate(ATT):
        point()
        run(10 * g + 4)
        gu[:, pl.ds(0, width)] = dot(xn[...], flat[g][...])

        def turn(rows):
            c, s = r.cos[rows, :], r.sin[rows, :]
            for j in range(2):
                cols = pl.ds(256 * i + 128 * j, 128)
                part = gu[rows, pl.ds(128 * j, 128)]
                part = part * c + swap_halves(part) * s
                q[rows, cols] = (part.astype(BF16).astype(F32) * HEAD**-0.5).astype(BF16)
                part = gu[rows, pl.ds(256 + 128 * j, 128)]
                kk[rows, cols] = (part * c + swap_halves(part) * s).astype(BF16)
                v[rows, cols] = gu[rows, pl.ds(512 + 128 * j, 128)].astype(BF16)

        tiles(length, turn)
        pairs(lambda j: attend_forward(2 * i + j, blocks, r))

    point()
    run(10 * OUT + 4)
    h1[...] = dot(r.attn[...], flat[OUT][...])

    def norm_two(rows):
        h = h1[rows, :] + x[rows, :].astype(F32)
        h1[rows, :] = h
        s = lax.rsqrt(jnp.mean(h * h, axis=1, keepdims=True) + EPSILON)
        norms[rows, 1:2] = s
        hn[rows, :] = (h * s * gain[1:2, :]).astype(BF16)

    tiles(length, norm_two)

    chunk = full[FFN[0]].shape[-1] // 2
    for j, g in enumerate(FFN):
        point()
        run(10 * g + 4)
        run(10 * (DOWN + j) + 4)
        down = flat[DOWN].at[pl.ds(chunk * j, chunk)]
        gu[...] = dot(hn[...], flat[g][...])
        dh[...] = dot(gy[...], down[...], NT)

        def gated(rows):
            gate, up, d = gu[rows, pl.ds(0, chunk)], gu[rows, pl.ds(chunk, chunk)], dh[rows, :]
            sig = 1.0 / (1.0 + jnp.exp(-gate))
            act = gate * sig
            t1[rows, pl.ds(0, chunk)] = (act * up).astype(BF16)
            t2[rows, pl.ds(0, chunk)] = (d * up * (sig * (1.0 + gate * (1.0 - sig)))).astype(BF16)
            t2[rows, pl.ds(chunk, chunk)] = (d * act).astype(BF16)

        point()
        tiles(length, gated)
        point()
        if j == 0:
            acc1[...] = dot(t1[:, pl.ds(0, chunk)], down[...])
            acc2[...] = dot(t2[...], flat[g][...], NT)
        else:
            acc1[...] += dot(t1[:, pl.ds(0, chunk)], down[...])
            acc2[...] += dot(t2[...], flat[g][...], NT)
        point()
        flat[g][...] = dot(hn[...], t2[...], TN).astype(BF16)
        run(1000 + 10 * g)
        point()
        down[...] = dot(t1[:, pl.ds(0, chunk)], gy[...], TN).astype(BF16)
    run(1000 + 10 * DOWN)

    def between(rows):
        h, s = h1[rows, :], norms[rows, 1:2]
        t1[rows, :] = (h + acc1[rows, :]).astype(BF16)
        n = h * s
        scaled = acc2[rows, :] * gain[1:2, :]
        d = gy[rows, :].astype(F32) + s * (scaled - n * jnp.mean(scaled * n, axis=1, keepdims=True))
        acc1[rows, :] = d
        hn[rows, :] = d.astype(BF16)

    point()
    tiles(length, between)
    out_copy = pltpu.make_async_copy(t1, r.out, r.local.at[0])
    out_copy.start()
    point()
    out_copy.wait()
    t1[...] = dot(hn[...], flat[OUT][...], NT).astype(BF16)
    point()
    flat[OUT][...] = dot(r.attn[...], hn[...], TN).astype(BF16)
    run(1000 + 10 * OUT)

    def joined(i):
        cols = pl.ds(256 * i, 256)
        return jnp.concatenate([a[pl.ds(0, length), cols] for a in (q, kk, v)], axis=1)

    for i, g in enumerate(ATT):
        pairs(lambda j: attend_backward(2 * i + j, blocks, length, r))
        point()
        place_of = flat[FFN[i]]
        run(1000 + 10 * FFN[i] + 1)
        if g in SUMMED:
            place_of[:, pl.ds(0, width)] = dot(xn[...], joined(i), TN).astype(BF16)
            run(1000 + 10 * g)
        else:
            for n, a in enumerate((q, kk, v)):
                part = a[pl.ds(0, length), pl.ds(256 * i, 256)]
                place_of[:, pl.ds(256 * n, 256)] = dot(xn[...], part, TN).astype(BF16)
                run(1000 + 10 * LAST[n])
                if n < 2:
                    point()
    for i, g in enumerate(ATT):
        point()
        if i == 0:
            acc2[...] = dot(joined(i), flat[g][...], NT)
        else:
            acc2[...] += dot(joined(i), flat[g][...], NT)

    def last(rows):
        s = norms[rows, 0:1]
        n = x[rows, :].astype(F32) * s
        scaled = acc2[rows, :] * gain[0:1, :]
        d = acc1[rows, :] + s * (scaled - n * jnp.mean(scaled * n, axis=1, keepdims=True))
        t1[rows, :] = d.astype(BF16)

    point()
    tiles(length, last)
    in_copy = pltpu.make_async_copy(t1, r.in_grad, r.local.at[0])
    in_copy.start()
    point()
    for step in range(6):
        for g in FFN + (DOWN, OUT) + ATT[:-1] + LAST:
            run(1000 + 10 * g + step)
    for copy in swapped:
        copy.wait_send()
    in_copy.wait()


SCHEDULE = (
    (),
    (0, 10, 1, 20, 2, 30, 11,),
    (40, 50, 3, 21, 12, 90,),
    (60, 100, 4, 31, 70, 80, 22, 13,),
    (41, 32, 110, 120,),
    (14,),
    (51, 23,),
    (42, 91,),
    (24, 33,),
    (52,),
    (),
    (34, 43, 101, 92, 61,),
    (),
    (71, 53, 102, 44,),
    (93,),
    (94, 54, 62,),
    (),
    (103, 111, 72,),
    (81, 104, 121, 63,),
    (),
    (1050, 112, 64,),
    (73,),
    (),
    (82, 122, 1051, 74, 113,),
    (),
    (1060, 114,),
    (83,),
    (123,),
    (),
    (124, 1061, 1070,),
    (84,),
    (1071,),
    (),
    (1062,),
    (1080, 1072, 1052,),
    (1090,),
    (1063, 1081,),
    (),
    (1053, 1040, 1091,),
    (),
    (),
    (1082, 1073,),
    (1092, 1010, 1041, 1083,),
    (1011,),
    (1093, 1020,),
    (1042, 1021,),
    (1012, 1043,),
    (),
    (),
    (1110, 1100, 1120, 1022,),
    (1013, 1111, 1094, 1054, 1121, 1101, 1023,),
    (1112, 1074, 1122, 1102, 1055, 1064, 1014, 1113, 1084, 1123,),
    (1103, 1065, 1095, 1024, 1044,),
    (1124, 1114, 1025, 1075, 1104, 1085, 1125, 1015, 1115, 1045, 1105,),
)


def layer(fold, ins):
    length, width = ins["x"].shape
    hidden = ins["wg"].shape[1]
    rows, drows = ins["wq"].shape[0], ins["wd"].shape[0]
    padded = (length + 127) // 128 * 128
    blocks = ((0, 256, 0, 256), (256, 592, 0, 640), (592, length, 512, padded))
    wide = hidden // 4 * 2
    names = dict(g_q="wq", g_k="wk", g_v="wv", g_o="wo", g_g="wg", g_u="wu", g_d="wd")
    big = jax.ShapeDtypeStruct((length, width), BF16)
    outs = dict(out=big, in_grad=big)
    outs.update({n: jax.ShapeDtypeStruct(ins[w].shape, F32) for n, w in names.items()})
    sizes = [(rows, 256)] + 4 * [(rows, width)] + 4 * [(rows, wide)] + [(drows, width)]
    vmem = pltpu.VMEM
    lead = ((4, 2, 2), (4, 2), (4,), (3,))
    low, wider = vmem((length, width), BF16), vmem((padded, width), BF16)
    lane, high = vmem((length, 128), F32), vmem((length, width), F32)
    sems = pltpu.SemaphoreType.DMA((len(sizes) + 3, 9))
    weights = ("wq", "wk", "wv", "wo", "wg", "wu", "wd")
    scratch = dict(
        full=[vmem((4, 2, 2, 2 * m, c), BF16) for m, c in sizes],
        bufs=[
            [vmem(d + (2 * m, c // 2), BF16) for d in lead] + 2 * [vmem((m, c // 2), F32)]
            for m, c in [sizes[i] for i in SUMMED[:-3]] + 3 * [(rows, 256)]
        ],
        gains=vmem((rows, 256), BF16),
        other=[vmem((rows, 256), BF16)] + [vmem(ins[n].shape, BF16) for n in weights],
        sems=4 * [sems],
        swap=2 * [pltpu.SemaphoreType.DMA((8,))],
        local=pltpu.SemaphoreType.DMA((1,)),
        xn=low,
        q=low,
        attn=low,
        hn=low,
        t1=low,
        k=wider,
        v=wider,
        t2=vmem((length, wide), BF16),
        h1=high,
        acc1=high,
        acc2=high,
        gu=vmem((length, wide), F32),
        dh=vmem((length, wide // 2), F32),
        bias=vmem((length, 640), BF16),
        cos=lane,
        sin=lane,
        lse=lane,
        norms=vmem((length, 2), F32),
        gain=vmem((8, width), F32),
    )
    leaves, tree = jax.tree.flatten(scratch)
    given = list(ins) + list(outs)

    def body(*refs):
        named = dict(zip(given, refs), **jax.tree.unflatten(tree, refs[len(given) :]))
        layer_kernel(fold, blocks, SimpleNamespace(**named))

    near, anywhere = pl.BlockSpec(memory_space=vmem), pl.BlockSpec(memory_space=pl.ANY)
    return pl.pallas_call(
        body,
        out_shape=list(outs.values()),
        in_specs=[near] * len(ins),
        out_specs=[anywhere] * 2 + [near] * (len(outs) - 2),
        scratch_shapes=leaves,
        compiler_params=pltpu.CompilerParams(
            collective_id=0, has_side_effects=True, vmem_limit_bytes=62 * 2**20
        ),
    )(*ins.values())


def finish_kernel(count, *refs):
    raw, weights, gains = refs[:count], refs[count : count + 5], refs[count + 5 : count + 7]
    outs, sums = refs[count + 7 : 2 * count + 7], refs[2 * count + 7 : 2 * count + 9]
    held, sems = refs[2 * count + 9 : -1], refs[-1]
    given = raw + weights
    loads = [pltpu.make_async_copy(a, h, sems.at[i]) for i, (a, h) in enumerate(zip(given, held))]
    stores = [
        pltpu.make_async_copy(h, o, sems.at[len(given) + i])
        for i, (h, o) in enumerate(zip(held, outs))
    ]
    for copy in loads:
        copy.start()
    for i, copy in enumerate(loads):
        copy.wait()
        if i < count:
            stores[i].start()
    for gain, out, which in zip(gains, sums, (((0, 2), (1, 3), (2, 4)), ((3, 6), (4, 7)))):
        n = gain.shape[1]
        column = sum(
            jnp.sum(held[count + w][...].astype(F32) * held[g][...], axis=1, keepdims=True)
            for w, g in which
        )
        same = lax.broadcasted_iota(jnp.int32, (n, n), 0) == lax.broadcasted_iota(jnp.int32, (n, n), 1)
        row = jnp.sum(jnp.where(same, column, 0.0), axis=0, keepdims=True)
        out[...] = row / gain[...].astype(F32)
    for copy in stores:
        copy.wait()


def finish_all(raw, weights, gains):
    near, anywhere = pl.BlockSpec(memory_space=pltpu.VMEM), pl.BlockSpec(memory_space=pl.ANY)
    held = list(raw) + list(weights)
    return pl.pallas_call(
        lambda *refs: finish_kernel(len(raw), *refs),
        out_shape=[jax.ShapeDtypeStruct(a.shape, a.dtype) for a in raw]
        + [jax.ShapeDtypeStruct(g.shape, F32) for g in gains],
        in_specs=[anywhere] * len(held) + [near] * 2,
        out_specs=[anywhere] * len(raw) + [near] * 2,
        scratch_shapes=[pltpu.VMEM(a.shape, a.dtype) for a in held]
        + [pltpu.SemaphoreType.DMA((len(held) + len(raw),))],
        compiler_params=pltpu.CompilerParams(vmem_limit_bytes=62 * 2**20),
    )(*raw, *weights, *gains)


def per_device(
    fold,
    block_input,
    seg_ids,
    gain_attn,
    w_query,
    w_key,
    w_value,
    w_out,
    gain_ffn,
    w_gate,
    w_up,
    w_down,
    cotangent,
):
    row_count, length, width = block_input.shape
    groups = [[c * fold + j for j in range(fold)] for c in range(CELLS)]
    gains = (gain_attn[None], gain_ffn[None])
    blocks = [w_query, w_key, w_value, w_out, w_gate, w_up, w_down]
    if fold > 1:
        blocks = [
            lax.all_gather(w, AXIS, axis=0, tiled=True, axis_index_groups=groups) for w in blocks
        ]
        gains = tuple(
            lax.all_gather(g, AXIS, axis=1, tiled=True, axis_index_groups=groups) for g in gains
        )
    exponent = (np.arange(HEAD // 2, dtype=np.float32) * np.float32(2.0)) / np.float32(HEAD)
    freq = jnp.asarray(np.tile(np.float32(10000.0) ** -exponent, 4)[None].astype(np.float32))
    wq, wk, wv, wo, wg, wu, wd = blocks
    output, input_grad, *parts = layer(
        fold,
        dict(
            x=block_input.reshape(row_count * length, width),
            seg=seg_ids,
            ga=gains[0],
            gf=gains[1],
            freq=freq,
            wq=wq,
            wk=wk,
            wv=wv,
            wo=wo,
            wg=wg,
            wu=wu,
            wd=wd,
            gy=cotangent.reshape(row_count * length, width),
        ),
    )
    if fold > 1:
        parts = [
            lax.psum_scatter(g, AXIS, scatter_dimension=0, tiled=True, axis_index_groups=groups)
            for g in parts
        ]
    output, input_grad, dq, dk, dv, do, dg, du, dd, gain_one, gain_two = finish_all(
        [output, input_grad] + parts,
        (w_query, w_key, w_value, w_gate, w_up),
        (gain_attn[None], gain_ffn[None]),
    )
    output, input_grad = (a.reshape(block_input.shape) for a in (output, input_grad))
    return (output, input_grad, gain_one[0], dq, dk, dv, do, gain_two[0], dg, du, dd)


def solution(mesh):
    fold = mesh.shape[AXIS] // CELLS
    rows, flat = P(AXIS, None), P(AXIS)
    cube = P(AXIS, None, None)

    def run(*args):
        return per_device(fold, *args)

    return jax.shard_map(
        run,
        mesh=mesh,
        in_specs=(cube, rows, flat, rows, rows, rows, rows, flat, rows, rows, rows, cube),
        out_specs=(cube, cube, flat, rows, rows, rows, rows, flat, rows, rows, rows),
        check_vma=False,
    )
```

```python
from types import SimpleNamespace

import jax
import jax.numpy as jnp
import numpy as np
from jax import lax
from jax.experimental import pallas as pl
from jax.experimental.pallas import tpu as pltpu
from jax.sharding import PartitionSpec as P

AXIS = "fsdp"
HEAD = 64
EPSILON = 1e-05
CELLS = 32
MESH = pl.DeviceIdType.MESH
F32 = jnp.float32
BF16 = jnp.bfloat16
NN = (((1,), (0,)), ((), ()))
NT = (((1,), (1,)), ((), ()))
TN = (((0,), (0,)), ((), ()))
TILE = 112
FIRST, ATT, OUT, FFN, DOWN = 0, (1, 2, 3), 4, (5, 6, 7, 8), 9
LAST = (10, 11, 12)
SUMMED = (1, 2, 4, 5, 6, 7, 8, 9) + LAST
X, Y, CORE = 4, 5, 6


def dot(a, b, dims=NN):
    return lax.dot_general(a, b, dims, preferred_element_type=F32)


def tiles(length, body):
    def step(i, carry):
        body(pl.ds(pl.multiple_of(i * TILE, TILE), TILE))
        return carry

    lax.fori_loop(0, length // TILE, step, 0)


def place(fold):
    me = lax.axis_index(AXIS)
    cell = me // fold
    k = cell % 2
    x = (cell // 2) % 2
    y = (cell // 4) % 2
    z = cell // 8
    ids = {
        CORE: me + (1 - 2 * k) * fold,
        X: me + (1 - 2 * x) * (2 * fold),
        Y: me + (1 - 2 * y) * (4 * fold),
    }
    for r in (1, 2, 3):
        ids[r] = me + ((z + r) % 4 - z) * (8 * fold)
    return z, y, x, k, ids


def greet(ids):
    barrier = pltpu.get_barrier_semaphore()
    for peer in ids.values():
        pl.semaphore_signal(barrier, inc=1, device_id=(peer,), device_id_type=MESH)
    pl.semaphore_wait(barrier, len(ids))


def remote(src, dst, send, recv, peer):
    return pltpu.make_async_remote_copy(
        src_ref=src,
        dst_ref=dst,
        send_sem=send,
        recv_sem=recv,
        device_id=(peer,),
        device_id_type=MESH,
    )


class Exchange:
    def copy(self, slot):
        src, dst, peer = self.route(slot)
        n = self.lanes[slot]
        return remote(src, dst, self.send.at[n], self.recv.at[n], self.where[4][peer])

    def start(self, *slots):
        for slot in slots:
            self.copy(slot).start()

    def pair(self, ref, lane):
        return remote(ref, ref, self.send.at[lane], self.recv.at[lane], self.where[4][CORE])

    def arrive(self, lane):
        self.pair(self.whole(lane), lane).wait_recv()

    def settle(self, *lanes):
        for lane in lanes:
            self.pair(self.whole(lane), lane).wait_send()


class Gather(Exchange):
    lanes = (0, 0, 0, 1, 1, 2, 2, 3)

    def __init__(self, where, full, send, recv, own):
        self.where, self.full, self.send, self.recv, self.own = where, full, send, recv, own

    def route(self, slot):
        z, y, x, k, ids = self.where
        half = self.full.shape[-1] // 2
        mine = pl.ds(pl.multiple_of(k * half, 128), half)
        low, high = pl.ds(0, 2), pl.ds(2, 2)
        index, peer = (
            ((z, y, x), 1),
            ((z, y, x), 2),
            ((z, y, x), 3),
            ((low, y, x), Y),
            ((high, y, x), X),
            ((low, slice(None), x), X),
            ((high, y), Y),
            ((), CORE),
        )[slot]
        index = index + (slice(None),) * (4 - len(index)) + (mine,)
        part = self.full.at[index]
        return part, part, peer

    def whole(self, lane):
        z, y, x, k, ids = self.where
        half = self.full.shape[-1] // 2
        every = slice(None)
        index = ((pl.ds(0, 3), y, x), (every, y, x), (every, every, x), (every, every, every))[lane]
        return self.full.at[index + (every, pl.ds(0, half))]

    def step(self, n):
        if n > 0:
            self.arrive(n - 1)
        if n == 0:
            self.own()
            self.start(1, 0, 2)
        elif n == 1:
            self.start(3, 4)
        elif n == 2:
            self.start(5, 6)
        elif n == 3:
            self.start(7)
        elif n == 4:
            self.settle(*range(4))


class PlaneGather(Exchange):
    lanes = Gather.lanes

    def __init__(self, where, j, full, send, recv, own):
        self.where, self.j, self.full, self.send, self.recv = where, j, full, send, recv
        self.own = own

    def route(self, slot):
        z, y, x, k, ids = self.where
        half, rows = self.full.shape[-1] // 2, self.full.shape[-2]
        mine = pl.ds(pl.multiple_of(k * half, 128), half)
        low, high, every = pl.ds(0, rows // 2), pl.ds(rows // 2, rows // 2), slice(None)
        index, peer = (
            ((y, x, every), 1),
            ((y, x, every), 2),
            ((y, x, every), 3),
            ((y, x, low), Y),
            ((y, x, high), X),
            ((every, x, low), X),
            ((y, every, high), Y),
            ((every, every, every), CORE),
        )[slot]
        part = self.full.at[(self.j,) + index + (mine,)]
        return part, part, peer

    def whole(self, lane):
        z, y, x, k, ids = self.where
        half, every = self.full.shape[-1] // 2, slice(None)
        index = ((y, x), (y, x), (every, x), (every, every))[lane]
        return self.full.at[(self.j,) + index + (every, pl.ds(0, half))]

    def step(self, n):
        z, y, x, k, ids = self.where
        here = z == self.j
        if n == 0:

            @pl.when(here)
            def _():
                self.own()
                self.start(1, 0, 2)

        elif n == 1:

            @pl.when(jnp.logical_not(here))
            def _():
                self.arrive(0)

            self.start(3, 4)
        elif n == 2:
            self.arrive(1)
            self.start(5, 6)
        elif n == 3:
            self.arrive(2)
            self.start(7)
        elif n == 4:
            self.arrive(3)
            self.settle(1, 2, 3)

            @pl.when(here)
            def _():
                half = self.full.shape[-1] // 2
                three = self.full.at[pl.ds(0, 3), y, x, :, pl.ds(0, half)]
                self.pair(three, 0).wait_send()


class Scatter(Exchange):
    lanes = (0, 1, 1, 2, 2, 3, 3, 3, 4)

    def __init__(self, where, full, base, bufs, send, recv, finish):
        self.where, self.full, self.base = where, full, base
        self.send, self.recv = send, recv
        self.r0, self.r1, self.r2, self.r3, self.give, self.r4 = bufs
        self.finish = finish

    def columns(self, k):
        half = self.r0.shape[-1]
        return pl.ds(pl.multiple_of(self.base + k * half, 128), half)

    def route(self, slot):
        z, y, x, k, ids = self.where
        low, high = pl.ds(0, 2), pl.ds(2, 2)
        if slot == 0:
            return self.full.at[:, :, :, :, self.columns(1 - k)], self.r0, CORE
        if slot == 1:
            return self.r0.at[low, :, 1 - x], self.r1.at[low], X
        if slot == 2:
            return self.r0.at[high, 1 - y], self.r1.at[high], Y
        if slot == 3:
            return self.r1.at[low, 1 - y], self.r2.at[low], Y
        if slot == 4:
            return self.r1.at[high, 1 - x], self.r2.at[high], X
        if slot == 8:
            return self.give, self.r4, CORE
        r = slot - 4
        return self.r2.at[(z + r) % 4], self.r3.at[r - 1], r

    def whole(self, lane):
        return (self.r0, self.r1, self.r2, self.r3, self.r4)[lane]

    def total(self):
        total = self.r2[self.where[0]].astype(F32)
        for r in range(3):
            total = total + self.r3[r].astype(F32)
        n = total.shape[0] // 2
        return total[:n], total[n:]

    def step(self, n):
        z, y, x, k, ids = self.where
        r0, r1, r2, full = self.r0, self.r1, self.r2, self.full
        if n == 0:
            self.start(0)
        elif n == 1:
            self.arrive(0)
            mine = self.columns(k)

            def add(i, carry):
                p, q, r = i // 4, (i // 2) % 2, i % 2
                r0[p, q, r] = r0[p, q, r] + full[p, q, r, :, mine]
                return carry

            lax.fori_loop(0, 16, add, 0)
            self.start(1, 2)
            self.settle(0)
        elif n == 2:
            self.arrive(1)

            def add(i, carry):
                p, q = i // 2, i % 2
                r1[p, q] = r1[p, q] + r0[p, q, x]
                r1[p + 2, q] = r1[p + 2, q] + r0[p + 2, y, q]
                return carry

            lax.fori_loop(0, 4, add, 0)
            self.start(3, 4)
        elif n == 3:
            self.arrive(2)
            for p in range(2):
                r2[p] = r2[p] + r1[p, y]
                r2[p + 2] = r2[p + 2] + r1[p + 2, x]
            self.start(6, 5, 7)
        elif n == 4:
            self.arrive(3)
            first, second = self.total()
            self.give[...] = jnp.where(k == 0, second, first)
            self.start(8)
        elif n == 5:
            self.arrive(4)
            first, second = self.total()
            own, other = jnp.where(k == 0, first, second), self.r4[...]
            self.finish(
                jnp.concatenate(
                    [jnp.where(k == 0, own, other), jnp.where(k == 0, other, own)], axis=1
                )
            )
            self.settle(*range(1, 5))


def regroup(v):
    lane = lax.broadcasted_iota(jnp.int32, (1, 128), 1)
    parts = []
    for i in range(v.shape[1] // 128):
        t = v[:, 128 * i : 128 * i + 128]
        down, up = pltpu.roll(t, 96, 1), pltpu.roll(t, 32, 1)
        middle = jnp.where(lane < HEAD, down, up)
        parts.append(jnp.where((lane >= HEAD // 2) & (lane < 3 * HEAD // 2), middle, t))
    return jnp.concatenate(parts, axis=1)


def swap_halves(v):
    return pltpu.roll(v, HEAD, 1)


def heads():
    lane = lax.broadcasted_iota(jnp.int32, (1, 128), 1)
    return lane < HEAD, lane % HEAD < HEAD // 2


def both_heads(a, first):
    zero = jnp.zeros_like(a)
    return jnp.concatenate([jnp.where(first, a, zero), jnp.where(first, zero, a)], axis=0)


def attend_forward(p, blocks, r):
    q, k, v, bias, lse = r.q, r.k, r.v, r.bias, r.lse
    cols = pl.ds(pl.multiple_of(p * 128, 128), 128)
    lane = lax.broadcasted_iota(jnp.int32, (1, 128), 1)
    first, even = heads()
    for r0, r1, c0, c1 in blocks:
        rows, keys = pl.ds(r0, r1 - r0), pl.ds(c0, c1 - c0)
        q2, k2, v2 = q[rows, cols], k[keys, cols], v[keys, cols]
        mask = bias[rows, pl.ds(0, c1 - c0)].astype(F32)
        weights, logs, scale = [], [], []
        for mine in (even, ~even):
            s = dot(jnp.where(mine, q2, jnp.zeros_like(q2)), k2, NT) + mask
            top = jnp.max(s, axis=1, keepdims=True)
            e = jnp.exp(s - top)
            total = jnp.sum(e, axis=1, keepdims=True)
            weights.append(e.astype(BF16))
            scale.append(1.0 / total)
            logs.append(top + jnp.log(total))
        mix = dot(jnp.concatenate(weights, axis=1), both_heads(v2, first))
        r.attn[rows, cols] = (mix * jnp.where(first, scale[0], scale[1])).astype(BF16)
        kept = jnp.where(lane == 2 * p, logs[0], lse[rows, :])
        lse[rows, :] = jnp.where(lane == 2 * p + 1, logs[1], kept)


def attend_backward(p, blocks, length, r):
    q, k, v, bias, cos, sin, sums = r.q, r.k, r.v, r.bias, r.cos, r.sin, r.gu
    cols = pl.ds(pl.multiple_of(p * 128, 128), 128)
    lane = lax.broadcasted_iota(jnp.int32, (1, 128), 1)
    first, even = heads()

    def clear(rows):
        sums[rows, pl.ds(0, 256)] = jnp.zeros((TILE, 256), F32)

    tiles(length, clear)
    for r0, r1, c0, c1 in blocks:
        rows, keys = pl.ds(r0, r1 - r0), pl.ds(c0, c1 - c0)
        q2, k2, v2, d2 = q[rows, cols], k[keys, cols], v[keys, cols], r.t1[rows, cols]
        both = r.attn[rows, cols].astype(F32) * d2.astype(F32)
        stat = r.lse[rows, :]
        mask = bias[rows, pl.ds(0, c1 - c0)].astype(F32)
        probs, grads = [], []
        for h, (mine, part) in enumerate(((first, even), (~first, ~even))):
            delta = jnp.sum(jnp.where(mine, both, 0.0), axis=1, keepdims=True)
            log = jnp.sum(jnp.where(lane == 2 * p + h, stat, 0.0), axis=1, keepdims=True)
            s = dot(jnp.where(part, q2, jnp.zeros_like(q2)), k2, NT) + mask
            prob = jnp.exp(s - log)
            dp = dot(jnp.where(mine, d2, jnp.zeros_like(d2)), v2, NT)
            grads.append((prob * (dp - delta)).astype(BF16))
            probs.append(prob.astype(BF16))
        dv = dot(jnp.concatenate(probs, axis=0), both_heads(d2, first), TN)
        dk = dot(jnp.concatenate(grads, axis=0), both_heads(q2, even), TN)
        dq = dot(jnp.concatenate(grads, axis=1), both_heads(k2, even)) * (HEAD**-0.5)
        dq = dq * cos[rows, :] - swap_halves(dq) * sin[rows, :]
        q[rows, cols] = dq.astype(BF16)
        n = min(c1, length) - c0
        sums[pl.ds(c0, n), pl.ds(0, 128)] += dk[:n]
        sums[pl.ds(c0, n), pl.ds(128, 128)] += dv[:n]

    def store(rows):
        dk = sums[rows, pl.ds(0, 128)]
        dk = dk * cos[rows, :] - swap_halves(dk) * sin[rows, :]
        k[rows, cols] = dk.astype(BF16)
        v[rows, cols] = sums[rows, pl.ds(128, 128)].astype(BF16)

    tiles(length, store)


def layer_kernel(fold, blocks, r):
    x, gy, gain, norms = r.x_near, r.gy_near, r.gain, r.norms
    far = (r.wq, r.wk, r.wv, r.wo, r.wg, r.wu, r.wd)
    loads = [
        pltpu.make_async_copy(a, b, r.local.at[1 + i])
        for i, (a, b) in enumerate(zip(far + (r.x, r.gy), r.near + [x, gy]))
    ]
    for copy in loads:
        copy.start()
    xn, hn, q, kk, v, bias, lse = r.xn, r.hn, r.q, r.k, r.v, r.bias, r.lse
    h1, acc1, acc2, gu, dh, t1, t2 = r.h1, r.acc1, r.acc2, r.gu, r.dh, r.t1, r.t2
    length, width = x.shape
    where = place(fold)
    z, y, xx, k, ids = where
    full = r.full
    flat = [f.reshape(-1, f.shape[-1]) for f in full]

    def finish(i):
        def put(total):
            if i in ATT:
                cols = pl.ds(256 * (i - ATT[0]), 256)
                r.g_q[:, cols] = regroup(total[:, 0:256])
                r.g_k[:, cols] = regroup(total[:, 256:512])
                r.g_v[:, cols] = total[:, 512:768]
            elif i in FFN:
                n = total.shape[1] // 2
                cols = pl.ds(n * (i - FFN[0]), n)
                r.g_g[:, cols] = total[:, :n]
                r.g_u[:, cols] = total[:, n:]
            else:
                (r.g_o if i == OUT else r.g_d)[...] = total

        return put

    def rest(n):
        def put(total):
            cols = pl.ds(256 * (len(ATT) - 1), 256)
            (r.g_q, r.g_k, r.g_v)[n][:, cols] = regroup(total) if n < 2 else total

        return put

    spots = {i: (full[FFN[i - ATT[0]] if i in ATT else i], 0, finish(i)) for i in SUMMED[:-3]}
    spots.update({LAST[n]: (full[FFN[len(ATT) - 1]], 256 * n, rest(n)) for n in range(3)})
    scatter = {
        i: Scatter(where, f, base, b, r.sems[2].at[n], r.sems[3].at[n], put)
        for n, ((i, (f, base, put)), b) in enumerate(zip(spots.items(), r.bufs))
    }

    for i, g in enumerate((r.ga, r.gf)):
        n = g.shape[1]
        same = lax.broadcasted_iota(jnp.int32, (n, n), 0) == lax.broadcasted_iota(jnp.int32, (n, n), 1)
        column = jnp.sum(jnp.where(same, g[...].astype(F32), 0.0), axis=1, keepdims=True)
        r.gains[:, pl.ds(128 * i, 128)] = jnp.broadcast_to(column, (n, 128)).astype(BF16)
    inputs = [r.gains] + r.near
    swapped = [
        remote(w, o, r.swap[0].at[i], r.swap[1].at[i], ids[CORE])
        for i, (w, o) in enumerate(zip((r.gains,) + far, r.other))
    ]

    def own(g):
        n = full[g].shape[-1] // 2
        if g == FIRST:
            c = pl.ds(0, 256)
            parts = [(1, c, regroup), (2, c, regroup), (0, c, None)]
        elif g == ATT[0]:
            parts = [(3, pl.ds(0, 256), None)]
        elif g in ATT:
            c = pl.ds(256 * (g - ATT[0]), 256)
            parts = [(1, c, regroup), (2, c, regroup), (3, c, None)]
        elif g in FFN:
            c = pl.ds(n * (g - FFN[0]), n)
            parts = [(5, c, None), (6, c, None)]
        else:
            parts = [({OUT: 4, DOWN: 7}[g], slice(None), None)]

        def row(refs):
            values = [(refs[w][:, c].astype(F32), f) for w, c, f in parts]
            return jnp.concatenate([f(t) if f else t for t, f in values], axis=1)

        a, b = row(inputs), row(r.other)
        a, b = (jnp.where(k == 0, t[:, :n], t[:, n:]) for t in (a, b))
        both = jnp.concatenate([jnp.where(k == 0, a, b), jnp.where(k == 0, b, a)], axis=0)
        cols = pl.ds(pl.multiple_of(k * n, 128), n)
        full[g][z, y, xx, :, cols] = both.astype(BF16)

    gather = [
        Gather(where, full[i], r.sems[0].at[i], r.sems[1].at[i], lambda i=i: own(i))
        for i in range(DOWN)
    ] + [
        PlaneGather(
            where, j, full[DOWN], r.sems[0].at[DOWN + j], r.sems[1].at[DOWN + j], lambda: own(DOWN)
        )
        for j in range(4)
    ]
    state = {}
    points = iter(SCHEDULE)

    def run(event):
        kind, g, step = event // 1000, event // 10 % 100, event % 10
        while state.get((kind, g), 0) <= step:
            n = state.get((kind, g), 0)
            (scatter if kind else gather)[g].step(n)
            state[kind, g] = n + 1

    def point():
        for event in next(points):
            run(event)

    def pairs(body):
        point()

        def step(i, carry):
            @pl.when(i == 1)
            def _():
                point()

            body(i)
            return carry

        lax.fori_loop(0, 2, step, 0)

    point()
    greet(ids)
    for copy in swapped:
        copy.start()

    def norm_one(rows):
        xf = x[rows, :].astype(F32)
        norms[rows, 0:1] = lax.rsqrt(jnp.mean(xf * xf, axis=1, keepdims=True) + EPSILON)
        lse[rows, :] = jnp.zeros((TILE, 128), F32)

    loads[-2].wait()
    tiles(length, norm_one)
    for copy in loads[:-2]:
        copy.wait()
    for copy in swapped:
        copy.wait_recv()
    point()

    point()
    ends, count = [], jnp.zeros((1, 1), F32)
    for label in range(3):
        count = count + jnp.sum((r.seg[...] == label).astype(F32), axis=1, keepdims=True)
        ends.append(count)

    def tables(rows):
        i = lax.broadcasted_iota(jnp.int32, (TILE, 1), 0).astype(F32) + rows.start.astype(F32)
        first = jnp.zeros_like(i)
        for end in ends:
            first = jnp.where(i >= end, end, first)
        angle = (i - first) * r.freq[...]
        lane = lax.broadcasted_iota(jnp.int32, (1, 128), 1)
        r.cos[rows, :] = jnp.cos(angle)
        r.sin[rows, :] = jnp.where(lane < HEAD, -1.0, 1.0) * jnp.sin(angle)

    tiles(length, tables)

    def label_of(i):
        return sum((i >= end).astype(F32) for end in ends)

    point()
    for r0, r1, c0, c1 in blocks:
        i = (lax.broadcasted_iota(jnp.int32, (r1 - r0, 1), 0) + r0).astype(F32)
        j = (lax.broadcasted_iota(jnp.int32, (1, c1 - c0), 1) + c0).astype(F32)
        allowed = (label_of(i) == label_of(j)) & (j <= i)
        bias[pl.ds(r0, r1 - r0), pl.ds(0, c1 - c0)] = jnp.where(allowed, 0.0, -1e30).astype(BF16)
    extra = kk.shape[0] - length
    kk[pl.ds(length, extra), :] = jnp.zeros((extra, width), BF16)
    v[pl.ds(length, extra), :] = jnp.zeros((extra, width), BF16)

    point()
    run(10 * FIRST + 4)
    for i in range(2):
        turned = jnp.transpose(flat[FIRST][:, pl.ds(512 + 128 * i, 128)].astype(F32))
        gain[i : i + 1, :] = turned[0:1, :]

    def scale_one(rows):
        xn[rows, :] = (x[rows, :].astype(F32) * norms[rows, 0:1] * gain[0:1, :]).astype(BF16)

    tiles(length, scale_one)

    for i, g in enumerate(ATT):
        point()
        if i == 0:
            gu[:, pl.ds(0, 512)] = dot(xn[...], flat[FIRST][:, pl.ds(0, 512)])
            point()
            run(10 * g + 4)
            gu[:, pl.ds(512, 256)] = dot(xn[...], flat[g][...])
        else:
            run(10 * g + 4)
            gu[:, pl.ds(0, width)] = dot(xn[...], flat[g][...])

        def turn(rows):
            c, s = r.cos[rows, :], r.sin[rows, :]
            for j in range(2):
                cols = pl.ds(256 * i + 128 * j, 128)
                part = gu[rows, pl.ds(128 * j, 128)]
                part = part * c + swap_halves(part) * s
                q[rows, cols] = (part.astype(BF16).astype(F32) * HEAD**-0.5).astype(BF16)
                part = gu[rows, pl.ds(256 + 128 * j, 128)]
                kk[rows, cols] = (part * c + swap_halves(part) * s).astype(BF16)
                v[rows, cols] = gu[rows, pl.ds(512 + 128 * j, 128)].astype(BF16)

        tiles(length, turn)
        pairs(lambda j: attend_forward(2 * i + j, blocks, r))

    point()
    run(10 * OUT + 4)
    h1[...] = dot(r.attn[...], flat[OUT][...])

    def norm_two(rows):
        h = h1[rows, :] + x[rows, :].astype(F32)
        h1[rows, :] = h
        s = lax.rsqrt(jnp.mean(h * h, axis=1, keepdims=True) + EPSILON)
        norms[rows, 1:2] = s
        hn[rows, :] = (h * s * gain[1:2, :]).astype(BF16)

    tiles(length, norm_two)

    loads[-1].wait()
    chunk = full[FFN[0]].shape[-1] // 2
    for j, g in enumerate(FFN):
        point()
        run(10 * g + 4)
        run(10 * (DOWN + j) + 4)
        down = flat[DOWN].at[pl.ds(chunk * j, chunk)]
        gu[...] = dot(hn[...], flat[g][...])
        dh[...] = dot(gy[...], down[...], NT)

        def gated(rows):
            gate, up, d = gu[rows, pl.ds(0, chunk)], gu[rows, pl.ds(chunk, chunk)], dh[rows, :]
            sig = 0.5 * jnp.tanh(0.5 * gate) + 0.5
            act = gate * sig
            t1[rows, pl.ds(0, chunk)] = (act * up).astype(BF16)
            t2[rows, pl.ds(0, chunk)] = (d * up * (sig * (1.0 + gate * (1.0 - sig)))).astype(BF16)
            t2[rows, pl.ds(chunk, chunk)] = (d * act).astype(BF16)

        point()
        tiles(length, gated)
        point()
        if j == 0:
            acc1[...] = dot(t1[:, pl.ds(0, chunk)], down[...])
            acc2[...] = dot(t2[...], flat[g][...], NT)
        else:
            acc1[...] += dot(t1[:, pl.ds(0, chunk)], down[...])
            acc2[...] += dot(t2[...], flat[g][...], NT)
        point()
        flat[g][...] = dot(hn[...], t2[...], TN).astype(BF16)
        run(1000 + 10 * g)
        point()
        down[...] = dot(t1[:, pl.ds(0, chunk)], gy[...], TN).astype(BF16)
    run(1000 + 10 * DOWN)

    def between(rows):
        h, s = h1[rows, :], norms[rows, 1:2]
        t1[rows, :] = (h + acc1[rows, :]).astype(BF16)
        n = h * s
        scaled = acc2[rows, :] * gain[1:2, :]
        d = gy[rows, :].astype(F32) + s * (scaled - n * jnp.mean(scaled * n, axis=1, keepdims=True))
        acc1[rows, :] = d
        hn[rows, :] = d.astype(BF16)

    point()
    tiles(length, between)
    out_copy = pltpu.make_async_copy(t1, r.out, r.local.at[0])
    out_copy.start()
    point()
    out_copy.wait()
    t1[...] = dot(hn[...], flat[OUT][...], NT).astype(BF16)
    point()
    flat[OUT][...] = dot(r.attn[...], hn[...], TN).astype(BF16)
    run(1000 + 10 * OUT)

    def joined(i):
        cols = pl.ds(256 * i, 256)
        return jnp.concatenate([a[pl.ds(0, length), cols] for a in (q, kk, v)], axis=1)

    for i, g in enumerate(ATT):
        pairs(lambda j: attend_backward(2 * i + j, blocks, length, r))
        point()
        place_of = flat[FFN[i]]
        run(1000 + 10 * FFN[i] + 1)
        if g in SUMMED:
            place_of[:, pl.ds(0, width)] = dot(xn[...], joined(i), TN).astype(BF16)
            run(1000 + 10 * g)
        else:
            for n, a in enumerate((q, kk, v)):
                part = a[pl.ds(0, length), pl.ds(256 * i, 256)]
                place_of[:, pl.ds(256 * n, 256)] = dot(xn[...], part, TN).astype(BF16)
                run(1000 + 10 * LAST[n])
                if n < 2:
                    point()
    for i, g in enumerate(ATT):
        point()
        if i == 0:
            both = joined(i)
            acc2[...] = dot(both[:, :512], flat[FIRST][:, pl.ds(0, 512)], NT) + dot(
                both[:, 512:], flat[g][...], NT
            )
        else:
            acc2[...] += dot(joined(i), flat[g][...], NT)

    def last(rows):
        s = norms[rows, 0:1]
        n = x[rows, :].astype(F32) * s
        scaled = acc2[rows, :] * gain[0:1, :]
        d = acc1[rows, :] + s * (scaled - n * jnp.mean(scaled * n, axis=1, keepdims=True))
        t1[rows, :] = d.astype(BF16)

    point()
    tiles(length, last)
    in_copy = pltpu.make_async_copy(t1, r.in_grad, r.local.at[0])
    in_copy.start()
    point()
    for step in range(6):
        for g in FFN + (DOWN, OUT) + ATT[:-1] + LAST:
            run(1000 + 10 * g + step)
    for copy in swapped:
        copy.wait_send()
    in_copy.wait()


SCHEDULE = (
    (),
    (10, 0, 20, 30, 90, 11,),
    (),
    (1, 12, 40, 50, 21, 60, 100, 2,),
    (13, 22, 3, 31, 4, 14, 91,),
    (41,),
    (32,),
    (70, 23, 51,),
    (92, 42,),
    (110, 33, 80, 24,),
    (52, 93,),
    (34,),
    (101, 61,),
    (94, 71,),
    (43, 120, 53, 102,),
    (62, 44,),
    (111, 54,),
    (),
    (103, 72,),
    (63,),
    (81, 112, 1050,),
    (121, 64, 104,),
    (73,),
    (82,),
    (113,),
    (122, 1051, 114,),
    (1060, 74,),
    (),
    (83, 1061, 123,),
    (),
    (1052, 124, 1070, 84,),
    (),
    (1071,),
    (),
    (1062,),
    (1080,),
    (1090, 1072, 1081, 1053,),
    (),
    (1063, 1091,),
    (),
    (),
    (1040,),
    (1010, 1073, 1082,),
    (1092, 1011, 1083,),
    (),
    (1020, 1041, 1093,),
    (1012, 1021,),
    (),
    (1074, 1100,),
    (1042, 1084, 1013,),
    (1120, 1110, 1085, 1101, 1064, 1075, 1022, 1121, 1054, 1111, 1043,),
    (1094,),
    (1023, 1102, 1122, 1112, 1103,),
    (1123, 1014, 1113, 1065, 1055,),
    (1024, 1044, 1104, 1015, 1124, 1114, 1105, 1095, 1125, 1045, 1025, 1115,),
)


def layer(fold, ins):
    length, width = ins["x"].shape
    hidden = ins["wg"].shape[1]
    rows, drows = ins["wq"].shape[0], ins["wd"].shape[0]
    padded = (length + 127) // 128 * 128
    blocks = ((0, 256, 0, 256), (256, 592, 0, 640), (592, length, 512, padded))
    wide = hidden // 4 * 2
    names = dict(g_q="wq", g_k="wk", g_v="wv", g_o="wo", g_g="wg", g_u="wu", g_d="wd")
    big = jax.ShapeDtypeStruct((length, width), BF16)
    outs = dict(out=big, in_grad=big)
    outs.update({n: jax.ShapeDtypeStruct(ins[w].shape, F32) for n, w in names.items()})
    sizes = [(rows, width), (rows, 256)] + 3 * [(rows, width)] + 4 * [(rows, wide)]
    sizes.append((drows, width))
    vmem = pltpu.VMEM
    lead = ((4, 2, 2), (4, 2), (4,), (3,))
    low, wider = vmem((length, width), BF16), vmem((padded, width), BF16)
    lane, high = vmem((length, 128), F32), vmem((length, width), F32)
    sems = 2 * [pltpu.SemaphoreType.DMA((len(sizes) + 3, 4))]
    sems += 2 * [pltpu.SemaphoreType.DMA((len(SUMMED), 5))]
    weights = ("wq", "wk", "wv", "wo", "wg", "wu", "wd")
    scratch = dict(
        full=[vmem((4, 2, 2, 2 * m, c), BF16) for m, c in sizes],
        bufs=[
            [vmem(d + (2 * m, c // 2), BF16) for d in lead] + 2 * [vmem((m, c // 2), F32)]
            for m, c in [(rows, width)] + [sizes[i] for i in SUMMED[1:-3]] + 3 * [(rows, 256)]
        ],
        gains=vmem((rows, 256), BF16),
        other=[vmem((rows, 256), BF16)] + [vmem(ins[n].shape, BF16) for n in weights],
        sems=sems,
        swap=2 * [pltpu.SemaphoreType.DMA((8,))],
        local=pltpu.SemaphoreType.DMA((10,)),
        near=[vmem(ins[n].shape, BF16) for n in weights],
        x_near=low,
        gy_near=low,
        xn=low,
        q=low,
        attn=low,
        hn=low,
        t1=low,
        k=wider,
        v=wider,
        t2=vmem((length, wide), BF16),
        h1=high,
        acc1=high,
        acc2=high,
        gu=vmem((length, wide), F32),
        dh=vmem((length, wide // 2), F32),
        bias=vmem((length, 640), BF16),
        cos=lane,
        sin=lane,
        lse=lane,
        norms=vmem((length, 2), F32),
        gain=vmem((8, width), F32),
    )
    leaves, tree = jax.tree.flatten(scratch)
    given = list(ins) + list(outs)

    def body(*refs):
        named = dict(zip(given, refs), **jax.tree.unflatten(tree, refs[len(given) :]))
        layer_kernel(fold, blocks, SimpleNamespace(**named))

    near, anywhere = pl.BlockSpec(memory_space=vmem), pl.BlockSpec(memory_space=pl.ANY)
    return pl.pallas_call(
        body,
        out_shape=list(outs.values()),
        in_specs=[anywhere if n in weights + ("x", "gy") else near for n in ins],
        out_specs=[anywhere] * 2 + [near] * (len(outs) - 2),
        scratch_shapes=leaves,
        compiler_params=pltpu.CompilerParams(
            collective_id=0, has_side_effects=True, vmem_limit_bytes=62 * 2**20
        ),
    )(*ins.values())


def finish_kernel(count, *refs):
    raw, weights, gains = refs[:count], refs[count : count + 5], refs[count + 5 : count + 7]
    outs, sums = refs[count + 7 : 2 * count + 7], refs[2 * count + 7 : 2 * count + 9]
    held, sems = refs[2 * count + 9 : -1], refs[-1]
    given = raw + weights
    loads = [pltpu.make_async_copy(a, h, sems.at[i]) for i, (a, h) in enumerate(zip(given, held))]
    stores = [
        pltpu.make_async_copy(h, o, sems.at[len(given) + i])
        for i, (h, o) in enumerate(zip(held, outs))
    ]
    for copy in loads:
        copy.start()
    for i, copy in enumerate(loads):
        copy.wait()
        if i < count:
            stores[i].start()
    for gain, out, which in zip(gains, sums, (((0, 2), (1, 3), (2, 4)), ((3, 6), (4, 7)))):
        n = gain.shape[1]
        column = sum(
            jnp.sum(held[count + w][...].astype(F32) * held[g][...], axis=1, keepdims=True)
            for w, g in which
        )
        same = lax.broadcasted_iota(jnp.int32, (n, n), 0) == lax.broadcasted_iota(jnp.int32, (n, n), 1)
        row = jnp.sum(jnp.where(same, column, 0.0), axis=0, keepdims=True)
        out[...] = row / gain[...].astype(F32)
    for copy in stores:
        copy.wait()


def finish_all(raw, weights, gains):
    near, anywhere = pl.BlockSpec(memory_space=pltpu.VMEM), pl.BlockSpec(memory_space=pl.ANY)
    held = list(raw) + list(weights)
    return pl.pallas_call(
        lambda *refs: finish_kernel(len(raw), *refs),
        out_shape=[jax.ShapeDtypeStruct(a.shape, a.dtype) for a in raw]
        + [jax.ShapeDtypeStruct(g.shape, F32) for g in gains],
        in_specs=[anywhere] * len(held) + [near] * 2,
        out_specs=[anywhere] * len(raw) + [near] * 2,
        scratch_shapes=[pltpu.VMEM(a.shape, a.dtype) for a in held]
        + [pltpu.SemaphoreType.DMA((len(held) + len(raw),))],
        compiler_params=pltpu.CompilerParams(vmem_limit_bytes=62 * 2**20),
    )(*raw, *weights, *gains)


def per_device(
    fold,
    block_input,
    seg_ids,
    gain_attn,
    w_query,
    w_key,
    w_value,
    w_out,
    gain_ffn,
    w_gate,
    w_up,
    w_down,
    cotangent,
):
    row_count, length, width = block_input.shape
    groups = [[c * fold + j for j in range(fold)] for c in range(CELLS)]
    gains = (gain_attn[None], gain_ffn[None])
    blocks = [w_query, w_key, w_value, w_out, w_gate, w_up, w_down]
    if fold > 1:
        blocks = [
            lax.all_gather(w, AXIS, axis=0, tiled=True, axis_index_groups=groups) for w in blocks
        ]
        gains = tuple(
            lax.all_gather(g, AXIS, axis=1, tiled=True, axis_index_groups=groups) for g in gains
        )
    exponent = (np.arange(HEAD // 2, dtype=np.float32) * np.float32(2.0)) / np.float32(HEAD)
    freq = jnp.asarray(np.tile(np.float32(10000.0) ** -exponent, 4)[None].astype(np.float32))
    wq, wk, wv, wo, wg, wu, wd = blocks
    output, input_grad, *parts = layer(
        fold,
        dict(
            x=block_input.reshape(row_count * length, width),
            seg=seg_ids,
            ga=gains[0],
            gf=gains[1],
            freq=freq,
            wq=wq,
            wk=wk,
            wv=wv,
            wo=wo,
            wg=wg,
            wu=wu,
            wd=wd,
            gy=cotangent.reshape(row_count * length, width),
        ),
    )
    if fold > 1:
        parts = [
            lax.psum_scatter(g, AXIS, scatter_dimension=0, tiled=True, axis_index_groups=groups)
            for g in parts
        ]
    output, input_grad, dq, dk, dv, do, dg, du, dd, gain_one, gain_two = finish_all(
        [output, input_grad] + parts,
        (w_query, w_key, w_value, w_gate, w_up),
        (gain_attn[None], gain_ffn[None]),
    )
    output, input_grad = (a.reshape(block_input.shape) for a in (output, input_grad))
    return (output, input_grad, gain_one[0], dq, dk, dv, do, gain_two[0], dg, du, dd)


def solution(mesh):
    fold = mesh.shape[AXIS] // CELLS
    rows, flat = P(AXIS, None), P(AXIS)
    cube = P(AXIS, None, None)

    def run(*args):
        return per_device(fold, *args)

    return jax.shard_map(
        run,
        mesh=mesh,
        in_specs=(cube, rows, flat, rows, rows, rows, rows, flat, rows, rows, rows, cube),
        out_specs=(cube, cube, flat, rows, rows, rows, rows, flat, rows, rows, rows),
        check_vma=False,
    )
```

```python
from types import SimpleNamespace

import jax
import jax.numpy as jnp
import numpy as np
from jax import lax
from jax.experimental import pallas as pl
from jax.experimental.pallas import tpu as pltpu
from jax.sharding import PartitionSpec as P

AXIS = "fsdp"
HEAD = 64
EPSILON = 1e-05
CELLS = 32
MESH = pl.DeviceIdType.MESH
F32 = jnp.float32
BF16 = jnp.bfloat16
NN = (((1,), (0,)), ((), ()))
NT = (((1,), (1,)), ((), ()))
TN = (((0,), (0,)), ((), ()))
TILE = 112
FIRST, ATT, OUT, FFN, DOWN = 0, (1, 2, 3), 4, (5, 6, 7, 8), 9
LAST = (10, 11, 12)
SUMMED = (1, 2, 4, 5, 6, 7, 8, 9) + LAST
X, Y, CORE = 4, 5, 6


def dot(a, b, dims=NN):
    return lax.dot_general(a, b, dims, preferred_element_type=F32)


def tiles(length, body):
    def step(i, carry):
        body(pl.ds(pl.multiple_of(i * TILE, TILE), TILE))
        return carry

    lax.fori_loop(0, length // TILE, step, 0)


def place(fold):
    me = lax.axis_index(AXIS)
    cell = me // fold
    k = cell % 2
    x = (cell // 2) % 2
    y = (cell // 4) % 2
    z = cell // 8
    ids = {
        CORE: me + (1 - 2 * k) * fold,
        X: me + (1 - 2 * x) * (2 * fold),
        Y: me + (1 - 2 * y) * (4 * fold),
    }
    for r in (1, 2, 3):
        ids[r] = me + ((z + r) % 4 - z) * (8 * fold)
    return z, y, x, k, ids


def greet(ids):
    barrier = pltpu.get_barrier_semaphore()
    for peer in ids.values():
        pl.semaphore_signal(barrier, inc=1, device_id=(peer,), device_id_type=MESH)
    pl.semaphore_wait(barrier, len(ids))


def remote(src, dst, send, recv, peer):
    return pltpu.make_async_remote_copy(
        src_ref=src,
        dst_ref=dst,
        send_sem=send,
        recv_sem=recv,
        device_id=(peer,),
        device_id_type=MESH,
    )


class Exchange:
    def copy(self, slot):
        src, dst, peer = self.route(slot)
        n = self.lanes[slot]
        return remote(src, dst, self.send.at[n], self.recv.at[n], self.where[4][peer])

    def start(self, *slots):
        for slot in slots:
            self.copy(slot).start()

    def pair(self, ref, lane):
        return remote(ref, ref, self.send.at[lane], self.recv.at[lane], self.where[4][CORE])

    def arrive(self, lane):
        self.pair(self.whole(lane), lane).wait_recv()

    def settle(self, *lanes):
        for lane in lanes:
            self.pair(self.whole(lane), lane).wait_send()


class Gather(Exchange):
    lanes = (0, 0, 0, 1, 1, 2, 2, 3)

    def __init__(self, where, full, send, recv, own):
        self.where, self.full, self.send, self.recv, self.own = where, full, send, recv, own

    def route(self, slot):
        z, y, x, k, ids = self.where
        half = self.full.shape[-1] // 2
        mine = pl.ds(pl.multiple_of(k * half, 128), half)
        low, high = pl.ds(0, 2), pl.ds(2, 2)
        index, peer = (
            ((z, y, x), 1),
            ((z, y, x), 2),
            ((z, y, x), 3),
            ((low, y, x), Y),
            ((high, y, x), X),
            ((low, slice(None), x), X),
            ((high, y), Y),
            ((), CORE),
        )[slot]
        index = index + (slice(None),) * (4 - len(index)) + (mine,)
        part = self.full.at[index]
        return part, part, peer

    def whole(self, lane):
        z, y, x, k, ids = self.where
        half = self.full.shape[-1] // 2
        every = slice(None)
        index = ((pl.ds(0, 3), y, x), (every, y, x), (every, every, x), (every, every, every))[lane]
        return self.full.at[index + (every, pl.ds(0, half))]

    def step(self, n):
        if n > 0:
            self.arrive(n - 1)
        if n == 0:
            self.own()
            self.start(1, 0, 2)
        elif n == 1:
            self.start(3, 4)
        elif n == 2:
            self.start(5, 6)
        elif n == 3:
            self.start(7)
        elif n == 4:
            self.settle(*range(4))


class LateGather(Exchange):
    lanes = (2, 2, 2, 0, 1, 0, 1, 3)

    def __init__(self, where, full, send, recv, own):
        self.where, self.full, self.send, self.recv, self.own = where, full, send, recv, own

    def route(self, slot):
        z, y, x, k, ids = self.where
        half, every = self.full.shape[-1] // 2, slice(None)
        mine = pl.ds(pl.multiple_of(k * half, 128), half)
        index, peer = (
            ((z, every, every), 1),
            ((z, every, every), 2),
            ((z, every, every), 3),
            ((z, y, x), X),
            ((z, y, every), Y),
            ((z, y, x), Y),
            ((z, every, x), X),
            ((every, every, every), CORE),
        )[slot]
        part = self.full.at[index + (every, mine)]
        return part, part, peer

    def whole(self, lane):
        z, y, x, k, ids = self.where
        half, every = self.full.shape[-1] // 2, slice(None)
        index = ((z, y, x), (z, y, every), (pl.ds(0, 3), every, every), (every, every, every))[lane]
        return self.full.at[index + (every, pl.ds(0, half))]

    def either(self, first, second):
        k = self.where[3]

        @pl.when(k == 0)
        def _():
            self.start(first)

        @pl.when(k == 1)
        def _():
            self.start(second)

    def step(self, n):
        if n > 0:
            self.arrive(n - 1)
        if n == 0:
            self.own()
            self.either(3, 5)
        elif n == 1:
            self.either(4, 6)
        elif n == 2:
            self.start(1, 0, 2)
        elif n == 3:
            self.start(7)
        elif n == 4:
            self.settle(*range(4))


class PlaneGather(Exchange):
    lanes = Gather.lanes

    def __init__(self, where, j, full, send, recv, own):
        self.where, self.j, self.full, self.send, self.recv = where, j, full, send, recv
        self.own = own

    def route(self, slot):
        z, y, x, k, ids = self.where
        half, rows = self.full.shape[-1] // 2, self.full.shape[-2]
        mine = pl.ds(pl.multiple_of(k * half, 128), half)
        low, high, every = pl.ds(0, rows // 2), pl.ds(rows // 2, rows // 2), slice(None)
        index, peer = (
            ((y, x, every), 1),
            ((y, x, every), 2),
            ((y, x, every), 3),
            ((y, x, low), Y),
            ((y, x, high), X),
            ((every, x, low), X),
            ((y, every, high), Y),
            ((every, every, every), CORE),
        )[slot]
        part = self.full.at[(self.j,) + index + (mine,)]
        return part, part, peer

    def whole(self, lane):
        z, y, x, k, ids = self.where
        half, every = self.full.shape[-1] // 2, slice(None)
        index = ((y, x), (y, x), (every, x), (every, every))[lane]
        return self.full.at[(self.j,) + index + (every, pl.ds(0, half))]

    def step(self, n):
        z, y, x, k, ids = self.where
        here = z == self.j
        if n == 0:

            @pl.when(here)
            def _():
                self.own()
                self.start(1, 0, 2)

        elif n == 1:

            @pl.when(jnp.logical_not(here))
            def _():
                self.arrive(0)

            self.start(3, 4)
        elif n == 2:
            self.arrive(1)
            self.start(5, 6)
        elif n == 3:
            self.arrive(2)
            self.start(7)
        elif n == 4:
            self.arrive(3)
            self.settle(1, 2, 3)

            @pl.when(here)
            def _():
                half = self.full.shape[-1] // 2
                three = self.full.at[pl.ds(0, 3), y, x, :, pl.ds(0, half)]
                self.pair(three, 0).wait_send()


class Scatter(Exchange):
    lanes = (0, 1, 1, 2, 2, 3, 3, 3, 4)

    def __init__(self, where, full, base, bufs, send, recv, finish):
        self.where, self.full, self.base = where, full, base
        self.send, self.recv = send, recv
        self.r0, self.r1, self.r2, self.r3, self.give, self.r4 = bufs
        self.finish = finish

    def columns(self, k):
        half = self.r0.shape[-1]
        return pl.ds(pl.multiple_of(self.base + k * half, 128), half)

    def route(self, slot):
        z, y, x, k, ids = self.where
        low, high = pl.ds(0, 2), pl.ds(2, 2)
        if slot == 0:
            return self.full.at[:, :, :, :, self.columns(1 - k)], self.r0, CORE
        if slot == 1:
            return self.r0.at[low, :, 1 - x], self.r1.at[low], X
        if slot == 2:
            return self.r0.at[high, 1 - y], self.r1.at[high], Y
        if slot == 3:
            return self.r1.at[low, 1 - y], self.r2.at[low], Y
        if slot == 4:
            return self.r1.at[high, 1 - x], self.r2.at[high], X
        if slot == 8:
            return self.give, self.r4, CORE
        r = slot - 4
        return self.r2.at[(z + r) % 4], self.r3.at[r - 1], r

    def whole(self, lane):
        return (self.r0, self.r1, self.r2, self.r3, self.r4)[lane]

    def total(self):
        total = self.r2[self.where[0]].astype(F32)
        for r in range(3):
            total = total + self.r3[r].astype(F32)
        n = total.shape[0] // 2
        return total[:n], total[n:]

    def step(self, n):
        z, y, x, k, ids = self.where
        r0, r1, r2, full = self.r0, self.r1, self.r2, self.full
        if n == 0:
            self.start(0)
        elif n == 1:
            self.arrive(0)
            mine = self.columns(k)

            def add(i, carry):
                p, q, r = i // 4, (i // 2) % 2, i % 2
                r0[p, q, r] = r0[p, q, r] + full[p, q, r, :, mine]
                return carry

            lax.fori_loop(0, 16, add, 0)
            self.start(1, 2)
            self.settle(0)
        elif n == 2:
            self.arrive(1)

            def add(i, carry):
                p, q = i // 2, i % 2
                r1[p, q] = r1[p, q] + r0[p, q, x]
                r1[p + 2, q] = r1[p + 2, q] + r0[p + 2, y, q]
                return carry

            lax.fori_loop(0, 4, add, 0)
            self.start(3, 4)
        elif n == 3:
            self.arrive(2)
            for p in range(2):
                r2[p] = r2[p] + r1[p, y]
                r2[p + 2] = r2[p + 2] + r1[p + 2, x]
            self.start(6, 5, 7)
        elif n == 4:
            self.arrive(3)
            first, second = self.total()
            self.give[...] = jnp.where(k == 0, second, first)
            self.start(8)
        elif n == 5:
            self.arrive(4)
            first, second = self.total()
            own, other = jnp.where(k == 0, first, second), self.r4[...]
            self.finish(
                jnp.concatenate(
                    [jnp.where(k == 0, own, other), jnp.where(k == 0, other, own)], axis=1
                )
            )
            self.settle(*range(1, 5))


def regroup(v):
    lane = lax.broadcasted_iota(jnp.int32, (1, 128), 1)
    parts = []
    for i in range(v.shape[1] // 128):
        t = v[:, 128 * i : 128 * i + 128]
        down, up = pltpu.roll(t, 96, 1), pltpu.roll(t, 32, 1)
        middle = jnp.where(lane < HEAD, down, up)
        parts.append(jnp.where((lane >= HEAD // 2) & (lane < 3 * HEAD // 2), middle, t))
    return jnp.concatenate(parts, axis=1)


def swap_halves(v):
    return pltpu.roll(v, HEAD, 1)


def heads():
    lane = lax.broadcasted_iota(jnp.int32, (1, 128), 1)
    return lane < HEAD, lane % HEAD < HEAD // 2


def both_heads(a, first):
    zero = jnp.zeros_like(a)
    return jnp.concatenate([jnp.where(first, a, zero), jnp.where(first, zero, a)], axis=0)


def attend_forward(p, blocks, r):
    q, k, v, bias, lse = r.q, r.k, r.v, r.bias, r.lse
    cols = pl.ds(pl.multiple_of(p * 128, 128), 128)
    lane = lax.broadcasted_iota(jnp.int32, (1, 128), 1)
    first, even = heads()
    for r0, r1, c0, c1 in blocks:
        rows, keys = pl.ds(r0, r1 - r0), pl.ds(c0, c1 - c0)
        q2, k2, v2 = q[rows, cols], k[keys, cols], v[keys, cols]
        mask = bias[rows, pl.ds(0, c1 - c0)].astype(F32)
        weights, logs, scale = [], [], []
        for mine in (even, ~even):
            s = dot(jnp.where(mine, q2, jnp.zeros_like(q2)), k2, NT) + mask
            top = jnp.max(s, axis=1, keepdims=True)
            e = jnp.exp(s - top)
            total = jnp.sum(e, axis=1, keepdims=True)
            weights.append(e.astype(BF16))
            scale.append(1.0 / total)
            logs.append(top + jnp.log(total))
        mix = dot(jnp.concatenate(weights, axis=1), both_heads(v2, first))
        r.attn[rows, cols] = (mix * jnp.where(first, scale[0], scale[1])).astype(BF16)
        kept = jnp.where(lane == 2 * p, logs[0], lse[rows, :])
        lse[rows, :] = jnp.where(lane == 2 * p + 1, logs[1], kept)


def attend_backward(p, blocks, length, r):
    q, k, v, bias, cos, sin, sums = r.q, r.k, r.v, r.bias, r.cos, r.sin, r.gu
    cols = pl.ds(pl.multiple_of(p * 128, 128), 128)
    lane = lax.broadcasted_iota(jnp.int32, (1, 128), 1)
    first, even = heads()

    def clear(rows):
        sums[rows, pl.ds(0, 256)] = jnp.zeros((TILE, 256), F32)

    tiles(length, clear)
    for r0, r1, c0, c1 in blocks:
        rows, keys = pl.ds(r0, r1 - r0), pl.ds(c0, c1 - c0)
        q2, k2, v2, d2 = q[rows, cols], k[keys, cols], v[keys, cols], r.t1[rows, cols]
        both = r.attn[rows, cols].astype(F32) * d2.astype(F32)
        stat = r.lse[rows, :]
        mask = bias[rows, pl.ds(0, c1 - c0)].astype(F32)
        probs, grads = [], []
        for h, (mine, part) in enumerate(((first, even), (~first, ~even))):
            delta = jnp.sum(jnp.where(mine, both, 0.0), axis=1, keepdims=True)
            log = jnp.sum(jnp.where(lane == 2 * p + h, stat, 0.0), axis=1, keepdims=True)
            s = dot(jnp.where(part, q2, jnp.zeros_like(q2)), k2, NT) + mask
            prob = jnp.exp(s - log)
            dp = dot(jnp.where(mine, d2, jnp.zeros_like(d2)), v2, NT)
            grads.append((prob * (dp - delta)).astype(BF16))
            probs.append(prob.astype(BF16))
        dv = dot(jnp.concatenate(probs, axis=0), both_heads(d2, first), TN)
        dk = dot(jnp.concatenate(grads, axis=0), both_heads(q2, even), TN)
        dq = dot(jnp.concatenate(grads, axis=1), both_heads(k2, even)) * (HEAD**-0.5)
        dq = dq * cos[rows, :] - swap_halves(dq) * sin[rows, :]
        q[rows, cols] = dq.astype(BF16)
        n = min(c1, length) - c0
        sums[pl.ds(c0, n), pl.ds(0, 128)] += dk[:n]
        sums[pl.ds(c0, n), pl.ds(128, 128)] += dv[:n]

    def store(rows):
        dk = sums[rows, pl.ds(0, 128)]
        dk = dk * cos[rows, :] - swap_halves(dk) * sin[rows, :]
        k[rows, cols] = dk.astype(BF16)
        v[rows, cols] = sums[rows, pl.ds(128, 128)].astype(BF16)

    tiles(length, store)


def layer_kernel(fold, blocks, r):
    x, gy, gain, norms = r.x_near, r.gy_near, r.gain, r.norms
    far = (r.wq, r.wk, r.wv, r.wo, r.wg, r.wu, r.wd)
    loads = [
        pltpu.make_async_copy(a, b, r.local.at[1 + i])
        for i, (a, b) in enumerate(zip(far + (r.x, r.gy), r.near + [x, gy]))
    ]
    for copy in loads:
        copy.start()
    xn, hn, q, kk, v, bias, lse = r.xn, r.hn, r.q, r.k, r.v, r.bias, r.lse
    h1, acc1, acc2, gu, dh, t1, t2 = r.h1, r.acc1, r.acc2, r.gu, r.dh, r.t1, r.t2
    length, width = x.shape
    where = place(fold)
    z, y, xx, k, ids = where
    full = r.full
    flat = [f.reshape(-1, f.shape[-1]) for f in full]

    def finish(i):
        def put(total):
            if i in ATT:
                cols = pl.ds(256 * (i - ATT[0]), 256)
                r.g_q[:, cols] = regroup(total[:, 0:256])
                r.g_k[:, cols] = regroup(total[:, 256:512])
                r.g_v[:, cols] = total[:, 512:768]
            elif i in FFN:
                n = total.shape[1] // 2
                cols = pl.ds(n * (i - FFN[0]), n)
                r.g_g[:, cols] = total[:, :n]
                r.g_u[:, cols] = total[:, n:]
            else:
                (r.g_o if i == OUT else r.g_d)[...] = total

        return put

    def rest(n):
        def put(total):
            cols = pl.ds(256 * (len(ATT) - 1), 256)
            (r.g_q, r.g_k, r.g_v)[n][:, cols] = regroup(total) if n < 2 else total

        return put

    spots = {i: (full[FFN[i - ATT[0]] if i in ATT else i], 0, finish(i)) for i in SUMMED[:-3]}
    spots.update({LAST[n]: (full[FFN[len(ATT) - 1]], 256 * n, rest(n)) for n in range(3)})
    scatter = {
        i: Scatter(where, f, base, b, r.sems[2].at[n], r.sems[3].at[n], put)
        for n, ((i, (f, base, put)), b) in enumerate(zip(spots.items(), r.bufs))
    }

    for i, g in enumerate((r.ga, r.gf)):
        n = g.shape[1]
        same = lax.broadcasted_iota(jnp.int32, (n, n), 0) == lax.broadcasted_iota(jnp.int32, (n, n), 1)
        column = jnp.sum(jnp.where(same, g[...].astype(F32), 0.0), axis=1, keepdims=True)
        r.gains[:, pl.ds(128 * i, 128)] = jnp.broadcast_to(column, (n, 128)).astype(BF16)
    inputs = [r.gains] + r.near
    swapped = [
        remote(w, o, r.swap[0].at[i], r.swap[1].at[i], ids[CORE])
        for i, (w, o) in enumerate(zip((r.gains,) + far, r.other))
    ]

    def own(g):
        n = full[g].shape[-1] // 2
        if g == FIRST:
            c = pl.ds(0, 256)
            parts = [(1, c, regroup), (2, c, regroup), (0, c, None)]
        elif g == ATT[0]:
            parts = [(3, pl.ds(0, 256), None)]
        elif g in ATT:
            c = pl.ds(256 * (g - ATT[0]), 256)
            parts = [(1, c, regroup), (2, c, regroup), (3, c, None)]
        elif g in FFN:
            c = pl.ds(n * (g - FFN[0]), n)
            parts = [(5, c, None), (6, c, None)]
        else:
            parts = [({OUT: 4, DOWN: 7}[g], slice(None), None)]

        def row(refs):
            values = [(refs[w][:, c].astype(F32), f) for w, c, f in parts]
            return jnp.concatenate([f(t) if f else t for t, f in values], axis=1)

        a, b = row(inputs), row(r.other)
        a, b = (jnp.where(k == 0, t[:, :n], t[:, n:]) for t in (a, b))
        both = jnp.concatenate([jnp.where(k == 0, a, b), jnp.where(k == 0, b, a)], axis=0)
        cols = pl.ds(pl.multiple_of(k * n, 128), n)
        full[g][z, y, xx, :, cols] = both.astype(BF16)

    gather = [
        (LateGather if i == FFN[-1] else Gather)(
            where, full[i], r.sems[0].at[i], r.sems[1].at[i], lambda i=i: own(i)
        )
        for i in range(DOWN)
    ] + [
        PlaneGather(
            where, j, full[DOWN], r.sems[0].at[DOWN + j], r.sems[1].at[DOWN + j], lambda: own(DOWN)
        )
        for j in range(4)
    ]
    state = {}
    points = iter(SCHEDULE)

    def run(event):
        kind, g, step = event // 1000, event // 10 % 100, event % 10
        while state.get((kind, g), 0) <= step:
            n = state.get((kind, g), 0)
            (scatter if kind else gather)[g].step(n)
            state[kind, g] = n + 1

    def point():
        for event in next(points):
            run(event)

    def pairs(body):
        point()

        def step(i, carry):
            @pl.when(i == 1)
            def _():
                point()

            body(i)
            return carry

        lax.fori_loop(0, 2, step, 0)

    point()
    greet(ids)
    for copy in swapped:
        copy.start()

    def norm_one(rows):
        xf = x[rows, :].astype(F32)
        norms[rows, 0:1] = lax.rsqrt(jnp.mean(xf * xf, axis=1, keepdims=True) + EPSILON)
        lse[rows, :] = jnp.zeros((TILE, 128), F32)

    loads[-2].wait()
    tiles(length, norm_one)
    for copy in loads[:-2]:
        copy.wait()
    for copy in swapped:
        copy.wait_recv()
    point()

    point()
    ends, count = [], jnp.zeros((1, 1), F32)
    for label in range(3):
        count = count + jnp.sum((r.seg[...] == label).astype(F32), axis=1, keepdims=True)
        ends.append(count)

    def tables(rows):
        i = lax.broadcasted_iota(jnp.int32, (TILE, 1), 0).astype(F32) + rows.start.astype(F32)
        first = jnp.zeros_like(i)
        for end in ends:
            first = jnp.where(i >= end, end, first)
        angle = (i - first) * r.freq[...]
        lane = lax.broadcasted_iota(jnp.int32, (1, 128), 1)
        r.cos[rows, :] = jnp.cos(angle)
        r.sin[rows, :] = jnp.where(lane < HEAD, -1.0, 1.0) * jnp.sin(angle)

    tiles(length, tables)

    def label_of(i):
        return sum((i >= end).astype(F32) for end in ends)

    point()
    for r0, r1, c0, c1 in blocks:
        i = (lax.broadcasted_iota(jnp.int32, (r1 - r0, 1), 0) + r0).astype(F32)
        j = (lax.broadcasted_iota(jnp.int32, (1, c1 - c0), 1) + c0).astype(F32)
        allowed = (label_of(i) == label_of(j)) & (j <= i)
        bias[pl.ds(r0, r1 - r0), pl.ds(0, c1 - c0)] = jnp.where(allowed, 0.0, -1e30).astype(BF16)
    extra = kk.shape[0] - length
    kk[pl.ds(length, extra), :] = jnp.zeros((extra, width), BF16)
    v[pl.ds(length, extra), :] = jnp.zeros((extra, width), BF16)

    point()
    run(10 * FIRST + 4)
    for i in range(2):
        turned = jnp.transpose(flat[FIRST][:, pl.ds(512 + 128 * i, 128)].astype(F32))
        gain[i : i + 1, :] = turned[0:1, :]

    def scale_one(rows):
        xn[rows, :] = (x[rows, :].astype(F32) * norms[rows, 0:1] * gain[0:1, :]).astype(BF16)

    tiles(length, scale_one)

    for i, g in enumerate(ATT):
        point()
        if i == 0:
            gu[:, pl.ds(0, 512)] = dot(xn[...], flat[FIRST][:, pl.ds(0, 512)])
            point()
            run(10 * g + 4)
            gu[:, pl.ds(512, 256)] = dot(xn[...], flat[g][...])
        else:
            run(10 * g + 4)
            gu[:, pl.ds(0, width)] = dot(xn[...], flat[g][...])

        def turn(rows):
            c, s = r.cos[rows, :], r.sin[rows, :]
            for j in range(2):
                cols = pl.ds(256 * i + 128 * j, 128)
                part = gu[rows, pl.ds(128 * j, 128)]
                part = part * c + swap_halves(part) * s
                q[rows, cols] = (part.astype(BF16).astype(F32) * HEAD**-0.5).astype(BF16)
                part = gu[rows, pl.ds(256 + 128 * j, 128)]
                kk[rows, cols] = (part * c + swap_halves(part) * s).astype(BF16)
                v[rows, cols] = gu[rows, pl.ds(512 + 128 * j, 128)].astype(BF16)

        tiles(length, turn)
        pairs(lambda j: attend_forward(2 * i + j, blocks, r))

    point()
    run(10 * OUT + 4)
    h1[...] = dot(r.attn[...], flat[OUT][...])

    def norm_two(rows):
        h = h1[rows, :] + x[rows, :].astype(F32)
        h1[rows, :] = h
        s = lax.rsqrt(jnp.mean(h * h, axis=1, keepdims=True) + EPSILON)
        norms[rows, 1:2] = s
        hn[rows, :] = (h * s * gain[1:2, :]).astype(BF16)

    tiles(length, norm_two)

    loads[-1].wait()
    chunk = full[FFN[0]].shape[-1] // 2
    for j, g in enumerate(FFN):
        point()
        run(10 * g + 4)
        run(10 * (DOWN + j) + 4)
        down = flat[DOWN].at[pl.ds(chunk * j, chunk)]
        gu[...] = dot(hn[...], flat[g][...])
        dh[...] = dot(gy[...], down[...], NT)

        def gated(rows):
            gate, up, d = gu[rows, pl.ds(0, chunk)], gu[rows, pl.ds(chunk, chunk)], dh[rows, :]
            sig = 0.5 * jnp.tanh(0.5 * gate) + 0.5
            act = gate * sig
            t1[rows, pl.ds(0, chunk)] = (act * up).astype(BF16)
            t2[rows, pl.ds(0, chunk)] = (d * up * (sig * (1.0 + gate * (1.0 - sig)))).astype(BF16)
            t2[rows, pl.ds(chunk, chunk)] = (d * act).astype(BF16)

        point()
        tiles(length, gated)
        point()
        if j == 0:
            acc1[...] = dot(t1[:, pl.ds(0, chunk)], down[...])
            acc2[...] = dot(t2[...], flat[g][...], NT)
        else:
            acc1[...] += dot(t1[:, pl.ds(0, chunk)], down[...])
            acc2[...] += dot(t2[...], flat[g][...], NT)
        point()
        flat[g][...] = dot(hn[...], t2[...], TN).astype(BF16)
        run(1000 + 10 * g)
        point()
        down[...] = dot(t1[:, pl.ds(0, chunk)], gy[...], TN).astype(BF16)
    run(1000 + 10 * DOWN)

    def between(rows):
        h, s = h1[rows, :], norms[rows, 1:2]
        t1[rows, :] = (h + acc1[rows, :]).astype(BF16)
        n = h * s
        scaled = acc2[rows, :] * gain[1:2, :]
        d = gy[rows, :].astype(F32) + s * (scaled - n * jnp.mean(scaled * n, axis=1, keepdims=True))
        acc1[rows, :] = d
        hn[rows, :] = d.astype(BF16)

    point()
    tiles(length, between)
    out_copy = pltpu.make_async_copy(t1, r.out, r.local.at[0])
    out_copy.start()
    point()
    out_copy.wait()
    t1[...] = dot(hn[...], flat[OUT][...], NT).astype(BF16)
    point()
    flat[OUT][...] = dot(r.attn[...], hn[...], TN).astype(BF16)
    run(1000 + 10 * OUT)

    def joined(i):
        cols = pl.ds(256 * i, 256)
        return jnp.concatenate([a[pl.ds(0, length), cols] for a in (q, kk, v)], axis=1)

    for i, g in enumerate(ATT):
        pairs(lambda j: attend_backward(2 * i + j, blocks, length, r))
        point()
        place_of = flat[FFN[i]]
        run(1000 + 10 * FFN[i] + 1)
        if g in SUMMED:
            place_of[:, pl.ds(0, width)] = dot(xn[...], joined(i), TN).astype(BF16)
            run(1000 + 10 * g)
        else:
            for n, a in enumerate((q, kk, v)):
                part = a[pl.ds(0, length), pl.ds(256 * i, 256)]
                place_of[:, pl.ds(256 * n, 256)] = dot(xn[...], part, TN).astype(BF16)
                run(1000 + 10 * LAST[n])
                if n < 2:
                    point()
    for i, g in enumerate(ATT):
        point()
        if i == 0:
            both = joined(i)
            acc2[...] = dot(both[:, :512], flat[FIRST][:, pl.ds(0, 512)], NT) + dot(
                both[:, 512:], flat[g][...], NT
            )
        else:
            acc2[...] += dot(joined(i), flat[g][...], NT)

    def last(rows):
        s = norms[rows, 0:1]
        n = x[rows, :].astype(F32) * s
        scaled = acc2[rows, :] * gain[0:1, :]
        d = acc1[rows, :] + s * (scaled - n * jnp.mean(scaled * n, axis=1, keepdims=True))
        t1[rows, :] = d.astype(BF16)

    point()
    tiles(length, last)
    in_copy = pltpu.make_async_copy(t1, r.in_grad, r.local.at[0])
    in_copy.start()
    point()
    for step in range(6):
        for g in FFN + (DOWN, OUT) + ATT[:-1] + LAST:
            run(1000 + 10 * g + step)
    for copy in swapped:
        copy.wait_send()
    in_copy.wait()


SCHEDULE = (
    (),
    (10, 80, 0, 20,),
    (11, 81,),
    (30, 12, 1, 90, 40, 50, 21, 2, 31, 22, 3, 100, 13, 91,),
    (60, 32, 4,),
    (),
    (14, 41, 23,),
    (92,),
    (24, 110, 51,),
    (33,),
    (101, 70, 42, 34,),
    (120, 52,),
    (),
    (),
    (61, 43, 102,),
    (93, 111, 53, 82, 44,),
    (94, 54, 62,),
    (71,),
    (103, 112,),
    (104, 63,),
    (1050, 72,),
    (64,),
    (113,),
    (),
    (121, 1051, 73, 114,),
    (1060,),
    (122, 74,),
    (83,),
    (1061,),
    (1052, 123, 84,),
    (1070, 124,),
    (),
    (1071,),
    (1062,),
    (),
    (1080,),
    (1090, 1053, 1072,),
    (1081,),
    (),
    (1091,),
    (1040, 1063,),
    (),
    (1082, 1010, 1073,),
    (1092,),
    (1064, 1083, 1041,),
    (1011, 1020, 1093, 1074,),
    (1042, 1021,),
    (),
    (),
    (1043, 1100, 1054, 1110, 1012, 1084,),
    (1111, 1120, 1085, 1022, 1101, 1121, 1013, 1065, 1112,),
    (1023,),
    (1044, 1102, 1113, 1122, 1094, 1103,),
    (1123, 1024, 1114,),
    (1075, 1014, 1104, 1025, 1045, 1115, 1124, 1105, 1095, 1055, 1015, 1125,),
)


def layer(fold, ins):
    length, width = ins["x"].shape
    hidden = ins["wg"].shape[1]
    rows, drows = ins["wq"].shape[0], ins["wd"].shape[0]
    padded = (length + 127) // 128 * 128
    blocks = ((0, 256, 0, 256), (256, 592, 0, 640), (592, length, 512, padded))
    wide = hidden // 4 * 2
    names = dict(g_q="wq", g_k="wk", g_v="wv", g_o="wo", g_g="wg", g_u="wu", g_d="wd")
    big = jax.ShapeDtypeStruct((length, width), BF16)
    outs = dict(out=big, in_grad=big)
    outs.update({n: jax.ShapeDtypeStruct(ins[w].shape, F32) for n, w in names.items()})
    sizes = [(rows, width), (rows, 256)] + 3 * [(rows, width)] + 4 * [(rows, wide)]
    sizes.append((drows, width))
    vmem = pltpu.VMEM
    lead = ((4, 2, 2), (4, 2), (4,), (3,))
    low, wider = vmem((length, width), BF16), vmem((padded, width), BF16)
    lane, high = vmem((length, 128), F32), vmem((length, width), F32)
    sems = 2 * [pltpu.SemaphoreType.DMA((len(sizes) + 3, 4))]
    sems += 2 * [pltpu.SemaphoreType.DMA((len(SUMMED), 5))]
    weights = ("wq", "wk", "wv", "wo", "wg", "wu", "wd")
    scratch = dict(
        full=[vmem((4, 2, 2, 2 * m, c), BF16) for m, c in sizes],
        bufs=[
            [vmem(d + (2 * m, c // 2), BF16) for d in lead] + 2 * [vmem((m, c // 2), F32)]
            for m, c in [(rows, width)] + [sizes[i] for i in SUMMED[1:-3]] + 3 * [(rows, 256)]
        ],
        gains=vmem((rows, 256), BF16),
        other=[vmem((rows, 256), BF16)] + [vmem(ins[n].shape, BF16) for n in weights],
        sems=sems,
        swap=2 * [pltpu.SemaphoreType.DMA((8,))],
        local=pltpu.SemaphoreType.DMA((10,)),
        near=[vmem(ins[n].shape, BF16) for n in weights],
        x_near=low,
        gy_near=low,
        xn=low,
        q=low,
        attn=low,
        hn=low,
        t1=low,
        k=wider,
        v=wider,
        t2=vmem((length, wide), BF16),
        h1=high,
        acc1=high,
        acc2=high,
        gu=vmem((length, wide), F32),
        dh=vmem((length, wide // 2), F32),
        bias=vmem((length, 640), BF16),
        cos=lane,
        sin=lane,
        lse=lane,
        norms=vmem((length, 2), F32),
        gain=vmem((8, width), F32),
    )
    leaves, tree = jax.tree.flatten(scratch)
    given = list(ins) + list(outs)

    def body(*refs):
        named = dict(zip(given, refs), **jax.tree.unflatten(tree, refs[len(given) :]))
        layer_kernel(fold, blocks, SimpleNamespace(**named))

    near, anywhere = pl.BlockSpec(memory_space=vmem), pl.BlockSpec(memory_space=pl.ANY)
    return pl.pallas_call(
        body,
        out_shape=list(outs.values()),
        in_specs=[anywhere if n in weights + ("x", "gy") else near for n in ins],
        out_specs=[anywhere] * 2 + [near] * (len(outs) - 2),
        scratch_shapes=leaves,
        compiler_params=pltpu.CompilerParams(
            collective_id=0, has_side_effects=True, vmem_limit_bytes=62 * 2**20
        ),
    )(*ins.values())


def finish_kernel(count, *refs):
    raw, weights, gains = refs[:count], refs[count : count + 5], refs[count + 5 : count + 7]
    outs, sums = refs[count + 7 : 2 * count + 7], refs[2 * count + 7 : 2 * count + 9]
    held, sems = refs[2 * count + 9 : -1], refs[-1]
    given = raw + weights
    loads = [pltpu.make_async_copy(a, h, sems.at[i]) for i, (a, h) in enumerate(zip(given, held))]
    stores = [
        pltpu.make_async_copy(h, o, sems.at[len(given) + i])
        for i, (h, o) in enumerate(zip(held, outs))
    ]
    for copy in loads:
        copy.start()
    for i, copy in enumerate(loads):
        copy.wait()
        if i < count:
            stores[i].start()
    for gain, out, which in zip(gains, sums, (((0, 2), (1, 3), (2, 4)), ((3, 6), (4, 7)))):
        n = gain.shape[1]
        column = sum(
            jnp.sum(held[count + w][...].astype(F32) * held[g][...], axis=1, keepdims=True)
            for w, g in which
        )
        same = lax.broadcasted_iota(jnp.int32, (n, n), 0) == lax.broadcasted_iota(jnp.int32, (n, n), 1)
        row = jnp.sum(jnp.where(same, column, 0.0), axis=0, keepdims=True)
        out[...] = row / gain[...].astype(F32)
    for copy in stores:
        copy.wait()


def finish_all(raw, weights, gains):
    near, anywhere = pl.BlockSpec(memory_space=pltpu.VMEM), pl.BlockSpec(memory_space=pl.ANY)
    held = list(raw) + list(weights)
    return pl.pallas_call(
        lambda *refs: finish_kernel(len(raw), *refs),
        out_shape=[jax.ShapeDtypeStruct(a.shape, a.dtype) for a in raw]
        + [jax.ShapeDtypeStruct(g.shape, F32) for g in gains],
        in_specs=[anywhere] * len(held) + [near] * 2,
        out_specs=[anywhere] * len(raw) + [near] * 2,
        scratch_shapes=[pltpu.VMEM(a.shape, a.dtype) for a in held]
        + [pltpu.SemaphoreType.DMA((len(held) + len(raw),))],
        compiler_params=pltpu.CompilerParams(vmem_limit_bytes=62 * 2**20),
    )(*raw, *weights, *gains)


def per_device(
    fold,
    block_input,
    seg_ids,
    gain_attn,
    w_query,
    w_key,
    w_value,
    w_out,
    gain_ffn,
    w_gate,
    w_up,
    w_down,
    cotangent,
):
    row_count, length, width = block_input.shape
    groups = [[c * fold + j for j in range(fold)] for c in range(CELLS)]
    gains = (gain_attn[None], gain_ffn[None])
    blocks = [w_query, w_key, w_value, w_out, w_gate, w_up, w_down]
    if fold > 1:
        blocks = [
            lax.all_gather(w, AXIS, axis=0, tiled=True, axis_index_groups=groups) for w in blocks
        ]
        gains = tuple(
            lax.all_gather(g, AXIS, axis=1, tiled=True, axis_index_groups=groups) for g in gains
        )
    exponent = (np.arange(HEAD // 2, dtype=np.float32) * np.float32(2.0)) / np.float32(HEAD)
    freq = jnp.asarray(np.tile(np.float32(10000.0) ** -exponent, 4)[None].astype(np.float32))
    wq, wk, wv, wo, wg, wu, wd = blocks
    output, input_grad, *parts = layer(
        fold,
        dict(
            x=block_input.reshape(row_count * length, width),
            seg=seg_ids,
            ga=gains[0],
            gf=gains[1],
            freq=freq,
            wq=wq,
            wk=wk,
            wv=wv,
            wo=wo,
            wg=wg,
            wu=wu,
            wd=wd,
            gy=cotangent.reshape(row_count * length, width),
        ),
    )
    if fold > 1:
        parts = [
            lax.psum_scatter(g, AXIS, scatter_dimension=0, tiled=True, axis_index_groups=groups)
            for g in parts
        ]
    output, input_grad, dq, dk, dv, do, dg, du, dd, gain_one, gain_two = finish_all(
        [output, input_grad] + parts,
        (w_query, w_key, w_value, w_gate, w_up),
        (gain_attn[None], gain_ffn[None]),
    )
    output, input_grad = (a.reshape(block_input.shape) for a in (output, input_grad))
    return (output, input_grad, gain_one[0], dq, dk, dv, do, gain_two[0], dg, du, dd)


def solution(mesh):
    fold = mesh.shape[AXIS] // CELLS
    rows, flat = P(AXIS, None), P(AXIS)
    cube = P(AXIS, None, None)

    def run(*args):
        return per_device(fold, *args)

    return jax.shard_map(
        run,
        mesh=mesh,
        in_specs=(cube, rows, flat, rows, rows, rows, rows, flat, rows, rows, rows, cube),
        out_specs=(cube, cube, flat, rows, rows, rows, rows, flat, rows, rows, rows),
        check_vma=False,
    )
```
